256 devices in a mesh: dom: 32 (over x_lo, z, core), kv: 8 (over y, x_hi).
Axes of the slice: x: 4 (x_hi: 2, x_lo: 2; x = x_hi * 2 + x_lo), y: 4, z: 8, core: 2. Of those that a mesh axis runs over, the one named last changes fastest.
Arguments:
- positions: float32 [3, 65536], P(None, ('dom', 'kv')), may hold values from 0 to 60
- features: bfloat16 [65536, 128], P(('dom', 'kv')), may hold values from -6 to 6
- nbr_index: int32 [65536, 64], P(('dom', 'kv')), may hold values from 0 to 4095
- nbr_count: int32 [65536], P(('dom', 'kv')), may hold values from 16 to 64
- nbr_dist: float32 [65536, 64], P(('dom', 'kv')), may hold values from 0.8 to 5
- halo_lists: int32 [32, 2, 1024], P('dom'), may hold values from 0 to 2047
- wave_vectors: float32 [3, 2048], replicated, may hold values from -1.2566371 to 1.2566371, as said below
- w_charge_first: bfloat16 [128, 16], replicated, may hold values from -0.5 to 0.5
- w_long_first: float32 [16, 128], replicated, may hold values from -1.5 to 1.5
- w_value: bfloat16 [128, 128], replicated, may hold values from -0.5 to 0.5
- w_filter: float32 [16, 128], replicated, may hold values from -1.5 to 1.5
- w_charge_second: bfloat16 [128, 16], replicated, may hold values from -0.5 to 0.5
- w_long_second: float32 [16, 128], replicated, may hold values from -1.5 to 1.5
Outputs:
- features_out: bfloat16 [65536, 128], P(('dom', 'kv'))
- forces: float32 [3, 65536], P(None, ('dom', 'kv'))
The draws below stay inside these ranges and needn't reach their ends.
Inputs may be any that keep to these rules, and one draw needn't show every extreme that they name: `nbr_index`: rows of the atom's own domain table. `nbr_count`: slots at or past the count are padding. `halo_lists`: rows among the domain's own 2048 atoms; repeats may occur. `wave_vectors`: the columns are 2 pi n / 60 for 2048 distinct nonzero integer vectors n of smallest length, no two equal or opposite, in no particular order.
All inputs are finite; a program needn't handle non-finite values.
Results may differ from the reference program's by a relative error of at most 0.0054.
Values may be sent and summed in bfloat16 or wider, within the bound.
No kernel may reach another device: no remote copies, remote signals or barrier semaphores. Data moves between devices by JAX's collectives and lax.ppermute only.
A program may use at most 64 MiB of HBM per device.

```python
import math
import jax
import jax.numpy as jnp
from jax import lax

HID = 128
CHAN = 16
KVEC = 2048
NEIGH = 64
NRBF = 16
DOMS = 32
DOM_ATOMS = 2048
HALO = 1024
ATOMS = 65536


def draw_wave_vectors(key, part):
    reach = 12
    side = 2 * reach + 1
    flat = jnp.arange(side * side * side, dtype=jnp.int32)
    first = flat // (side * side) - reach
    second = flat // side % side - reach
    third = flat % side - reach
    upper = (first > 0) | (first == 0) & (second > 0) | (first == 0) & (second == 0) & (third > 0)
    sq_len = first * first + second * second + third * third
    order_key = jax.random.fold_in(key, 11)
    sign_key = jax.random.fold_in(key, 23)
    place_key = jax.random.fold_in(key, 37)
    tie_break = jax.random.permutation(order_key, side * side * side).astype(jnp.int32)
    scores = jnp.where(upper, sq_len * 32768 + tie_break, 1073741823)
    chosen = jnp.argsort(scores, stable=True)[:KVEC]
    integer_vecs = jnp.stack([first[chosen], second[chosen], third[chosen]], axis=0)
    signs = jax.random.randint(sign_key, (KVEC,), 0, 2).astype(jnp.int32) * 2 - 1
    integer_vecs = integer_vecs * signs[None, :]
    placed = jax.random.permutation(place_key, KVEC)
    integer_vecs = integer_vecs[:, placed]
    return integer_vecs.astype(jnp.float32) * jnp.float32(2.0 * math.pi / 60.0)


def set_ends(values, key, least, top_value):
    longest = values.shape.index(max(values.shape))
    spots = []
    for shift in (0, 1):
        where = [jax.random.randint(jax.random.fold_in(key, axis), (), 0, length) for axis, length in enumerate(values.shape)]
        where[longest] = (where[longest] + shift) % values.shape[longest]
        spots.append(tuple(where))
    return values.at[spots[0]].set(least).at[spots[1]].set(top_value)


def block_scale(key, dims, cuts, least, top_value):
    loudness = 1.0
    for dim, shards_of in cuts:
        draws = jax.random.uniform(jax.random.fold_in(jax.random.fold_in(key, 6), dim), (shards_of,), jnp.float32, least / len(cuts), top_value / len(cuts))
        loudness = loudness * jnp.repeat(jnp.exp(draws), dims[dim] // shards_of).reshape((-1,) + (1,) * (len(dims) - 1 - dim))
    return loudness


def noise(own_key, dims, scale, bound, shards=(), kind=jnp.bfloat16):
    level = block_scale(own_key, dims, shards, -0.22, 0.18) if shards else 1.0
    array = jax.random.normal(own_key, dims, jnp.float32) * scale * level
    return jnp.minimum(jnp.maximum(array, -bound), bound).astype(kind)


def setup_inputs(seed: int = 0) -> dict:
    key_of = jax.random.split(jax.random.key(seed), 14)
    return {
        "positions": jnp.clip(60.0 * jax.random.uniform(key_of[0], (3, ATOMS), jnp.float32) ** block_scale(key_of[0], (3, ATOMS), ((1, 256),), -0.2, 0.2), 0.0, 60.0),
        "features": noise(key_of[1], (ATOMS, HID), 1.0, 6.0, ((0, 256),)),
        "nbr_index": set_ends(jax.random.randint(key_of[2], (ATOMS, NEIGH), 0, DOM_ATOMS + 2 * HALO), jax.random.fold_in(key_of[2], 1), 0, (DOM_ATOMS + 2 * HALO) - 1).astype(jnp.int32),
        "nbr_count": set_ends(jax.random.randint(key_of[3], (ATOMS,), NEIGH // 4, NEIGH + 1), jax.random.fold_in(key_of[3], 1), NEIGH // 4, NEIGH).astype(jnp.int32),
        "nbr_dist": jnp.clip(0.8 + 4.2 * jax.random.uniform(key_of[4], (ATOMS, NEIGH), jnp.float32) ** block_scale(key_of[4], (ATOMS, NEIGH), ((0, 256),), -0.2, 0.2), 0.8, 5.0),
        "halo_lists": set_ends(jax.random.randint(key_of[5], (DOMS, 2, HALO), 0, DOM_ATOMS), jax.random.fold_in(key_of[5], 1), 0, DOM_ATOMS - 1).astype(jnp.int32),
        "wave_vectors": draw_wave_vectors(jax.random.fold_in(key_of[13], 71), 0),
        "w_charge_first": noise(key_of[7], (HID, CHAN), HID ** -0.5, 0.5),
        "w_long_first": noise(key_of[8], (CHAN, HID), CHAN ** -0.5, 1.5, (), jnp.float32),
        "w_value": noise(key_of[9], (HID, HID), HID ** -0.5, 0.5),
        "w_filter": noise(key_of[10], (NRBF, HID), NRBF ** -0.5, 1.5, (), jnp.float32),
        "w_charge_second": noise(key_of[11], (HID, CHAN), HID ** -0.5, 0.5),
        "w_long_second": noise(key_of[12], (CHAN, HID), CHAN ** -0.5, 1.5, (), jnp.float32),
    }


HIGHEST_PRECISION = lax.Precision.HIGHEST
LONG_SCALE = 2.0

def wave_weight(wavevec):
    sq_norm = wavevec[0] * wavevec[0] + wavevec[1] * wavevec[1] + wavevec[2] * wavevec[2]
    return jnp.exp(-0.5 * sq_norm) / (sq_norm + 1.0)

def phase_tables(wavevec, coords):
    phase_angle = wavevec[0][:, None] * coords[0][None, :] + wavevec[1][:, None] * coords[1][None, :] + wavevec[2][:, None] * coords[2][None, :]
    return (jnp.cos(phase_angle), jnp.sin(phase_angle))

def partial_structure(wavevec, coords, charge):
    cos_table, sin_table = phase_tables(wavevec, coords)
    return (jnp.dot(cos_table, charge, precision=HIGHEST_PRECISION, preferred_element_type=jnp.float32), jnp.dot(sin_table, charge, precision=HIGHEST_PRECISION, preferred_element_type=jnp.float32))

def partial_project(wavevec, coords, charge, cos_part, sin_part):
    cos_table, sin_table = phase_tables(wavevec, coords)
    weight = wave_weight(wavevec)[:, None]
    cos_weighted = weight * cos_part
    sin_weighted = weight * sin_part
    contract_dims = (((0,), (0,)), ((), ()))
    potential = lax.dot_general(cos_table, cos_weighted, contract_dims, precision=HIGHEST_PRECISION, preferred_element_type=jnp.float32)
    potential = potential + lax.dot_general(sin_table, sin_weighted, contract_dims, precision=HIGHEST_PRECISION, preferred_element_type=jnp.float32)
    along_cos = jnp.dot(cos_weighted, charge.T, precision=HIGHEST_PRECISION, preferred_element_type=jnp.float32)
    along_sin = jnp.dot(sin_weighted, charge.T, precision=HIGHEST_PRECISION, preferred_element_type=jnp.float32)
    mixed = sin_table * along_cos - cos_table * along_sin
    force = jnp.dot(wavevec, mixed, precision=HIGHEST_PRECISION, preferred_element_type=jnp.float32)
    return (potential, force)

def long_range(hidden, w_charge, positions, wave_vectors):
    charge = jnp.dot(hidden, w_charge, preferred_element_type=jnp.float32)
    wave_block = min(256, KVEC)
    block_count = KVEC // wave_block
    wave_blocks = wave_vectors.reshape(3, block_count, wave_block).transpose(1, 0, 2)
    cos_part, sin_part = lax.map(lambda wavevec: partial_structure(wavevec, positions, charge), wave_blocks)
    inv_root = 1.0 / math.sqrt(ATOMS)
    cos_part = cos_part * inv_root
    sin_part = sin_part * inv_root

    def accumulate(running, member):
        pot_add, force_add = partial_project(member[0], positions, charge, member[1], member[2])
        return ((running[0] + pot_add, running[1] + force_add), None)
    start_state = (jnp.zeros((ATOMS, CHAN), jnp.float32), jnp.zeros((3, ATOMS), jnp.float32))
    (potential, force), _ = lax.scan(accumulate, start_state, (wave_blocks, cos_part, sin_part))
    prefactor = LONG_SCALE / math.sqrt(KVEC)
    return (potential * prefactor, force * prefactor)

def basis_of(distance, live_count):
    centers = 0.5 + 4.5 / (NRBF - 1) * jnp.arange(NRBF, dtype=jnp.int32).astype(jnp.float32)
    sharpness = ((NRBF - 1) / 4.5) ** 2
    envelope = 0.5 * (jnp.cos(math.pi * distance / 5.0) + 1.0)
    in_list = (jnp.arange(distance.shape[1], dtype=jnp.int32)[None, :] < live_count[:, None]).astype(jnp.float32)
    radial = jnp.exp(-sharpness * (distance[..., None] - centers) ** 2)
    return (radial * (envelope * in_list)[..., None]).astype(jnp.bfloat16)

def short_range(hidden, w_value, w_filter, nbr_index, nbr_count, nbr_dist, halo_lists):
    values = jnp.dot(hidden, w_value, preferred_element_type=jnp.float32).astype(jnp.bfloat16)
    by_domain = values.reshape(DOMS, DOM_ATOMS, HID)
    selected = jax.vmap(lambda rows_of, picks: rows_of[picks])(by_domain, halo_lists)
    from_below = jnp.roll(selected[:, 0], 1, axis=0)
    from_above = jnp.roll(selected[:, 1], -1, axis=0)
    value_table = jnp.concatenate([by_domain, from_below, from_above], axis=1)

    def one_domain(member):
        table_rows, index_rows, count_rows, dist_rows = member
        picked = table_rows[index_rows].astype(jnp.float32)
        basis = basis_of(dist_rows, count_rows).astype(jnp.float32)
        contracted = jnp.einsum('ajr,ajf->arf', basis, picked, precision=HIGHEST_PRECISION)
        return jnp.einsum('arf,rf->af', contracted, w_filter, precision=HIGHEST_PRECISION)
    message = lax.map(one_domain, (value_table, nbr_index.reshape(DOMS, DOM_ATOMS, NEIGH), nbr_count.reshape(DOMS, DOM_ATOMS), nbr_dist.reshape(DOMS, DOM_ATOMS, NEIGH))).reshape(ATOMS, HID)
    return (hidden.astype(jnp.float32) + jax.nn.silu(message)).astype(jnp.bfloat16)

def reference(positions, features, nbr_index, nbr_count, nbr_dist, halo_lists, wave_vectors, w_charge_first, w_long_first, w_value, w_filter, w_charge_second, w_long_second):
    pot_first, force_first = long_range(features, w_charge_first, positions, wave_vectors)
    lifted = jnp.dot(pot_first, w_long_first, precision=HIGHEST_PRECISION, preferred_element_type=jnp.float32)
    hidden_first = (features.astype(jnp.float32) + jax.nn.silu(lifted)).astype(jnp.bfloat16)
    hidden_second = short_range(hidden_first, w_value, w_filter, nbr_index, nbr_count, nbr_dist, halo_lists)
    pot_second, force_second = long_range(hidden_second, w_charge_second, positions, wave_vectors)
    lifted = jnp.dot(pot_second, w_long_second, precision=HIGHEST_PRECISION, preferred_element_type=jnp.float32)
    features_out = (hidden_second.astype(jnp.float32) + jax.nn.silu(lifted)).astype(jnp.bfloat16)
    return (features_out, force_first + force_second)
```

```python
import math

import jax
import jax.numpy as jnp
from jax import lax
from jax.experimental import pallas as pl
from jax.experimental.pallas import tpu as pltpu
from jax.sharding import PartitionSpec as P

F32 = jnp.float32
BF16 = jnp.bfloat16
HIGHEST = lax.Precision.HIGHEST
LONG_SCALE = 2.0
CELL = 60.0
EVERY = ("dom", "kv")

COS_COEF = (
    1.0,
    -19.73920440673828,
    64.93911743164062,
    -85.45014190673828,
    60.16762924194336,
    -25.967599868774414,
    6.528658390045166,
)
SIN_COEF = (
    6.2831854820251465,
    -41.34170150756836,
    81.60513305664062,
    -76.70301818847656,
    42.02592849731445,
    -14.899847030639648,
    3.2381374835968018,
)

NN = (((1,), (0,)), ((), ()))
NT = (((1,), (1,)), ((), ()))
TN = (((0,), (0,)), ((), ()))


def horner(coefs, v):
    total = v * coefs[-1] + coefs[-2]
    for coef in coefs[-3::-1]:
        total = total * v + coef
    return total


def dot(a, b, dims=NN, precision=None):
    return lax.dot_general(a, b, dims, precision=precision, preferred_element_type=F32)


def silu(x):
    return x / (1.0 + jnp.exp(-x))


def wave_weight(wave):
    sq_norm = wave[0:1] * wave[0:1] + wave[1:2] * wave[1:2] + wave[2:3] * wave[2:3]
    return jnp.exp(-0.5 * sq_norm) / (sq_norm + 1.0)


def split_rows(x):
    high = x.astype(BF16)
    return jnp.concatenate([high, (x - high.astype(F32)).astype(BF16)], axis=0)


def structure_part(charge_t, cos_ref, sin_ref, wave_ref, part_ref, scale):
    chan = charge_t.shape[0]
    waves = cos_ref.shape[1]
    rows = split_rows(charge_t)
    cos_sum = dot(rows, cos_ref[...])
    sin_sum = dot(rows, sin_ref[...])
    weight = wave_weight(wave_ref[...]) * scale
    cos_sum = (cos_sum[:chan] + cos_sum[chan:]) * weight
    sin_sum = (sin_sum[:chan] + sin_sum[chan:]) * weight
    for t in range(waves // 128):
        lanes = slice(t * 128, (t + 1) * 128)
        part_ref[t * 2 * chan : t * 2 * chan + chan, :] = cos_sum[:, lanes].astype(BF16)
        part_ref[t * 2 * chan + chan : (t + 1) * 2 * chan, :] = sin_sum[:, lanes].astype(BF16)


def table_kernel(pos_ref, feat_ref, wc_ref, wave_ref, cos_ref, sin_ref, part_ref, turns, pad, *, scale):
    atoms, waves = cos_ref.shape
    pad[...] = jnp.zeros_like(pad)
    pad[0:3, :] = pos_ref[...] * (1.0 / CELL)
    columns = jnp.transpose(pad[...])
    for c in range(3):
        turns[c] = jnp.broadcast_to(columns[:, c : c + 1], (atoms, 128))
    rows = 64

    def one_tile(t, carry):
        lanes = pl.ds(pl.multiple_of(t * 128, 128), 128)
        whole = jnp.round(wave_ref[:, lanes] * (CELL / (2.0 * math.pi)))
        for b in range(atoms // rows):
            at = slice(b * rows, (b + 1) * rows)
            u = (
                turns[0, at, :] * whole[0:1]
                + turns[1, at, :] * whole[1:2]
                + turns[2, at, :] * whole[2:3]
            )
            u = u - jnp.round(u)
            v = u * u
            cos_ref[at, lanes] = horner(COS_COEF, v).astype(BF16)
            sin_ref[at, lanes] = (u * horner(SIN_COEF, v)).astype(BF16)
        return carry

    lax.fori_loop(0, waves // 128, one_tile, 0)
    charge_t = dot(wc_ref[...], feat_ref[...], (((0,), (1,)), ((), ())))
    structure_part(charge_t, cos_ref, sin_ref, wave_ref, part_ref, scale)


def fold_kernel(in_ref, out_ref):
    rows = in_ref.shape[0]
    total = jnp.sum(in_ref[...].astype(F32).reshape(rows // 8, 8, 128), axis=0)
    total = total + pltpu.roll(total, 4, 0)
    total = total + pltpu.roll(total, 2, 0)
    out_ref[...] = jnp.broadcast_to(total[None], (rows // 8, 8, 128)).reshape(rows, 128).astype(BF16)


def project(sums_ref, cos_ref, sin_ref, wave_ref, charge_t, with_cos, with_sin):
    chan = charge_t.shape[0]
    waves = cos_ref.shape[1]
    for t in range(waves // 128):
        lanes = slice(t * 128, (t + 1) * 128)
        wave = wave_ref[:, lanes]
        cos_w = sums_ref[t * 2 * chan : t * 2 * chan + chan, :].astype(F32)
        sin_w = sums_ref[t * 2 * chan + chan : (t + 1) * 2 * chan, :].astype(F32)
        with_cos[0:chan, lanes] = cos_w.astype(BF16)
        with_sin[0:chan, lanes] = sin_w.astype(BF16)
        for c in range(3):
            at = slice((c + 1) * chan, (c + 2) * chan)
            with_cos[at, lanes] = (-wave[c : c + 1] * sin_w).astype(BF16)
            with_sin[at, lanes] = (wave[c : c + 1] * cos_w).astype(BF16)
    both = dot(with_cos[...], cos_ref[...], NT) + dot(with_sin[...], sin_ref[...], NT)
    potential_t = both[:chan]
    force = [
        jnp.sum(charge_t * both[(c + 1) * chan : (c + 2) * chan], axis=0, keepdims=True)
        for c in range(3)
    ]
    return potential_t, force


def first_project_kernel(
    sums_ref, cos_ref, sin_ref, wave_ref, feat_ref, wc_ref, wl_ref, wv_ref,
    hidden_ref, values_ref, force_ref, with_cos, with_sin,
):
    charge_t = dot(wc_ref[...], feat_ref[...], (((0,), (1,)), ((), ())))
    potential_t, force = project(sums_ref, cos_ref, sin_ref, wave_ref, charge_t, with_cos, with_sin)
    for c in range(3):
        force_ref[c : c + 1, :] = force[c]
    lifted = dot(potential_t, wl_ref[...], TN, HIGHEST)
    hidden = (feat_ref[...].astype(F32) + silu(lifted)).astype(BF16)
    hidden_ref[...] = hidden
    values = dot(hidden, wv_ref[...]).astype(BF16)
    atoms = values.shape[0]
    for j in range(values_ref.shape[0] // atoms):
        values_ref[j * atoms : (j + 1) * atoms, :] = values


def last_project_kernel(
    sums_ref, cos_ref, sin_ref, wave_ref, hidden_ref, wc_ref, wl_ref, force_in,
    feat_out, force_out, with_cos, with_sin,
):
    charge_t = dot(wc_ref[...], hidden_ref[...], (((0,), (1,)), ((), ())))
    potential_t, force = project(sums_ref, cos_ref, sin_ref, wave_ref, charge_t, with_cos, with_sin)
    for c in range(3):
        force_out[c : c + 1, :] = force_in[c : c + 1, :] + force[c]
    lifted = dot(potential_t, wl_ref[...], TN, HIGHEST)
    feat_out[...] = (hidden_ref[...].astype(F32) + silu(lifted)).astype(BF16)


def halo_kernel(list_ref, values_ref, below_ref, above_ref, table, picked):
    table[...] = values_ref[...].astype(F32)
    count = below_ref.shape[0]
    for side, out_ref in ((0, below_ref), (1, above_ref)):

        def some_rows(b, carry, side=side):
            for j in range(16):
                picked[pl.ds(b * 16 + j, 1), :] = table[pl.ds(list_ref[side, b * 16 + j], 1), :]
            return carry

        lax.fori_loop(0, count // 16, some_rows, 0)
        out_ref[...] = picked[...].astype(BF16)


def weight_kernel(count_ref, dist_ref, wf_ref, out_ref, taper, wide):
    step = pl.program_id(0)
    rows = dist_ref.shape[0]
    basis = wf_ref.shape[0]
    sharpness = ((basis - 1) / 4.5) ** 2
    centers = 0.5 + 4.5 / (basis - 1) * lax.broadcasted_iota(jnp.int32, (basis, 128), 0).astype(F32)
    scaled = dist_ref[...] * 0.1
    taper[...] = 0.5 * (horner(COS_COEF, scaled * scaled) + 1.0)
    wf_high = wf_ref[...].astype(BF16)
    wide[0:basis, :] = wf_high
    wide[basis : 2 * basis, :] = (wf_ref[...] - wf_high.astype(F32)).astype(BF16)
    lane = lax.broadcasted_iota(jnp.int32, (1, 128), 1)

    for j in range(rows):
        atom = (step * rows + j) * 2
        live = jnp.where(lane < 64, count_ref[atom], count_ref[atom + 1] + 64)
        away = jnp.broadcast_to(dist_ref[j : j + 1, :], (basis, 128)) - centers
        height = jnp.where(lane < live, taper[j : j + 1, :], 0.0)
        radial = (jnp.exp(-sharpness * (away * away)) * height).astype(BF16)
        both = jnp.concatenate([radial, radial], axis=0)
        out_ref[j * 128 : (j + 1) * 128, :] = dot(both, wide[...], TN)


def neighbour_kernel(
    index_ref, weight_ref, values_ref, below_ref, above_ref, hidden_ref, wc_ref, cos_ref, sin_ref, wave_ref,
    hidden_out, part_ref, table, message, *, scale,
):
    step = pl.program_id(0)
    own = values_ref.shape[0]
    halo = below_ref.shape[0]
    slots = index_ref.shape[1]
    atoms = weight_ref.shape[0] // slots

    @pl.when(step == 0)
    def _():
        table[0:own, :] = values_ref[...].astype(F32)
        table[own : own + halo, :] = below_ref[...].astype(F32)
        table[own + halo : own + 2 * halo, :] = above_ref[...].astype(F32)

    sub = lax.broadcasted_iota(jnp.int32, (8, 128), 0)

    def one_atom(a, carry):
        atom = step * atoms + a
        total = jnp.zeros((8, 128), F32)
        for s in range(0, slots, 8):
            rows = table[pl.ds(index_ref[atom, s], 8, stride=0), :]
            for j in range(1, 8):
                rows = jnp.where(sub == j, table[pl.ds(index_ref[atom, s + j], 8, stride=0), :], rows)
            at = pl.ds(pl.multiple_of(a * slots + s, 8), 8)
            total = total + rows * weight_ref[at, :]
        message[pl.ds(atom, 1), :] = jnp.sum(total, axis=0, keepdims=True)
        return carry

    lax.fori_loop(0, atoms, one_atom, 0)

    @pl.when(step == pl.num_programs(0) - 1)
    def _():
        hidden = (hidden_ref[...].astype(F32) + silu(message[...])).astype(BF16)
        hidden_out[...] = hidden
        charge_t = dot(wc_ref[...], hidden, (((0,), (1,)), ((), ())))
        structure_part(charge_t, cos_ref, sin_ref, wave_ref, part_ref, scale)


def shape(dims, kind):
    return jax.ShapeDtypeStruct(dims, kind)


def everything(part, name):
    sums = lax.all_to_all(part, EVERY, 0, 0, tiled=True)
    folded = pl.pallas_call(fold_kernel, out_shape=shape(part.shape, BF16), name=name)(sums)
    return lax.all_to_all(folded, EVERY, 0, 0, tiled=True)


def local(
    positions, features, nbr_index, nbr_count, nbr_dist, halo_lists, wave_vectors,
    w_charge_first, w_long_first, w_value, w_filter, w_charge_second, w_long_second,
):
    atoms, hid = features.shape
    chan = w_charge_first.shape[1]
    waves = wave_vectors.shape[1]
    slots = nbr_index.shape[1]
    kv = lax.axis_size("kv")
    doms = lax.axis_size("dom")
    total_atoms = atoms * doms * kv
    scale = LONG_SCALE / math.sqrt(waves) / math.sqrt(total_atoms)
    part_rows = 2 * chan * waves // 128
    halo = halo_lists.shape[2]
    smem = pl.BlockSpec(memory_space=pltpu.SMEM)

    cos_table, sin_table, part = pl.pallas_call(
        lambda *refs: table_kernel(*refs, scale=scale),
        out_shape=(shape((atoms, waves), BF16), shape((atoms, waves), BF16), shape((part_rows, 128), BF16)),
        scratch_shapes=[pltpu.VMEM((3, atoms, 128), F32), pltpu.VMEM((8, atoms), F32)],
        name="tables",
    )(positions, features, w_charge_first, wave_vectors)
    sums = everything(part, "fold_first")
    hidden_first, values, force_first = pl.pallas_call(
        first_project_kernel,
        out_shape=(shape((atoms, hid), BF16), shape((kv * atoms, hid), BF16), shape((3, atoms), F32)),
        scratch_shapes=[pltpu.VMEM((4 * chan, waves), BF16)] * 2,
        name="project_first",
    )(sums, cos_table, sin_table, wave_vectors, features, w_charge_first, w_long_first, w_value)

    v_dom = lax.all_to_all(values, "kv", 0, 0, tiled=True)
    to_next, to_previous = pl.pallas_call(
        halo_kernel,
        in_specs=[smem, pl.BlockSpec(memory_space=pltpu.VMEM)],
        out_shape=(shape((halo, hid), BF16), shape((halo, hid), BF16)),
        scratch_shapes=[pltpu.VMEM((kv * atoms, hid), F32), pltpu.VMEM((halo, hid), F32)],
        name="halo_rows",
    )(halo_lists[0], v_dom)
    from_below = lax.ppermute(to_next, "dom", [(i, (i + 1) % doms) for i in range(doms)])
    from_above = lax.ppermute(to_previous, "dom", [(i, (i - 1) % doms) for i in range(doms)])

    steps = 8
    pair_rows = atoms * slots // 128
    weights = pl.pallas_call(
        weight_kernel,
        grid=(steps,),
        in_specs=[
            smem,
            pl.BlockSpec((pair_rows // steps, 128), lambda i: (i, 0)),
            pl.BlockSpec(w_filter.shape, lambda i: (0, 0)),
        ],
        out_specs=pl.BlockSpec((atoms * slots // steps, hid), lambda i: (i, 0)),
        out_shape=shape((atoms * slots, hid), F32),
        scratch_shapes=[
            pltpu.VMEM((pair_rows // steps, 128), F32),
            pltpu.VMEM((2 * w_filter.shape[0], hid), BF16),
        ],
        cost_estimate=pl.CostEstimate(flops=2 * atoms * slots * hid * 32, bytes_accessed=atoms * slots * hid * 4, transcendentals=atoms * slots * 16),
        name="slot_weights",
    )(nbr_count, nbr_dist.reshape(pair_rows, 128), w_filter)

    whole = lambda a: pl.BlockSpec(a, lambda i: (0, 0))
    hidden_second, part = pl.pallas_call(
        lambda *refs: neighbour_kernel(*refs, scale=scale),
        grid=(steps,),
        in_specs=[
            smem,
            pl.BlockSpec((atoms * slots // steps, hid), lambda i: (i, 0)),
            whole((kv * atoms, hid)),
            whole((halo, hid)),
            whole((halo, hid)),
            whole((atoms, hid)),
            whole((hid, chan)),
            whole((atoms, waves)),
            whole((atoms, waves)),
            whole((3, waves)),
        ],
        out_specs=(whole((atoms, hid)), whole((part_rows, 128))),
        out_shape=(shape((atoms, hid), BF16), shape((part_rows, 128), BF16)),
        scratch_shapes=[pltpu.VMEM((kv * atoms + 2 * halo, hid), F32), pltpu.VMEM((atoms, hid), F32)],
        name="neighbours",
    )(
        nbr_index, weights, v_dom, from_below, from_above, hidden_first,
        w_charge_second, cos_table, sin_table, wave_vectors,
    )
    sums = everything(part, "fold_second")
    return pl.pallas_call(
        last_project_kernel,
        out_shape=(shape((atoms, hid), BF16), shape((3, atoms), F32)),
        scratch_shapes=[pltpu.VMEM((4 * chan, waves), BF16)] * 2,
        name="project_second",
    )(sums, cos_table, sin_table, wave_vectors, hidden_second, w_charge_second, w_long_second, force_first)


def solution(mesh):
    return jax.shard_map(
        local,
        mesh=mesh,
        in_specs=(
            P(None, EVERY), P(EVERY, None), P(EVERY, None), P(EVERY), P(EVERY, None), P("dom", None, None),
            P(), P(), P(), P(), P(), P(), P(),
        ),
        out_specs=(P(EVERY, None), P(None, EVERY)),
        check_vma=False,
    )
```

```python
import math

import jax
import jax.numpy as jnp
from jax import lax
from jax.experimental import pallas as pl
from jax.experimental.pallas import tpu as pltpu
from jax.sharding import PartitionSpec as P

F32 = jnp.float32
BF16 = jnp.bfloat16
HIGHEST = lax.Precision.HIGHEST
LONG_SCALE = 2.0
CELL = 60.0
EVERY = ("dom", "kv")

COS_COEF = (
    1.0,
    -19.73920440673828,
    64.93911743164062,
    -85.45014190673828,
    60.16762924194336,
    -25.967599868774414,
    6.528658390045166,
)
SIN_COEF = (
    6.2831854820251465,
    -41.34170150756836,
    81.60513305664062,
    -76.70301818847656,
    42.02592849731445,
    -14.899847030639648,
    3.2381374835968018,
)

NN = (((1,), (0,)), ((), ()))
NT = (((1,), (1,)), ((), ()))
TN = (((0,), (0,)), ((), ()))


def horner(coefs, v):
    total = v * coefs[-1] + coefs[-2]
    for coef in coefs[-3::-1]:
        total = total * v + coef
    return total


def dot(a, b, dims=NN, precision=None):
    return lax.dot_general(a, b, dims, precision=precision, preferred_element_type=F32)


def silu(x):
    return x / (1.0 + jnp.exp(-x))


def wave_weight(wave):
    sq_norm = wave[0:1] * wave[0:1] + wave[1:2] * wave[1:2] + wave[2:3] * wave[2:3]
    return jnp.exp(-0.5 * sq_norm) / (sq_norm + 1.0)


def split_rows(x):
    high = x.astype(BF16)
    return jnp.concatenate([high, (x - high.astype(F32)).astype(BF16)], axis=0)


def structure_part(charge_t, cos_ref, sin_ref, wave_ref, part_ref, scale):
    chan = charge_t.shape[0]
    waves = cos_ref.shape[1]
    rows = split_rows(charge_t)
    cos_sum = dot(rows, cos_ref[...])
    sin_sum = dot(rows, sin_ref[...])
    weight = wave_weight(wave_ref[...]) * scale
    cos_sum = (cos_sum[:chan] + cos_sum[chan:]) * weight
    sin_sum = (sin_sum[:chan] + sin_sum[chan:]) * weight
    for t in range(waves // 128):
        lanes = slice(t * 128, (t + 1) * 128)
        part_ref[t * 2 * chan : t * 2 * chan + chan, :] = cos_sum[:, lanes].astype(BF16)
        part_ref[t * 2 * chan + chan : (t + 1) * 2 * chan, :] = sin_sum[:, lanes].astype(BF16)


def table_kernel(pos_ref, feat_ref, wc_ref, wave_ref, cos_ref, sin_ref, part_ref, turns, pad, *, scale):
    atoms, waves = cos_ref.shape
    pad[...] = jnp.zeros_like(pad)
    pad[0:3, :] = pos_ref[...] * (1.0 / CELL)
    columns = jnp.transpose(pad[...])
    for c in range(3):
        turns[c] = jnp.broadcast_to(columns[:, c : c + 1], (atoms, 128))
    rows = 64

    def one_tile(t, carry):
        lanes = pl.ds(pl.multiple_of(t * 128, 128), 128)
        whole = jnp.round(wave_ref[:, lanes] * (CELL / (2.0 * math.pi)))
        for b in range(atoms // rows):
            at = slice(b * rows, (b + 1) * rows)
            u = (
                turns[0, at, :] * whole[0:1]
                + turns[1, at, :] * whole[1:2]
                + turns[2, at, :] * whole[2:3]
            )
            u = u - jnp.round(u)
            v = u * u
            cos_ref[at, lanes] = horner(COS_COEF, v).astype(BF16)
            sin_ref[at, lanes] = (u * horner(SIN_COEF, v)).astype(BF16)
        return carry

    lax.fori_loop(0, waves // 128, one_tile, 0)
    charge_t = dot(wc_ref[...], feat_ref[...], NT)
    structure_part(charge_t, cos_ref, sin_ref, wave_ref, part_ref, scale)


def fold_kernel(in_ref, out_ref):
    rows = in_ref.shape[0]
    total = jnp.sum(in_ref[...].astype(F32).reshape(rows // 8, 8, 128), axis=0)
    total = total + pltpu.roll(total, 4, 0)
    total = total + pltpu.roll(total, 2, 0)
    out_ref[...] = jnp.broadcast_to(total[None], (rows // 8, 8, 128)).reshape(rows, 128).astype(BF16)


def project(sums_ref, cos_ref, sin_ref, wave_ref, charge_t, with_cos, with_sin):
    chan = charge_t.shape[0]
    waves = cos_ref.shape[1]
    for t in range(waves // 128):
        lanes = slice(t * 128, (t + 1) * 128)
        wave = wave_ref[:, lanes]
        cos_w = sums_ref[t * 2 * chan : t * 2 * chan + chan, :].astype(F32)
        sin_w = sums_ref[t * 2 * chan + chan : (t + 1) * 2 * chan, :].astype(F32)
        with_cos[0:chan, lanes] = cos_w.astype(BF16)
        with_sin[0:chan, lanes] = sin_w.astype(BF16)
        for c in range(3):
            at = slice((c + 1) * chan, (c + 2) * chan)
            with_cos[at, lanes] = (-wave[c : c + 1] * sin_w).astype(BF16)
            with_sin[at, lanes] = (wave[c : c + 1] * cos_w).astype(BF16)
    both = dot(with_cos[...], cos_ref[...], NT) + dot(with_sin[...], sin_ref[...], NT)
    potential_t = both[:chan]
    force = [
        jnp.sum(charge_t * both[(c + 1) * chan : (c + 2) * chan], axis=0, keepdims=True)
        for c in range(3)
    ]
    return potential_t, force


def first_project_kernel(
    sums_ref, cos_ref, sin_ref, wave_ref, feat_ref, wc_ref, wl_ref, wv_ref,
    hidden_ref, values_ref, force_ref, with_cos, with_sin,
):
    charge_t = dot(wc_ref[...], feat_ref[...], NT)
    potential_t, force = project(sums_ref, cos_ref, sin_ref, wave_ref, charge_t, with_cos, with_sin)
    for c in range(3):
        force_ref[c : c + 1, :] = force[c]
    lifted = dot(potential_t, wl_ref[...], TN, HIGHEST)
    hidden = (feat_ref[...].astype(F32) + silu(lifted)).astype(BF16)
    hidden_ref[...] = hidden
    values = dot(hidden, wv_ref[...]).astype(BF16)
    atoms = values.shape[0]
    for j in range(values_ref.shape[0] // atoms):
        values_ref[j * atoms : (j + 1) * atoms, :] = values


def last_project_kernel(
    sums_ref, cos_ref, sin_ref, wave_ref, hidden_ref, wc_ref, wl_ref, force_in,
    feat_out, force_out, with_cos, with_sin,
):
    charge_t = dot(wc_ref[...], hidden_ref[...], NT)
    potential_t, force = project(sums_ref, cos_ref, sin_ref, wave_ref, charge_t, with_cos, with_sin)
    for c in range(3):
        force_out[c : c + 1, :] = force_in[c : c + 1, :] + force[c]
    lifted = dot(potential_t, wl_ref[...], TN, HIGHEST)
    feat_out[...] = (hidden_ref[...].astype(F32) + silu(lifted)).astype(BF16)


def row_tile(table, rows, bits):
    tiles = [table[pl.ds(row, 8, stride=0), :] for row in rows]
    for bit in bits:
        tiles = [jnp.where(bit, odd, even) for even, odd in zip(tiles[::2], tiles[1::2])]
    return tiles[0]


def sublane_bits():
    sub = lax.broadcasted_iota(jnp.int32, (8, 128), 0)
    return [(sub & bit) != 0 for bit in (1, 2, 4)]


def halo_kernel(*refs):
    lists, (values_ref, below_ref, above_ref, table, picked) = refs[:-5], refs[-5:]
    table[...] = values_ref[...].astype(F32)
    bits = sublane_bits()

    def some_rows(g, carry):
        first = g * 8
        at = [[first + j for j in range(8)] for side in (0, 1)]
        for b, list_ref in enumerate(lists):
            for side in (0, 1):
                rows = [list_ref[side, lane] for lane in at[side]]
                picked[side, pl.ds(pl.multiple_of(b * 128 + first, 8), 8), :] = row_tile(table, rows, bits)
        return carry

    lax.fori_loop(0, 16, some_rows, 0)
    below_ref[...] = picked[0].astype(BF16)
    above_ref[...] = picked[1].astype(BF16)


def weight_kernel(count_ref, dist_ref, wf_ref, out_ref, turned, near, taper, wide):
    step = pl.program_id(0)
    slots, atoms = dist_ref.shape
    basis = wf_ref.shape[0]
    pairs = out_ref.shape[0] // 2
    sharpness = ((basis - 1) / 4.5) ** 2

    def paired(block):
        turned[...] = jnp.transpose(block)
        return jnp.concatenate(
            [turned[pl.ds(0, atoms // 2, stride=2), :], turned[pl.ds(1, atoms // 2, stride=2), :]], axis=1
        )

    @pl.when(step == 0)
    def _():
        dist = dist_ref[...]
        scaled = dist * 0.1
        height = 0.5 * (horner(COS_COEF, scaled * scaled) + 1.0)
        slot = lax.broadcasted_iota(jnp.int32, (slots, atoms), 0)
        near[...] = paired(dist)
        taper[...] = paired(jnp.where(slot < count_ref[...], height, 0.0))
        wf_high = wf_ref[...].astype(BF16)
        wide[0:basis, :] = wf_high
        wide[basis : 2 * basis, :] = (wf_ref[...] - wf_high.astype(F32)).astype(BF16)

    centers = 0.5 + 4.5 / (basis - 1) * lax.broadcasted_iota(jnp.int32, (basis, 2 * slots), 0).astype(F32)
    for p in range(pairs):
        row = pl.ds(step * pairs + p, 1)
        away = near[row, :] - centers
        radial = (jnp.exp(-sharpness * (away * away)) * taper[row, :]).astype(BF16)
        both = dot(jnp.concatenate([radial, radial], axis=0), wide[...], TN)
        out_ref[2 * p] = both[:slots]
        out_ref[2 * p + 1] = both[slots:]


def neighbour_kernel(*refs, scale):
    index_refs = refs[:-13]
    (
        weight_ref, values_ref, below_ref, above_ref, hidden_ref, wc_ref, cos_ref, sin_ref, wave_ref,
        hidden_out, part_ref, table, sums,
    ) = refs[-13:]
    step = pl.program_id(0)
    own = values_ref.shape[0]
    halo = below_ref.shape[0]
    halves, atoms, slots, _ = weight_ref.shape

    @pl.when(step == 0)
    def _():
        table[0:own, :] = values_ref[...].astype(F32)
        table[own : own + halo, :] = below_ref[...].astype(F32)
        table[own + halo : own + 2 * halo, :] = above_ref[...].astype(F32)

    bits = sublane_bits()
    for half in range(halves):

        def one_atom(a, carry, half=half):
            lane = step * atoms + a
            total = jnp.zeros((8, 128), F32)
            for b in range(slots // 8):
                rows = [index_refs[b * halves + half][s, lane] for s in range(8)]
                total = total + row_tile(table, rows, bits) * weight_ref[half, a, 8 * b : 8 * b + 8, :]
            sums[pl.ds(pl.multiple_of((half * 128 + lane) * 8, 8), 8), :] = total
            return carry

        lax.fori_loop(0, atoms, one_atom, 0)

    @pl.when(step == pl.num_programs(0) - 1)
    def _():
        count = hidden_ref.shape[0]
        message = sums[pl.ds(0, count, stride=8), :]
        for k in range(1, 8):
            message = message + sums[pl.ds(k, count, stride=8), :]
        hidden = (hidden_ref[...].astype(F32) + silu(message)).astype(BF16)
        hidden_out[...] = hidden
        charge_t = dot(wc_ref[...], hidden, NT)
        structure_part(charge_t, cos_ref, sin_ref, wave_ref, part_ref, scale)


def shape(dims, kind):
    return jax.ShapeDtypeStruct(dims, kind)


def everything(part, name):
    sums = lax.all_to_all(part, EVERY, 0, 0, tiled=True)
    folded = pl.pallas_call(fold_kernel, out_shape=shape(part.shape, BF16), name=name)(sums)
    return lax.all_to_all(folded, EVERY, 0, 0, tiled=True)


def local(
    positions, features, nbr_index, nbr_count, nbr_dist, halo_lists, wave_vectors,
    w_charge_first, w_long_first, w_value, w_filter, w_charge_second, w_long_second,
):
    atoms, hid = features.shape
    chan = w_charge_first.shape[1]
    waves = wave_vectors.shape[1]
    slots = nbr_index.shape[1]
    kv = lax.axis_size("kv")
    doms = lax.axis_size("dom")
    total_atoms = atoms * doms * kv
    scale = LONG_SCALE / math.sqrt(waves) / math.sqrt(total_atoms)
    part_rows = 2 * chan * waves // 128
    halo = halo_lists.shape[2]
    w_charge_first = w_charge_first.T
    w_charge_second = w_charge_second.T
    lists = halo_lists[0]
    index_t = nbr_index.T
    dist_t = nbr_dist.T

    cos_table, sin_table, part = pl.pallas_call(
        lambda *refs: table_kernel(*refs, scale=scale),
        out_shape=(shape((atoms, waves), BF16), shape((atoms, waves), BF16), shape((part_rows, 128), BF16)),
        scratch_shapes=[pltpu.VMEM((3, atoms, 128), F32), pltpu.VMEM((8, atoms), F32)],
        name="tables",
    )(positions, features, w_charge_first, wave_vectors)
    sums = everything(part, "fold_first")
    hidden_first, values, force_first = pl.pallas_call(
        first_project_kernel,
        out_shape=(shape((atoms, hid), BF16), shape((kv * atoms, hid), BF16), shape((3, atoms), F32)),
        scratch_shapes=[pltpu.VMEM((4 * chan, waves), BF16)] * 2,
        name="project_first",
    )(sums, cos_table, sin_table, wave_vectors, features, w_charge_first, w_long_first, w_value)

    v_dom = lax.all_to_all(values, "kv", 0, 0, tiled=True)
    to_next, to_previous = pl.pallas_call(
        halo_kernel,
        grid=(1,),
        in_specs=[
            pl.BlockSpec((2, 128), lambda i, b=b: (0, b), memory_space=pltpu.SMEM) for b in range(halo // 128)
        ] + [pl.BlockSpec((kv * atoms, hid), lambda i: (0, 0))],
        out_specs=(pl.BlockSpec((halo, hid), lambda i: (0, 0)), pl.BlockSpec((halo, hid), lambda i: (0, 0))),
        out_shape=(shape((halo, hid), BF16), shape((halo, hid), BF16)),
        scratch_shapes=[pltpu.VMEM((kv * atoms, hid), F32), pltpu.VMEM((2, halo, hid), F32)],
        name="halo_rows",
    )(*[lists] * (halo // 128), v_dom)
    from_below = lax.ppermute(to_next, "dom", [(i, (i + 1) % doms) for i in range(doms)])
    from_above = lax.ppermute(to_previous, "dom", [(i, (i - 1) % doms) for i in range(doms)])

    steps = 8
    halves = atoms // 128
    whole = lambda dims: pl.BlockSpec(dims, lambda i: (0, 0))
    weights = pl.pallas_call(
        weight_kernel,
        grid=(steps,),
        in_specs=[
            whole((1, atoms)),
            whole((slots, atoms)),
            whole(w_filter.shape),
        ],
        out_specs=pl.BlockSpec((atoms // steps, slots, hid), lambda i: (i, 0, 0)),
        out_shape=shape((atoms, slots, hid), F32),
        scratch_shapes=[
            pltpu.VMEM((atoms, slots), F32),
            pltpu.VMEM((atoms // 2, 2 * slots), F32),
            pltpu.VMEM((atoms // 2, 2 * slots), F32),
            pltpu.VMEM((2 * w_filter.shape[0], hid), BF16),
        ],
        cost_estimate=pl.CostEstimate(
            flops=2 * atoms * slots * hid * 32,
            bytes_accessed=atoms * slots * hid * 4,
            transcendentals=atoms * slots * 16,
        ),
        name="slot_weights",
    )(nbr_count.reshape(1, atoms), dist_t, w_filter)

    blocks = [(b, h) for b in range(slots // 8) for h in range(halves)]
    hidden_second, part = pl.pallas_call(
        lambda *refs: neighbour_kernel(*refs, scale=scale),
        grid=(steps,),
        in_specs=[
            pl.BlockSpec((8, 128), lambda i, at=at: at, memory_space=pltpu.SMEM) for at in blocks
        ] + [
            pl.BlockSpec((halves, 128 // steps, slots, hid), lambda i: (0, i, 0, 0)),
            whole((kv * atoms, hid)),
            whole((halo, hid)),
            whole((halo, hid)),
            whole((atoms, hid)),
            whole((chan, hid)),
            whole((atoms, waves)),
            whole((atoms, waves)),
            whole((3, waves)),
        ],
        out_specs=(whole((atoms, hid)), whole((part_rows, 128))),
        out_shape=(shape((atoms, hid), BF16), shape((part_rows, 128), BF16)),
        scratch_shapes=[pltpu.VMEM((kv * atoms + 2 * halo, hid), F32), pltpu.VMEM((8 * atoms, hid), F32)],
        name="neighbours",
    )(
        *[index_t] * len(blocks), weights.reshape(halves, 128, slots, hid), v_dom, from_below, from_above,
        hidden_first, w_charge_second, cos_table, sin_table, wave_vectors,
    )
    sums = everything(part, "fold_second")
    return pl.pallas_call(
        last_project_kernel,
        out_shape=(shape((atoms, hid), BF16), shape((3, atoms), F32)),
        scratch_shapes=[pltpu.VMEM((4 * chan, waves), BF16)] * 2,
        name="project_second",
    )(sums, cos_table, sin_table, wave_vectors, hidden_second, w_charge_second, w_long_second, force_first)


def solution(mesh):
    return jax.shard_map(
        local,
        mesh=mesh,
        in_specs=(
            P(None, EVERY), P(EVERY, None), P(EVERY, None), P(EVERY), P(EVERY, None), P("dom", None, None),
            P(), P(), P(), P(), P(), P(), P(),
        ),
        out_specs=(P(EVERY, None), P(None, EVERY)),
        check_vma=False,
    )
```

```python
import math

import jax
import jax.numpy as jnp
from jax import lax
from jax.experimental import pallas as pl
from jax.experimental.pallas import tpu as pltpu
from jax.sharding import PartitionSpec as P

F32 = jnp.float32
BF16 = jnp.bfloat16
HIGHEST = lax.Precision.HIGHEST
LONG_SCALE = 2.0
CELL = 60.0
EVERY = ("dom", "kv")

COS_COEF = (
    1.0,
    -19.73920440673828,
    64.93911743164062,
    -85.45014190673828,
    60.16762924194336,
    -25.967599868774414,
    6.528658390045166,
)
SIN_COEF = (
    6.2831854820251465,
    -41.34170150756836,
    81.60513305664062,
    -76.70301818847656,
    42.02592849731445,
    -14.899847030639648,
    3.2381374835968018,
)

NN = (((1,), (0,)), ((), ()))
NT = (((1,), (1,)), ((), ()))
TN = (((0,), (0,)), ((), ()))


def horner(coefs, v):
    total = v * coefs[-1] + coefs[-2]
    for coef in coefs[-3::-1]:
        total = total * v + coef
    return total


def dot(a, b, dims=NN, precision=None):
    return lax.dot_general(a, b, dims, precision=precision, preferred_element_type=F32)


def silu(x):
    return x / (1.0 + jnp.exp(-x))


def wave_weight(wave):
    sq_norm = wave[0:1] * wave[0:1] + wave[1:2] * wave[1:2] + wave[2:3] * wave[2:3]
    return jnp.exp(-0.5 * sq_norm) / (sq_norm + 1.0)


def split_rows(x):
    high = x.astype(BF16)
    return jnp.concatenate([high, (x - high.astype(F32)).astype(BF16)], axis=0)


def structure_part(charge_t, cos_ref, sin_ref, wave_ref, part_ref, scale):
    chan = charge_t.shape[0]
    waves = cos_ref.shape[1]
    rows = split_rows(charge_t)
    cos_sum = dot(rows, cos_ref[...])
    sin_sum = dot(rows, sin_ref[...])
    weight = wave_weight(wave_ref[...]) * scale
    cos_sum = (cos_sum[:chan] + cos_sum[chan:]) * weight
    sin_sum = (sin_sum[:chan] + sin_sum[chan:]) * weight
    for t in range(waves // 128):
        lanes = slice(t * 128, (t + 1) * 128)
        part_ref[t * 2 * chan : t * 2 * chan + chan, :] = cos_sum[:, lanes].astype(BF16)
        part_ref[t * 2 * chan + chan : (t + 1) * 2 * chan, :] = sin_sum[:, lanes].astype(BF16)


def table_kernel(pos_ref, feat_ref, wc_ref, wave_ref, cos_ref, sin_ref, part_ref, turns, pad, *, scale):
    atoms, waves = cos_ref.shape
    pad[...] = jnp.zeros_like(pad)
    pad[0:3, :] = pos_ref[...] * (1.0 / CELL)
    columns = jnp.transpose(pad[...])
    for c in range(3):
        turns[c] = jnp.broadcast_to(columns[:, c : c + 1], (atoms, 128))
    rows = 64

    def one_tile(t, carry):
        lanes = pl.ds(pl.multiple_of(t * 128, 128), 128)
        whole = jnp.round(wave_ref[:, lanes] * (CELL / (2.0 * math.pi)))
        for b in range(atoms // rows):
            at = slice(b * rows, (b + 1) * rows)
            u = (
                turns[0, at, :] * whole[0:1]
                + turns[1, at, :] * whole[1:2]
                + turns[2, at, :] * whole[2:3]
            )
            u = u - jnp.round(u)
            v = u * u
            cos_ref[at, lanes] = horner(COS_COEF, v).astype(BF16)
            sin_ref[at, lanes] = (u * horner(SIN_COEF, v)).astype(BF16)
        return carry

    lax.fori_loop(0, waves // 128, one_tile, 0)
    charge_t = dot(wc_ref[...], feat_ref[...], NT)
    structure_part(charge_t, cos_ref, sin_ref, wave_ref, part_ref, scale)


def fold_kernel(in_ref, out_ref):
    rows = in_ref.shape[0]
    total = jnp.sum(in_ref[...].astype(F32).reshape(rows // 8, 8, 128), axis=0)
    total = total + pltpu.roll(total, 4, 0)
    total = total + pltpu.roll(total, 2, 0)
    out_ref[...] = jnp.broadcast_to(total[None], (rows // 8, 8, 128)).reshape(rows, 128).astype(BF16)


def project(sums_ref, cos_ref, sin_ref, wave_ref, charge_t, with_cos, with_sin):
    chan = charge_t.shape[0]
    waves = cos_ref.shape[1]
    for t in range(waves // 128):
        lanes = slice(t * 128, (t + 1) * 128)
        wave = wave_ref[:, lanes]
        cos_w = sums_ref[t * 2 * chan : t * 2 * chan + chan, :].astype(F32)
        sin_w = sums_ref[t * 2 * chan + chan : (t + 1) * 2 * chan, :].astype(F32)
        with_cos[0:chan, lanes] = cos_w.astype(BF16)
        with_sin[0:chan, lanes] = sin_w.astype(BF16)
        for c in range(3):
            at = slice((c + 1) * chan, (c + 2) * chan)
            with_cos[at, lanes] = (-wave[c : c + 1] * sin_w).astype(BF16)
            with_sin[at, lanes] = (wave[c : c + 1] * cos_w).astype(BF16)
    both = dot(with_cos[...], cos_ref[...], NT) + dot(with_sin[...], sin_ref[...], NT)
    potential_t = both[:chan]
    force = [
        jnp.sum(charge_t * both[(c + 1) * chan : (c + 2) * chan], axis=0, keepdims=True)
        for c in range(3)
    ]
    return potential_t, force


def first_project_kernel(
    sums_ref, cos_ref, sin_ref, wave_ref, feat_ref, wc_ref, wl_ref, wv_ref,
    hidden_ref, values_ref, force_ref, with_cos, with_sin,
):
    charge_t = dot(wc_ref[...], feat_ref[...], NT)
    potential_t, force = project(sums_ref, cos_ref, sin_ref, wave_ref, charge_t, with_cos, with_sin)
    for c in range(3):
        force_ref[c : c + 1, :] = force[c]
    lifted = dot(potential_t, wl_ref[...], TN, HIGHEST)
    hidden = (feat_ref[...].astype(F32) + silu(lifted)).astype(BF16)
    hidden_ref[...] = hidden
    values = dot(hidden, wv_ref[...]).astype(BF16)
    atoms = values.shape[0]
    for j in range(values_ref.shape[0] // atoms):
        values_ref[j * atoms : (j + 1) * atoms, :] = values


def last_project_kernel(
    sums_ref, cos_ref, sin_ref, wave_ref, hidden_ref, wc_ref, wl_ref, force_in,
    feat_out, force_out, with_cos, with_sin,
):
    charge_t = dot(wc_ref[...], hidden_ref[...], NT)
    potential_t, force = project(sums_ref, cos_ref, sin_ref, wave_ref, charge_t, with_cos, with_sin)
    for c in range(3):
        force_out[c : c + 1, :] = force_in[c : c + 1, :] + force[c]
    lifted = dot(potential_t, wl_ref[...], TN, HIGHEST)
    feat_out[...] = (hidden_ref[...].astype(F32) + silu(lifted)).astype(BF16)


def row_tile(table, rows, bits):
    tiles = [table[pl.ds(row, 8, stride=0), :] for row in rows]
    for bit in bits:
        tiles = [jnp.where(bit, odd, even) for even, odd in zip(tiles[::2], tiles[1::2])]
    return tiles[0]


def sublane_bits():
    sub = lax.broadcasted_iota(jnp.int32, (8, 128), 0)
    return [(sub & bit) != 0 for bit in (1, 2, 4)]


def halo_kernel(*refs):
    lists, (values_ref, below_ref, above_ref, table, picked) = refs[:-5], refs[-5:]
    table[...] = values_ref[...].astype(F32)
    bits = sublane_bits()

    def some_rows(g, carry):
        first = g * 8
        at = [[first + j for j in range(8)] for side in (0, 1)]
        for b, list_ref in enumerate(lists):
            for side in (0, 1):
                rows = [list_ref[side, lane] for lane in at[side]]
                picked[side, pl.ds(pl.multiple_of(b * 128 + first, 8), 8), :] = row_tile(table, rows, bits)
        return carry

    lax.fori_loop(0, 16, some_rows, 0)
    below_ref[...] = picked[0].astype(BF16)
    above_ref[...] = picked[1].astype(BF16)


def weight_kernel(count_ref, dist_ref, wf_ref, out_ref, turned, near, taper, wide):
    step = pl.program_id(0)
    slots, atoms = dist_ref.shape
    basis = wf_ref.shape[0]
    pairs = out_ref.shape[0] // 2
    sharpness = ((basis - 1) / 4.5) ** 2

    def paired(block):
        turned[...] = jnp.transpose(block)
        return jnp.concatenate(
            [turned[pl.ds(0, atoms // 2, stride=2), :], turned[pl.ds(1, atoms // 2, stride=2), :]], axis=1
        )

    @pl.when(step == 0)
    def _():
        dist = dist_ref[...]
        scaled = dist * 0.1
        height = 0.5 * (horner(COS_COEF, scaled * scaled) + 1.0)
        slot = lax.broadcasted_iota(jnp.int32, (slots, atoms), 0)
        near[...] = paired(dist)
        taper[...] = paired(jnp.where(slot < count_ref[...], height, 0.0))
        wf_high = wf_ref[...].astype(BF16)
        wide[0:basis, :] = wf_high
        wide[basis : 2 * basis, :] = (wf_ref[...] - wf_high.astype(F32)).astype(BF16)

    centers = 0.5 + 4.5 / (basis - 1) * lax.broadcasted_iota(jnp.int32, (basis, 2 * slots), 0).astype(F32)
    for p in range(pairs):
        row = pl.ds(step * pairs + p, 1)
        away = near[row, :] - centers
        radial = (jnp.exp(-sharpness * (away * away)) * taper[row, :]).astype(BF16)
        both = dot(jnp.concatenate([radial, radial], axis=0), wide[...], TN)
        out_ref[2 * p] = both[:slots]
        out_ref[2 * p + 1] = both[slots:]


def neighbour_kernel(*refs, scale):
    count_ref, index_refs = refs[0], refs[1:-13]
    (
        weight_ref, values_ref, below_ref, above_ref, hidden_ref, wc_ref, cos_ref, sin_ref, wave_ref,
        hidden_out, part_ref, table, sums,
    ) = refs[-13:]
    step = pl.program_id(0)
    own = values_ref.shape[0]
    halo = below_ref.shape[0]
    halves, atoms, slots, _ = weight_ref.shape

    @pl.when(step == 0)
    def _():
        table[0:own, :] = values_ref[...].astype(F32)
        table[own : own + halo, :] = below_ref[...].astype(F32)
        table[own + halo : own + 2 * halo, :] = above_ref[...].astype(F32)

    bits = sublane_bits()
    for half in range(halves):

        def one_atom(a, carry, half=half):
            lane = step * atoms + a
            at = pl.ds(pl.multiple_of((half * 128 + lane) * 8, 8), 8)

            def some_slots(blocks):
                total = jnp.zeros((8, 128), F32)
                for b in blocks:
                    rows = [index_refs[b * halves + half][s, lane] for s in range(8)]
                    total = total + row_tile(table, rows, bits) * weight_ref[half, a, 8 * b : 8 * b + 8, :]
                return total

            middle = slots // 16
            sums[at, :] = some_slots(range(middle))

            @pl.when(count_ref[half * 128 + lane] > middle * 8)
            def _():
                sums[at, :] = sums[at, :] + some_slots(range(middle, slots // 8))

            return carry

        lax.fori_loop(0, atoms, one_atom, 0)

    @pl.when(step == pl.num_programs(0) - 1)
    def _():
        count = hidden_ref.shape[0]
        message = sums[pl.ds(0, count, stride=8), :]
        for k in range(1, 8):
            message = message + sums[pl.ds(k, count, stride=8), :]
        hidden = (hidden_ref[...].astype(F32) + silu(message)).astype(BF16)
        hidden_out[...] = hidden
        charge_t = dot(wc_ref[...], hidden, NT)
        structure_part(charge_t, cos_ref, sin_ref, wave_ref, part_ref, scale)


def shape(dims, kind):
    return jax.ShapeDtypeStruct(dims, kind)


def vmem(mib):
    return pltpu.CompilerParams(vmem_limit_bytes=mib * 1024 * 1024)


def everything(part, name):
    sums = lax.all_to_all(part, EVERY, 0, 0, tiled=True)
    folded = pl.pallas_call(fold_kernel, out_shape=shape(part.shape, BF16), compiler_params=vmem(2), name=name)(sums)
    return lax.all_to_all(folded, EVERY, 0, 0, tiled=True)


def local(
    positions, features, nbr_index, nbr_count, nbr_dist, halo_lists, wave_vectors,
    w_charge_first, w_long_first, w_value, w_filter, w_charge_second, w_long_second,
):
    atoms, hid = features.shape
    chan = w_charge_first.shape[1]
    waves = wave_vectors.shape[1]
    slots = nbr_index.shape[1]
    kv = lax.axis_size("kv")
    doms = lax.axis_size("dom")
    total_atoms = atoms * doms * kv
    scale = LONG_SCALE / math.sqrt(waves) / math.sqrt(total_atoms)
    part_rows = 2 * chan * waves // 128
    halo = halo_lists.shape[2]
    smem = pl.BlockSpec(memory_space=pltpu.SMEM)
    w_charge_first = w_charge_first.T
    w_charge_second = w_charge_second.T
    lists = halo_lists[0]
    index_t = nbr_index.T
    dist_t = nbr_dist.T

    cos_table, sin_table, part = pl.pallas_call(
        lambda *refs: table_kernel(*refs, scale=scale),
        out_shape=(shape((atoms, waves), BF16), shape((atoms, waves), BF16), shape((part_rows, 128), BF16)),
        scratch_shapes=[pltpu.VMEM((3, atoms, 128), F32), pltpu.VMEM((8, atoms), F32)],
        compiler_params=vmem(6),
        name="tables",
    )(positions, features, w_charge_first, wave_vectors)
    sums = everything(part, "fold_first")
    hidden_first, values, force_first = pl.pallas_call(
        first_project_kernel,
        out_shape=(shape((atoms, hid), BF16), shape((kv * atoms, hid), BF16), shape((3, atoms), F32)),
        scratch_shapes=[pltpu.VMEM((4 * chan, waves), BF16)] * 2,
        compiler_params=vmem(6),
        name="project_first",
    )(sums, cos_table, sin_table, wave_vectors, features, w_charge_first, w_long_first, w_value)

    v_dom = lax.all_to_all(values, "kv", 0, 0, tiled=True)
    to_next, to_previous = pl.pallas_call(
        halo_kernel,
        grid=(1,),
        in_specs=[
            pl.BlockSpec((2, 128), lambda i, b=b: (0, b), memory_space=pltpu.SMEM) for b in range(halo // 128)
        ] + [pl.BlockSpec((kv * atoms, hid), lambda i: (0, 0))],
        out_specs=(pl.BlockSpec((halo, hid), lambda i: (0, 0)), pl.BlockSpec((halo, hid), lambda i: (0, 0))),
        out_shape=(shape((halo, hid), BF16), shape((halo, hid), BF16)),
        scratch_shapes=[pltpu.VMEM((kv * atoms, hid), F32), pltpu.VMEM((2, halo, hid), F32)],
        compiler_params=vmem(6),
        name="halo_rows",
    )(*[lists] * (halo // 128), v_dom)
    from_below = lax.ppermute(to_next, "dom", [(i, (i + 1) % doms) for i in range(doms)])
    from_above = lax.ppermute(to_previous, "dom", [(i, (i - 1) % doms) for i in range(doms)])

    steps = 8
    halves = atoms // 128
    whole = lambda dims: pl.BlockSpec(dims, lambda i: (0, 0))
    weights = pl.pallas_call(
        weight_kernel,
        grid=(steps,),
        in_specs=[
            whole((1, atoms)),
            whole((slots, atoms)),
            whole(w_filter.shape),
        ],
        out_specs=pl.BlockSpec((atoms // steps, slots, hid), lambda i: (i, 0, 0)),
        out_shape=shape((atoms, slots, hid), F32),
        scratch_shapes=[
            pltpu.VMEM((atoms, slots), F32),
            pltpu.VMEM((atoms // 2, 2 * slots), F32),
            pltpu.VMEM((atoms // 2, 2 * slots), F32),
            pltpu.VMEM((2 * w_filter.shape[0], hid), BF16),
        ],
        cost_estimate=pl.CostEstimate(
            flops=2 * atoms * slots * hid * 32,
            bytes_accessed=atoms * slots * hid * 4,
            transcendentals=atoms * slots * 16,
        ),
        compiler_params=vmem(6),
        name="slot_weights",
    )(nbr_count.reshape(1, atoms), dist_t, w_filter)

    blocks = [(b, h) for b in range(slots // 8) for h in range(halves)]
    hidden_second, part = pl.pallas_call(
        lambda *refs: neighbour_kernel(*refs, scale=scale),
        grid=(steps,),
        in_specs=[smem] + [
            pl.BlockSpec((8, 128), lambda i, at=at: at, memory_space=pltpu.SMEM) for at in blocks
        ] + [
            pl.BlockSpec((halves, 128 // steps, slots, hid), lambda i: (0, i, 0, 0)),
            whole((kv * atoms, hid)),
            whole((halo, hid)),
            whole((halo, hid)),
            whole((atoms, hid)),
            whole((chan, hid)),
            whole((atoms, waves)),
            whole((atoms, waves)),
            whole((3, waves)),
        ],
        out_specs=(whole((atoms, hid)), whole((part_rows, 128))),
        out_shape=(shape((atoms, hid), BF16), shape((part_rows, 128), BF16)),
        scratch_shapes=[pltpu.VMEM((kv * atoms + 2 * halo, hid), F32), pltpu.VMEM((8 * atoms, hid), F32)],
        compiler_params=vmem(14),
        name="neighbours",
    )(
        nbr_count, *[index_t] * len(blocks), weights.reshape(halves, 128, slots, hid), v_dom, from_below, from_above,
        hidden_first, w_charge_second, cos_table, sin_table, wave_vectors,
    )
    sums = everything(part, "fold_second")
    return pl.pallas_call(
        last_project_kernel,
        out_shape=(shape((atoms, hid), BF16), shape((3, atoms), F32)),
        scratch_shapes=[pltpu.VMEM((4 * chan, waves), BF16)] * 2,
        compiler_params=vmem(6),
        name="project_second",
    )(sums, cos_table, sin_table, wave_vectors, hidden_second, w_charge_second, w_long_second, force_first)


def solution(mesh):
    return jax.shard_map(
        local,
        mesh=mesh,
        in_specs=(
            P(None, EVERY), P(EVERY, None), P(EVERY, None), P(EVERY), P(EVERY, None), P("dom", None, None),
            P(), P(), P(), P(), P(), P(), P(),
        ),
        out_specs=(P(EVERY, None), P(None, EVERY)),
        check_vma=False,
    )
```

```python
import math

import jax
import jax.numpy as jnp
from jax import lax
from jax.experimental import pallas as pl
from jax.experimental.pallas import tpu as pltpu
from jax.sharding import PartitionSpec as P

F32 = jnp.float32
BF16 = jnp.bfloat16
HIGHEST = lax.Precision.HIGHEST
LONG_SCALE = 2.0
CELL = 60.0
PARTS = (("xlo", 2), ("z", 8), ("core", 2), ("y", 4), ("xhi", 2))
EVERY = tuple(name for name, _ in PARTS)
DOM = ("xlo", "z", "core")
KV = ("y", "xhi")
COLUMN = ("z", "core")
PLANE = ("xlo", "y", "xhi")

COS_COEF = (
    1.0,
    -19.73920440673828,
    64.93911743164062,
    -85.45014190673828,
    60.16762924194336,
    -25.967599868774414,
    6.528658390045166,
)
SIN_COEF = (
    6.2831854820251465,
    -41.34170150756836,
    81.60513305664062,
    -76.70301818847656,
    42.02592849731445,
    -14.899847030639648,
    3.2381374835968018,
)

NN = (((1,), (0,)), ((), ()))
NT = (((1,), (1,)), ((), ()))
TN = (((0,), (0,)), ((), ()))


def horner(coefs, v):
    total = v * coefs[-1] + coefs[-2]
    for coef in coefs[-3::-1]:
        total = total * v + coef
    return total


def dot(a, b, dims=NN, precision=None):
    return lax.dot_general(a, b, dims, precision=precision, preferred_element_type=F32)


def silu(x):
    return x / (1.0 + jnp.exp(-x))


def wave_weight(wave):
    sq_norm = wave[0:1] * wave[0:1] + wave[1:2] * wave[1:2] + wave[2:3] * wave[2:3]
    return jnp.exp(-0.5 * sq_norm) / (sq_norm + 1.0)


def split_rows(x):
    high = x.astype(BF16)
    return jnp.concatenate([high, (x - high.astype(F32)).astype(BF16)], axis=0)


def structure_part(charge_t, cos_ref, sin_ref, wave_ref, part_ref, scale):
    chan = charge_t.shape[0]
    waves = cos_ref.shape[1]
    rows = split_rows(charge_t)
    cos_sum = dot(rows, cos_ref[...])
    sin_sum = dot(rows, sin_ref[...])
    weight = wave_weight(wave_ref[...]) * scale
    cos_sum = (cos_sum[:chan] + cos_sum[chan:]) * weight
    sin_sum = (sin_sum[:chan] + sin_sum[chan:]) * weight
    for t in range(waves // 128):
        lanes = slice(t * 128, (t + 1) * 128)
        part_ref[t * 2 * chan : t * 2 * chan + chan, :] = cos_sum[:, lanes].astype(BF16)
        part_ref[t * 2 * chan + chan : (t + 1) * 2 * chan, :] = sin_sum[:, lanes].astype(BF16)


def table_kernel(pos_ref, feat_ref, wc_ref, wave_ref, cos_ref, sin_ref, part_ref, turns, pad, *, scale):
    atoms, waves = cos_ref.shape
    pad[...] = jnp.zeros_like(pad)
    pad[0:3, :] = pos_ref[...] * (1.0 / CELL)
    columns = jnp.transpose(pad[...])
    for c in range(3):
        turns[c] = jnp.broadcast_to(columns[:, c : c + 1], (atoms, 128))
    rows = 64

    def one_tile(t, carry):
        lanes = pl.ds(pl.multiple_of(t * 128, 128), 128)
        whole = jnp.round(wave_ref[:, lanes] * (CELL / (2.0 * math.pi)))
        for b in range(atoms // rows):
            at = slice(b * rows, (b + 1) * rows)
            u = (
                turns[0, at, :] * whole[0:1]
                + turns[1, at, :] * whole[1:2]
                + turns[2, at, :] * whole[2:3]
            )
            u = u - jnp.round(u)
            v = u * u
            cos_ref[at, lanes] = horner(COS_COEF, v).astype(BF16)
            sin_ref[at, lanes] = (u * horner(SIN_COEF, v)).astype(BF16)
        return carry

    lax.fori_loop(0, waves // 128, one_tile, 0)
    charge_t = dot(wc_ref[...], feat_ref[...], NT)
    structure_part(charge_t, cos_ref, sin_ref, wave_ref, part_ref, scale)


def fold_kernel(in_ref, out_ref, *, members, copies):
    rows = in_ref.shape[0] // members
    total = in_ref[0:rows, :].astype(F32)
    for m in range(1, members):
        total = total + in_ref[m * rows : (m + 1) * rows, :].astype(F32)
    total = total.astype(BF16)
    for m in range(copies):
        out_ref[m * rows : (m + 1) * rows, :] = total


def project(sums_ref, cos_ref, sin_ref, wave_ref, charge_t, with_cos, with_sin):
    chan = charge_t.shape[0]
    waves = cos_ref.shape[1]
    for t in range(waves // 128):
        lanes = slice(t * 128, (t + 1) * 128)
        wave = wave_ref[:, lanes]
        cos_w = sums_ref[t * 2 * chan : t * 2 * chan + chan, :].astype(F32)
        sin_w = sums_ref[t * 2 * chan + chan : (t + 1) * 2 * chan, :].astype(F32)
        with_cos[0:chan, lanes] = cos_w.astype(BF16)
        with_sin[0:chan, lanes] = sin_w.astype(BF16)
        for c in range(3):
            at = slice((c + 1) * chan, (c + 2) * chan)
            with_cos[at, lanes] = (-wave[c : c + 1] * sin_w).astype(BF16)
            with_sin[at, lanes] = (wave[c : c + 1] * cos_w).astype(BF16)
    both = dot(with_cos[...], cos_ref[...], NT) + dot(with_sin[...], sin_ref[...], NT)
    potential_t = both[:chan]
    force = [
        jnp.sum(charge_t * both[(c + 1) * chan : (c + 2) * chan], axis=0, keepdims=True)
        for c in range(3)
    ]
    return potential_t, force


def first_project_kernel(
    sums_ref, cos_ref, sin_ref, wave_ref, feat_ref, wc_ref, wl_ref, wv_ref,
    hidden_ref, values_ref, force_ref, with_cos, with_sin,
):
    charge_t = dot(wc_ref[...], feat_ref[...], NT)
    potential_t, force = project(sums_ref, cos_ref, sin_ref, wave_ref, charge_t, with_cos, with_sin)
    for c in range(3):
        force_ref[c : c + 1, :] = force[c]
    lifted = dot(potential_t, wl_ref[...], TN, HIGHEST)
    hidden = (feat_ref[...].astype(F32) + silu(lifted)).astype(BF16)
    hidden_ref[...] = hidden
    values = dot(hidden, wv_ref[...]).astype(BF16)
    atoms = values.shape[0]
    for j in range(values_ref.shape[0] // atoms):
        values_ref[j * atoms : (j + 1) * atoms, :] = values


def last_project_kernel(
    sums_ref, cos_ref, sin_ref, wave_ref, hidden_ref, wc_ref, wl_ref, force_in,
    feat_out, force_out, with_cos, with_sin,
):
    charge_t = dot(wc_ref[...], hidden_ref[...], NT)
    potential_t, force = project(sums_ref, cos_ref, sin_ref, wave_ref, charge_t, with_cos, with_sin)
    for c in range(3):
        force_out[c : c + 1, :] = force_in[c : c + 1, :] + force[c]
    lifted = dot(potential_t, wl_ref[...], TN, HIGHEST)
    feat_out[...] = (hidden_ref[...].astype(F32) + silu(lifted)).astype(BF16)


def row_tile(table, rows, bits):
    tiles = [table[pl.ds(row, 8, stride=0), :] for row in rows]
    for bit in bits:
        tiles = [jnp.where(bit, odd, even) for even, odd in zip(tiles[::2], tiles[1::2])]
    return tiles[0]


def sublane_bits():
    sub = lax.broadcasted_iota(jnp.int32, (8, 128), 0)
    return [(sub & bit) != 0 for bit in (1, 2, 4)]


def halo_kernel(*refs):
    lists, (values_ref, below_ref, above_ref, table, picked) = refs[:-5], refs[-5:]
    table[...] = values_ref[...].astype(F32)
    bits = sublane_bits()

    def some_rows(g, carry):
        first = g * 8
        at = [[first + j for j in range(8)] for side in (0, 1)]
        for b, list_ref in enumerate(lists):
            for side in (0, 1):
                rows = [list_ref[side, lane] for lane in at[side]]
                picked[side, pl.ds(pl.multiple_of(b * 128 + first, 8), 8), :] = row_tile(table, rows, bits)
        return carry

    lax.fori_loop(0, 16, some_rows, 0)
    below_ref[...] = picked[0].astype(BF16)
    above_ref[...] = picked[1].astype(BF16)


def weight_kernel(count_ref, dist_ref, wf_ref, out_ref, turned, near, taper, wide):
    step = pl.program_id(0)
    slots, atoms = dist_ref.shape
    basis = wf_ref.shape[0]
    pairs = out_ref.shape[0] // 2
    sharpness = ((basis - 1) / 4.5) ** 2

    def paired(block):
        turned[...] = jnp.transpose(block)
        return jnp.concatenate(
            [turned[pl.ds(0, atoms // 2, stride=2), :], turned[pl.ds(1, atoms // 2, stride=2), :]], axis=1
        )

    @pl.when(step == 0)
    def _():
        dist = dist_ref[...]
        scaled = dist * 0.1
        height = 0.5 * (horner(COS_COEF, scaled * scaled) + 1.0)
        slot = lax.broadcasted_iota(jnp.int32, (slots, atoms), 0)
        near[...] = paired(dist)
        taper[...] = paired(jnp.where(slot < count_ref[...], height, 0.0))
        wf_high = wf_ref[...].astype(BF16)
        wide[0:basis, :] = wf_high
        wide[basis : 2 * basis, :] = (wf_ref[...] - wf_high.astype(F32)).astype(BF16)

    centers = 0.5 + 4.5 / (basis - 1) * lax.broadcasted_iota(jnp.int32, (basis, 2 * slots), 0).astype(F32)
    for p in range(pairs):
        row = pl.ds(step * pairs + p, 1)
        away = near[row, :] - centers
        radial = (jnp.exp(-sharpness * (away * away)) * taper[row, :]).astype(BF16)
        both = dot(jnp.concatenate([radial, radial], axis=0), wide[...], TN)
        out_ref[2 * p] = both[:slots]
        out_ref[2 * p + 1] = both[slots:]


def neighbour_kernel(*refs, scale):
    count_ref, index_refs = refs[0], refs[1:-13]
    (
        weight_ref, values_ref, below_ref, above_ref, hidden_ref, wc_ref, cos_ref, sin_ref, wave_ref,
        hidden_out, part_ref, table, sums,
    ) = refs[-13:]
    step = pl.program_id(0)
    own = values_ref.shape[0]
    halo = below_ref.shape[0]
    halves, atoms, slots, _ = weight_ref.shape

    @pl.when(step == 0)
    def _():
        table[0:own, :] = values_ref[...].astype(F32)
        table[own : own + halo, :] = below_ref[...].astype(F32)
        table[own + halo : own + 2 * halo, :] = above_ref[...].astype(F32)

    bits = sublane_bits()
    for half in range(halves):

        def one_atom(a, carry, half=half):
            lane = step * atoms + a
            at = pl.ds(pl.multiple_of((half * 128 + lane) * 8, 8), 8)

            def some_slots(blocks):
                total = jnp.zeros((8, 128), F32)
                for b in blocks:
                    rows = [index_refs[b * halves + half][s, lane] for s in range(8)]
                    total = total + row_tile(table, rows, bits) * weight_ref[half, a, 8 * b : 8 * b + 8, :]
                return total

            middle = slots // 16
            sums[at, :] = some_slots(range(middle))

            @pl.when(count_ref[half * 128 + lane] > middle * 8)
            def _():
                sums[at, :] = sums[at, :] + some_slots(range(middle, slots // 8))

            return carry

        lax.fori_loop(0, atoms, one_atom, 0)

    @pl.when(step == pl.num_programs(0) - 1)
    def _():
        count = hidden_ref.shape[0]
        message = sums[pl.ds(0, count, stride=8), :]
        for k in range(1, 8):
            message = message + sums[pl.ds(k, count, stride=8), :]
        hidden = (hidden_ref[...].astype(F32) + silu(message)).astype(BF16)
        hidden_out[...] = hidden
        charge_t = dot(wc_ref[...], hidden, NT)
        structure_part(charge_t, cos_ref, sin_ref, wave_ref, part_ref, scale)


def shape(dims, kind):
    return jax.ShapeDtypeStruct(dims, kind)


def in_hbm(*arrays):
    return tuple(pltpu.with_memory_space_constraint(array, pltpu.HBM) for array in arrays)


def vmem(mib):
    return pltpu.CompilerParams(vmem_limit_bytes=mib * 1024 * 1024)


def fold(sums, members, copies, name):
    rows = sums.shape[0] // members
    return pl.pallas_call(
        lambda *refs: fold_kernel(*refs, members=members, copies=copies),
        out_shape=shape((copies * rows, sums.shape[1]), BF16),
        compiler_params=vmem(2),
        name=name,
    )(sums)


def everything(part, name):
    column = lax.axis_size(COLUMN)
    plane = lax.axis_size(PLANE)
    share = lax.all_to_all(part, COLUMN, 0, 0, tiled=True)
    share = fold(share, column, plane, name + "_column")
    share = lax.all_to_all(share, PLANE, 0, 0, tiled=True)
    share = fold(share, plane, column, name + "_plane")
    return lax.all_to_all(share, COLUMN, 0, 0, tiled=True)


def local(
    positions, features, nbr_index, nbr_count, nbr_dist, halo_lists, wave_vectors,
    w_charge_first, w_long_first, w_value, w_filter, w_charge_second, w_long_second,
):
    atoms, hid = features.shape
    chan = w_charge_first.shape[1]
    waves = wave_vectors.shape[1]
    slots = nbr_index.shape[1]
    kv = lax.axis_size(KV)
    doms = lax.axis_size(DOM)
    total_atoms = atoms * doms * kv
    scale = LONG_SCALE / math.sqrt(waves) / math.sqrt(total_atoms)
    part_rows = 2 * chan * waves // 128
    halo = halo_lists.shape[2]
    smem = pl.BlockSpec(memory_space=pltpu.SMEM)
    w_charge_first = w_charge_first.T
    w_charge_second = w_charge_second.T
    lists = halo_lists[0]
    index_t = nbr_index.T
    dist_t = nbr_dist.T

    cos_table, sin_table, part = pl.pallas_call(
        lambda *refs: table_kernel(*refs, scale=scale),
        out_shape=(shape((atoms, waves), BF16), shape((atoms, waves), BF16), shape((part_rows, 128), BF16)),
        scratch_shapes=[pltpu.VMEM((3, atoms, 128), F32), pltpu.VMEM((8, atoms), F32)],
        compiler_params=vmem(6),
        name="tables",
    )(*in_hbm(positions, features, w_charge_first, wave_vectors))
    sums = everything(part, "fold_first")
    hidden_first, values, force_first = pl.pallas_call(
        first_project_kernel,
        out_shape=(shape((atoms, hid), BF16), shape((kv * atoms, hid), BF16), shape((3, atoms), F32)),
        scratch_shapes=[pltpu.VMEM((4 * chan, waves), BF16)] * 2,
        compiler_params=vmem(6),
        name="project_first",
    )(sums, cos_table, sin_table, *in_hbm(wave_vectors, features, w_charge_first, w_long_first, w_value))

    v_dom = lax.all_to_all(values, KV, 0, 0, tiled=True)
    to_next, to_previous = pl.pallas_call(
        halo_kernel,
        grid=(1,),
        in_specs=[
            pl.BlockSpec((2, 128), lambda i, b=b: (0, b), memory_space=pltpu.SMEM) for b in range(halo // 128)
        ] + [pl.BlockSpec((kv * atoms, hid), lambda i: (0, 0))],
        out_specs=(pl.BlockSpec((halo, hid), lambda i: (0, 0)), pl.BlockSpec((halo, hid), lambda i: (0, 0))),
        out_shape=(shape((halo, hid), BF16), shape((halo, hid), BF16)),
        scratch_shapes=[pltpu.VMEM((kv * atoms, hid), F32), pltpu.VMEM((2, halo, hid), F32)],
        compiler_params=vmem(6),
        name="halo_rows",
    )(*in_hbm(*[lists] * (halo // 128)), v_dom)
    from_below = lax.ppermute(to_next, DOM, [(i, (i + 1) % doms) for i in range(doms)])
    from_above = lax.ppermute(to_previous, DOM, [(i, (i - 1) % doms) for i in range(doms)])

    steps = 8
    halves = atoms // 128
    whole = lambda dims: pl.BlockSpec(dims, lambda i: (0, 0))
    weights = pl.pallas_call(
        weight_kernel,
        grid=(steps,),
        in_specs=[
            whole((1, atoms)),
            whole((slots, atoms)),
            whole(w_filter.shape),
        ],
        out_specs=pl.BlockSpec((atoms // steps, slots, hid), lambda i: (i, 0, 0)),
        out_shape=shape((atoms, slots, hid), F32),
        scratch_shapes=[
            pltpu.VMEM((atoms, slots), F32),
            pltpu.VMEM((atoms // 2, 2 * slots), F32),
            pltpu.VMEM((atoms // 2, 2 * slots), F32),
            pltpu.VMEM((2 * w_filter.shape[0], hid), BF16),
        ],
        cost_estimate=pl.CostEstimate(
            flops=2 * atoms * slots * hid * 32,
            bytes_accessed=atoms * slots * hid * 4,
            transcendentals=atoms * slots * 16,
        ),
        compiler_params=vmem(6),
        name="slot_weights",
    )(*in_hbm(nbr_count.reshape(1, atoms), dist_t, w_filter))

    blocks = [(b, h) for b in range(slots // 8) for h in range(halves)]
    hidden_second, part = pl.pallas_call(
        lambda *refs: neighbour_kernel(*refs, scale=scale),
        grid=(steps,),
        in_specs=[smem] + [
            pl.BlockSpec((8, 128), lambda i, at=at: at, memory_space=pltpu.SMEM) for at in blocks
        ] + [
            pl.BlockSpec((halves, 128 // steps, slots, hid), lambda i: (0, i, 0, 0)),
            whole((kv * atoms, hid)),
            whole((halo, hid)),
            whole((halo, hid)),
            whole((atoms, hid)),
            whole((chan, hid)),
            whole((atoms, waves)),
            whole((atoms, waves)),
            whole((3, waves)),
        ],
        out_specs=(whole((atoms, hid)), whole((part_rows, 128))),
        out_shape=(shape((atoms, hid), BF16), shape((part_rows, 128), BF16)),
        scratch_shapes=[pltpu.VMEM((kv * atoms + 2 * halo, hid), F32), pltpu.VMEM((8 * atoms, hid), F32)],
        compiler_params=vmem(14),
        name="neighbours",
    )(
        *in_hbm(nbr_count, *[index_t] * len(blocks)), weights.reshape(halves, 128, slots, hid), v_dom, from_below, from_above,
        hidden_first, *in_hbm(w_charge_second), cos_table, sin_table, *in_hbm(wave_vectors),
    )
    sums = everything(part, "fold_second")
    return pl.pallas_call(
        last_project_kernel,
        out_shape=(shape((atoms, hid), BF16), shape((3, atoms), F32)),
        scratch_shapes=[pltpu.VMEM((4 * chan, waves), BF16)] * 2,
        compiler_params=vmem(6),
        name="project_second",
    )(
        sums, cos_table, sin_table, *in_hbm(wave_vectors), hidden_second,
        *in_hbm(w_charge_second, w_long_second), force_first,
    )


def solution(mesh):
    sizes = tuple(size for _, size in PARTS)
    return jax.shard_map(
        local,
        mesh=jax.sharding.Mesh(mesh.devices.reshape(sizes), EVERY),
        in_specs=(
            P(None, EVERY), P(EVERY, None), P(EVERY, None), P(EVERY), P(EVERY, None), P(DOM, None, None),
            P(), P(), P(), P(), P(), P(), P(),
        ),
        out_specs=(P(EVERY, None), P(None, EVERY)),
        check_vma=False,
    )
```

```python
import math

import jax
import jax.numpy as jnp
from jax import lax
from jax.experimental import pallas as pl
from jax.experimental.pallas import tpu as pltpu
from jax.sharding import PartitionSpec as P

F32 = jnp.float32
BF16 = jnp.bfloat16
HIGHEST = lax.Precision.HIGHEST
LONG_SCALE = 2.0
CELL = 60.0
PARTS = (("xlo", 2), ("z", 8), ("core", 2), ("y", 4), ("xhi", 2))
EVERY = tuple(name for name, _ in PARTS)
DOM = ("xlo", "z", "core")
KV = ("y", "xhi")
LINE = ("z",)
PLANE = ("xlo", "core", "y", "xhi")

COS_COEF = (
    1.0,
    -19.73920440673828,
    64.93911743164062,
    -85.45014190673828,
    60.16762924194336,
    -25.967599868774414,
    6.528658390045166,
)
SIN_COEF = (
    6.2831854820251465,
    -41.34170150756836,
    81.60513305664062,
    -76.70301818847656,
    42.02592849731445,
    -14.899847030639648,
    3.2381374835968018,
)

NN = (((1,), (0,)), ((), ()))
NT = (((1,), (1,)), ((), ()))
TN = (((0,), (0,)), ((), ()))


def horner(coefs, v):
    total = v * coefs[-1] + coefs[-2]
    for coef in coefs[-3::-1]:
        total = total * v + coef
    return total


def dot(a, b, dims=NN, precision=None):
    return lax.dot_general(a, b, dims, precision=precision, preferred_element_type=F32)


def silu(x):
    return x / (1.0 + jnp.exp(-x))


def wave_weight(wave):
    sq_norm = wave[0:1] * wave[0:1] + wave[1:2] * wave[1:2] + wave[2:3] * wave[2:3]
    return jnp.exp(-0.5 * sq_norm) / (sq_norm + 1.0)


def split_rows(x):
    high = x.astype(BF16)
    return jnp.concatenate([high, (x - high.astype(F32)).astype(BF16)], axis=0)


def structure_part(charge_t, cos_ref, sin_ref, wave_ref, part_ref, scale):
    chan = charge_t.shape[0]
    waves = cos_ref.shape[1]
    rows = split_rows(charge_t)
    cos_sum = dot(rows, cos_ref[...])
    sin_sum = dot(rows, sin_ref[...])
    weight = wave_weight(wave_ref[...]) * scale
    cos_sum = (cos_sum[:chan] + cos_sum[chan:]) * weight
    sin_sum = (sin_sum[:chan] + sin_sum[chan:]) * weight
    for t in range(waves // 128):
        lanes = slice(t * 128, (t + 1) * 128)
        part_ref[t * 2 * chan : t * 2 * chan + chan, :] = cos_sum[:, lanes].astype(BF16)
        part_ref[t * 2 * chan + chan : (t + 1) * 2 * chan, :] = sin_sum[:, lanes].astype(BF16)


def table_kernel(*refs, scale):
    later = (len(refs) - 6) // 2
    pos_ref, kept_in, cos_ref, sin_ref, part_ref = refs[0], refs[1 : 1 + later], *refs[1 + later : 4 + later]
    kept_out, turns, pad = refs[4 + later : -2], *refs[-2:]
    feat_ref, wc_ref, wave_ref = kept_in[:3]
    atoms, waves = cos_ref.shape
    for in_ref, out_ref in zip(kept_in, kept_out):
        out_ref[...] = in_ref[...]
    pad[...] = jnp.zeros_like(pad)
    pad[0:3, :] = pos_ref[...] * (1.0 / CELL)
    columns = jnp.transpose(pad[...])
    for c in range(3):
        turns[c] = jnp.broadcast_to(columns[:, c : c + 1], (atoms, 128))
    rows = 64

    def one_tile(t, carry):
        lanes = pl.ds(pl.multiple_of(t * 128, 128), 128)
        whole = jnp.round(wave_ref[:, lanes] * (CELL / (2.0 * math.pi)))
        for b in range(atoms // rows):
            at = slice(b * rows, (b + 1) * rows)
            u = (
                turns[0, at, :] * whole[0:1]
                + turns[1, at, :] * whole[1:2]
                + turns[2, at, :] * whole[2:3]
            )
            u = u - jnp.round(u)
            v = u * u
            cos_ref[at, lanes] = horner(COS_COEF, v).astype(BF16)
            sin_ref[at, lanes] = (u * horner(SIN_COEF, v)).astype(BF16)
        return carry

    lax.fori_loop(0, waves // 128, one_tile, 0)
    charge_t = dot(wc_ref[...], feat_ref[...], NT)
    structure_part(charge_t, cos_ref, sin_ref, wave_ref, part_ref, scale)


def fold_kernel(in_ref, out_ref, *, members, copies):
    rows = in_ref.shape[0] // members
    total = in_ref[0:rows, :].astype(F32)
    for m in range(1, members):
        total = total + in_ref[m * rows : (m + 1) * rows, :].astype(F32)
    total = total.astype(out_ref.dtype)
    for m in range(copies):
        out_ref[m * rows : (m + 1) * rows, :] = total


def project(sums_ref, cos_ref, sin_ref, wave_ref, charge_t, with_cos, with_sin):
    chan = charge_t.shape[0]
    waves = cos_ref.shape[1]
    for t in range(waves // 128):
        lanes = slice(t * 128, (t + 1) * 128)
        wave = wave_ref[:, lanes]
        cos_w = sums_ref[t * 2 * chan : t * 2 * chan + chan, :].astype(F32)
        sin_w = sums_ref[t * 2 * chan + chan : (t + 1) * 2 * chan, :].astype(F32)
        with_cos[0:chan, lanes] = cos_w.astype(BF16)
        with_sin[0:chan, lanes] = sin_w.astype(BF16)
        for c in range(3):
            at = slice((c + 1) * chan, (c + 2) * chan)
            with_cos[at, lanes] = (-wave[c : c + 1] * sin_w).astype(BF16)
            with_sin[at, lanes] = (wave[c : c + 1] * cos_w).astype(BF16)
    both = dot(with_cos[...], cos_ref[...], NT) + dot(with_sin[...], sin_ref[...], NT)
    potential_t = both[:chan]
    force = [
        jnp.sum(charge_t * both[(c + 1) * chan : (c + 2) * chan], axis=0, keepdims=True)
        for c in range(3)
    ]
    return potential_t, force


def first_project_kernel(
    sums_ref, cos_ref, sin_ref, wave_ref, feat_ref, wc_ref, wl_ref, wv_ref,
    hidden_ref, values_ref, force_ref, with_cos, with_sin,
):
    charge_t = dot(wc_ref[...], feat_ref[...], NT)
    potential_t, force = project(sums_ref, cos_ref, sin_ref, wave_ref, charge_t, with_cos, with_sin)
    for c in range(3):
        force_ref[c : c + 1, :] = force[c]
    lifted = dot(potential_t, wl_ref[...], TN, HIGHEST)
    hidden = (feat_ref[...].astype(F32) + silu(lifted)).astype(BF16)
    hidden_ref[...] = hidden
    values = dot(hidden, wv_ref[...]).astype(BF16)
    atoms = values.shape[0]
    for j in range(values_ref.shape[0] // atoms):
        values_ref[j * atoms : (j + 1) * atoms, :] = values


def last_project_kernel(
    sums_ref, cos_ref, sin_ref, wave_ref, hidden_ref, wc_ref, wl_ref, force_in,
    feat_out, force_out, with_cos, with_sin,
):
    charge_t = dot(wc_ref[...], hidden_ref[...], NT)
    potential_t, force = project(sums_ref, cos_ref, sin_ref, wave_ref, charge_t, with_cos, with_sin)
    for c in range(3):
        force_out[c : c + 1, :] = force_in[c : c + 1, :] + force[c]
    lifted = dot(potential_t, wl_ref[...], TN, HIGHEST)
    feat_out[...] = (hidden_ref[...].astype(F32) + silu(lifted)).astype(BF16)


def row_tile(table, rows, bits):
    tiles = [table[pl.ds(row, 8, stride=0), :] for row in rows]
    for bit in bits:
        tiles = [jnp.where(bit, odd, even) for even, odd in zip(tiles[::2], tiles[1::2])]
    return tiles[0]


def sublane_bits():
    sub = lax.broadcasted_iota(jnp.int32, (8, 128), 0)
    return [(sub & bit) != 0 for bit in (1, 2, 4)]


def halo_kernel(*refs):
    lists, (values_ref, below_ref, above_ref, table, picked) = refs[:-5], refs[-5:]
    table[...] = values_ref[...].astype(F32)
    bits = sublane_bits()

    def some_rows(g, carry):
        first = g * 8
        at = [[first + j for j in range(8)] for side in (0, 1)]
        for b, list_ref in enumerate(lists):
            for side in (0, 1):
                rows = [list_ref[side, lane] for lane in at[side]]
                picked[side, pl.ds(pl.multiple_of(b * 128 + first, 8), 8), :] = row_tile(table, rows, bits)
        return carry

    lax.fori_loop(0, 16, some_rows, 0)
    below_ref[...] = picked[0].astype(BF16)
    above_ref[...] = picked[1].astype(BF16)


def weight_kernel(count_ref, dist_ref, wf_ref, out_ref, turned, near, taper, wide):
    step = pl.program_id(0)
    slots, atoms = dist_ref.shape
    basis = wf_ref.shape[0]
    pairs = out_ref.shape[0] // 2
    sharpness = ((basis - 1) / 4.5) ** 2

    def paired(block):
        turned[...] = jnp.transpose(block)
        return jnp.concatenate(
            [turned[pl.ds(0, atoms // 2, stride=2), :], turned[pl.ds(1, atoms // 2, stride=2), :]], axis=1
        )

    @pl.when(step == 0)
    def _():
        dist = dist_ref[...]
        scaled = dist * 0.1
        height = 0.5 * (horner(COS_COEF, scaled * scaled) + 1.0)
        slot = lax.broadcasted_iota(jnp.int32, (slots, atoms), 0)
        near[...] = paired(dist)
        taper[...] = paired(jnp.where(slot < count_ref[...], height, 0.0))
        wf_high = wf_ref[...].astype(BF16)
        wide[0:basis, :] = wf_high
        wide[basis : 2 * basis, :] = (wf_ref[...] - wf_high.astype(F32)).astype(BF16)

    centers = 0.5 + 4.5 / (basis - 1) * lax.broadcasted_iota(jnp.int32, (basis, 2 * slots), 0).astype(F32)
    for p in range(pairs):
        row = pl.ds(step * pairs + p, 1)
        away = near[row, :] - centers
        radial = (jnp.exp(-sharpness * (away * away)) * taper[row, :]).astype(BF16)
        both = dot(jnp.concatenate([radial, radial], axis=0), wide[...], TN)
        out_ref[2 * p] = both[:slots]
        out_ref[2 * p + 1] = both[slots:]


def neighbour_kernel(*refs, scale):
    count_ref, index_refs = refs[0], refs[1:-13]
    (
        weight_ref, values_ref, below_ref, above_ref, hidden_ref, wc_ref, cos_ref, sin_ref, wave_ref,
        hidden_out, part_ref, table, sums,
    ) = refs[-13:]
    step = pl.program_id(0)
    own = values_ref.shape[0]
    halo = below_ref.shape[0]
    halves, atoms, slots, _ = weight_ref.shape

    @pl.when(step == 0)
    def _():
        table[0:own, :] = values_ref[...].astype(F32)
        table[own : own + halo, :] = below_ref[...].astype(F32)
        table[own + halo : own + 2 * halo, :] = above_ref[...].astype(F32)

    bits = sublane_bits()
    for half in range(halves):

        def one_atom(a, carry, half=half):
            atom = half * 128 + step * atoms + a
            at = pl.ds(pl.multiple_of(atom * 8, 8), 8)
            spots = [atom + q * halves * 128 for q in range(4)]

            def some_slots(blocks):
                total = jnp.zeros((8, 128), F32)
                for b in blocks:
                    rows = [index_refs[2 * b + s // 4][spots[s % 4]] for s in range(8)]
                    total = total + row_tile(table, rows, bits) * weight_ref[half, a, 8 * b : 8 * b + 8, :]
                return total

            middle = slots // 16
            sums[at, :] = some_slots(range(middle))

            @pl.when(count_ref[atom] > middle * 8)
            def _():
                sums[at, :] = sums[at, :] + some_slots(range(middle, slots // 8))

            return carry

        lax.fori_loop(0, atoms, one_atom, 0)

    @pl.when(step == pl.num_programs(0) - 1)
    def _():
        count = hidden_ref.shape[0]
        message = sums[pl.ds(0, count, stride=8), :]
        for k in range(1, 8):
            message = message + sums[pl.ds(k, count, stride=8), :]
        hidden = (hidden_ref[...].astype(F32) + silu(message)).astype(BF16)
        hidden_out[...] = hidden
        charge_t = dot(wc_ref[...], hidden, NT)
        structure_part(charge_t, cos_ref, sin_ref, wave_ref, part_ref, scale)


def shape(dims, kind):
    return jax.ShapeDtypeStruct(dims, kind)


def in_hbm(*arrays):
    return tuple(pltpu.with_memory_space_constraint(array, pltpu.HBM) for array in arrays)


def vmem(mib):
    return pltpu.CompilerParams(vmem_limit_bytes=mib * 1024 * 1024)


def fold(sums, members, copies, kind, name):
    rows = sums.shape[0] // members
    return pl.pallas_call(
        lambda *refs: fold_kernel(*refs, members=members, copies=copies),
        out_shape=shape((copies * rows, sums.shape[1]), kind),
        compiler_params=vmem(2),
        name=name,
    )(sums)


def everything(part, name):
    line = lax.axis_size(LINE)
    plane = lax.axis_size(PLANE)
    share = lax.all_to_all(part, PLANE, 0, 0, tiled=True)
    share = fold(share, plane, line, F32, name + "_plane")
    share = lax.all_to_all(share, LINE, 0, 0, tiled=True)
    share = fold(share, line, plane, BF16, name + "_line")
    return lax.all_to_all(share, PLANE, 0, 0, tiled=True)


def local(
    positions, features, nbr_index, nbr_count, nbr_dist, halo_lists, wave_vectors,
    w_charge_first, w_long_first, w_value, w_filter, w_charge_second, w_long_second,
):
    atoms, hid = features.shape
    chan = w_charge_first.shape[1]
    waves = wave_vectors.shape[1]
    slots = nbr_index.shape[1]
    kv = lax.axis_size(KV)
    doms = lax.axis_size(DOM)
    total_atoms = atoms * doms * kv
    scale = LONG_SCALE / math.sqrt(waves) / math.sqrt(total_atoms)
    part_rows = 2 * chan * waves // 128
    halo = halo_lists.shape[2]
    smem = pl.BlockSpec(memory_space=pltpu.SMEM)
    w_charge_first = w_charge_first.T
    w_charge_second = w_charge_second.T
    lists = halo_lists[0]
    index_t = nbr_index.T
    dist_t = nbr_dist.T

    kept = (
        features, w_charge_first, wave_vectors, w_long_first, w_value, w_charge_second, w_long_second,
        dist_t, nbr_count.reshape(1, atoms), w_filter,
    )
    cos_table, sin_table, part, *kept = pl.pallas_call(
        lambda *refs: table_kernel(*refs, scale=scale),
        out_shape=(
            shape((atoms, waves), BF16), shape((atoms, waves), BF16), shape((part_rows, 128), BF16),
            *(shape(a.shape, a.dtype) for a in kept),
        ),
        scratch_shapes=[pltpu.VMEM((3, atoms, 128), F32), pltpu.VMEM((8, atoms), F32)],
        compiler_params=vmem(6),
        name="tables",
    )(*in_hbm(positions, *kept))
    (
        features, w_charge_first, wave_vectors, w_long_first, w_value, w_charge_second, w_long_second,
        dist_t, count_row, w_filter,
    ) = kept
    sums = everything(part, "fold_first")
    hidden_first, values, force_first = pl.pallas_call(
        first_project_kernel,
        out_shape=(shape((atoms, hid), BF16), shape((kv * atoms, hid), BF16), shape((3, atoms), F32)),
        scratch_shapes=[pltpu.VMEM((4 * chan, waves), BF16)] * 2,
        compiler_params=vmem(6),
        name="project_first",
    )(sums, cos_table, sin_table, wave_vectors, features, w_charge_first, w_long_first, w_value)

    v_dom = lax.all_to_all(values, KV, 0, 0, tiled=True)
    to_next, to_previous = pl.pallas_call(
        halo_kernel,
        grid=(1,),
        in_specs=[
            pl.BlockSpec((2, 128), lambda i, b=b: (0, b), memory_space=pltpu.SMEM) for b in range(halo // 128)
        ] + [pl.BlockSpec((kv * atoms, hid), lambda i: (0, 0))],
        out_specs=(pl.BlockSpec((halo, hid), lambda i: (0, 0)), pl.BlockSpec((halo, hid), lambda i: (0, 0))),
        out_shape=(shape((halo, hid), BF16), shape((halo, hid), BF16)),
        scratch_shapes=[pltpu.VMEM((kv * atoms, hid), F32), pltpu.VMEM((2, halo, hid), F32)],
        compiler_params=vmem(6),
        name="halo_rows",
    )(*in_hbm(*[lists] * (halo // 128)), v_dom)
    from_below = lax.ppermute(to_next, DOM, [(i, (i + 1) % doms) for i in range(doms)])
    from_above = lax.ppermute(to_previous, DOM, [(i, (i - 1) % doms) for i in range(doms)])

    steps = 8
    halves = atoms // 128
    whole = lambda dims: pl.BlockSpec(dims, lambda i: (0, 0))
    weights = pl.pallas_call(
        weight_kernel,
        grid=(steps,),
        in_specs=[
            whole((1, atoms)),
            whole((slots, atoms)),
            whole(w_filter.shape),
        ],
        out_specs=pl.BlockSpec((atoms // steps, slots, hid), lambda i: (i, 0, 0)),
        out_shape=shape((atoms, slots, hid), F32),
        scratch_shapes=[
            pltpu.VMEM((atoms, slots), F32),
            pltpu.VMEM((atoms // 2, 2 * slots), F32),
            pltpu.VMEM((atoms // 2, 2 * slots), F32),
            pltpu.VMEM((2 * w_filter.shape[0], hid), BF16),
        ],
        cost_estimate=pl.CostEstimate(
            flops=2 * atoms * slots * hid * 32,
            bytes_accessed=atoms * slots * hid * 4,
            transcendentals=atoms * slots * 16,
        ),
        compiler_params=vmem(6),
        name="slot_weights",
    )(count_row, dist_t, w_filter)

    blocks = range(slots // 4)
    index_t, _ = lax.optimization_barrier((index_t, to_next))
    index_flat = index_t.reshape(slots * atoms)
    hidden_second, part = pl.pallas_call(
        lambda *refs: neighbour_kernel(*refs, scale=scale),
        grid=(steps,),
        in_specs=[smem] + [
            pl.BlockSpec((4 * atoms,), lambda i, at=at: (at,), memory_space=pltpu.SMEM) for at in blocks
        ] + [
            pl.BlockSpec((halves, 128 // steps, slots, hid), lambda i: (0, i, 0, 0)),
            whole((kv * atoms, hid)),
            whole((halo, hid)),
            whole((halo, hid)),
            whole((atoms, hid)),
            whole((chan, hid)),
            whole((atoms, waves)),
            whole((atoms, waves)),
            whole((3, waves)),
        ],
        out_specs=(whole((atoms, hid)), whole((part_rows, 128))),
        out_shape=(shape((atoms, hid), BF16), shape((part_rows, 128), BF16)),
        scratch_shapes=[pltpu.VMEM((kv * atoms + 2 * halo, hid), F32), pltpu.VMEM((8 * atoms, hid), F32)],
        compiler_params=vmem(14),
        name="neighbours",
    )(
        *in_hbm(nbr_count), *[index_flat] * len(blocks), weights.reshape(halves, 128, slots, hid), v_dom, from_below, from_above,
        hidden_first, w_charge_second, cos_table, sin_table, wave_vectors,
    )
    sums = everything(part, "fold_second")
    return pl.pallas_call(
        last_project_kernel,
        out_shape=(shape((atoms, hid), BF16), shape((3, atoms), F32)),
        scratch_shapes=[pltpu.VMEM((4 * chan, waves), BF16)] * 2,
        compiler_params=vmem(6),
        name="project_second",
    )(
        sums, cos_table, sin_table, wave_vectors, hidden_second, w_charge_second, w_long_second, force_first,
    )


def solution(mesh):
    sizes = tuple(size for _, size in PARTS)
    return jax.shard_map(
        local,
        mesh=jax.sharding.Mesh(mesh.devices.reshape(sizes), EVERY),
        in_specs=(
            P(None, EVERY), P(EVERY, None), P(EVERY, None), P(EVERY), P(EVERY, None), P(DOM, None, None),
            P(), P(), P(), P(), P(), P(), P(),
        ),
        out_specs=(P(EVERY, None), P(None, EVERY)),
        check_vma=False,
    )
```

```python
import math

import jax
import jax.numpy as jnp
from jax import lax
from jax.experimental import pallas as pl
from jax.experimental.pallas import tpu as pltpu
from jax.sharding import PartitionSpec as P

F32 = jnp.float32
BF16 = jnp.bfloat16
HIGHEST = lax.Precision.HIGHEST
LONG_SCALE = 2.0
CELL = 60.0
PARTS = (("xlo", 2), ("z", 8), ("core", 2), ("y", 4), ("xhi", 2))
EVERY = tuple(name for name, _ in PARTS)
DOM = ("xlo", "z", "core")
KV = ("y", "xhi")
LINE = ("z",)
PLANE = ("xlo", "core", "y", "xhi")

COS_COEF = (
    0.9999992251396179,
    -19.738981246948242,
    64.92865753173828,
    -85.27162170410156,
    58.79049301147461,
    -21.07110595703125,
)
SIN_COEF = (
    6.283185005187988,
    -41.341590881347656,
    81.59994506835938,
    -76.61447143554688,
    41.3428840637207,
    -12.471243858337402,
)

NN = (((1,), (0,)), ((), ()))
NT = (((1,), (1,)), ((), ()))
TN = (((0,), (0,)), ((), ()))


def horner(coefs, v):
    total = v * coefs[-1] + coefs[-2]
    for coef in coefs[-3::-1]:
        total = total * v + coef
    return total


def dot(a, b, dims=NN, precision=None):
    return lax.dot_general(a, b, dims, precision=precision, preferred_element_type=F32)


def silu(x):
    return x / (1.0 + jnp.exp(-x))


def wave_weight(wave):
    sq_norm = wave[0:1] * wave[0:1] + wave[1:2] * wave[1:2] + wave[2:3] * wave[2:3]
    return jnp.exp(-0.5 * sq_norm) / (sq_norm + 1.0)


def split_rows(x):
    high = x.astype(BF16)
    return jnp.concatenate([high, (x - high.astype(F32)).astype(BF16)], axis=0)


def structure_part(charge_t, cos_ref, sin_ref, wave_ref, part_ref, scale):
    chan = charge_t.shape[0]
    waves = cos_ref.shape[1]
    rows = split_rows(charge_t)
    cos_sum = dot(rows, cos_ref[...])
    sin_sum = dot(rows, sin_ref[...])
    weight = wave_weight(wave_ref[...]) * scale
    cos_sum = (cos_sum[:chan] + cos_sum[chan:]) * weight
    sin_sum = (sin_sum[:chan] + sin_sum[chan:]) * weight
    for t in range(waves // 128):
        lanes = slice(t * 128, (t + 1) * 128)
        part_ref[t * 2 * chan : t * 2 * chan + chan, :] = cos_sum[:, lanes].astype(BF16)
        part_ref[t * 2 * chan + chan : (t + 1) * 2 * chan, :] = sin_sum[:, lanes].astype(BF16)


def table_kernel(*refs, scale):
    later = (len(refs) - 6) // 2
    pos_ref, kept_in, cos_ref, sin_ref, part_ref = refs[0], refs[1 : 1 + later], *refs[1 + later : 4 + later]
    kept_out, turns, pad = refs[4 + later : -2], *refs[-2:]
    feat_ref, wc_ref, wave_ref = kept_in[:3]
    atoms, waves = cos_ref.shape
    for in_ref, out_ref in zip(kept_in, kept_out):
        out_ref[...] = in_ref[...]
    pad[...] = jnp.zeros_like(pad)
    pad[0:3, :] = pos_ref[...] * (1.0 / CELL)
    columns = jnp.transpose(pad[...])
    for c in range(3):
        turns[c] = jnp.broadcast_to(columns[:, c : c + 1], (atoms, 128))
    rows = 64

    def one_tile(t, carry):
        lanes = pl.ds(pl.multiple_of(t * 128, 128), 128)
        whole = jnp.round(wave_ref[:, lanes] * (CELL / (2.0 * math.pi)))
        for b in range(atoms // rows):
            at = slice(b * rows, (b + 1) * rows)
            u = (
                turns[0, at, :] * whole[0:1]
                + turns[1, at, :] * whole[1:2]
                + turns[2, at, :] * whole[2:3]
            )
            u = u - jnp.round(u)
            v = u * u
            cos_ref[at, lanes] = horner(COS_COEF, v).astype(BF16)
            sin_ref[at, lanes] = (u * horner(SIN_COEF, v)).astype(BF16)
        return carry

    lax.fori_loop(0, waves // 128, one_tile, 0)
    charge_t = dot(wc_ref[...], feat_ref[...], NT)
    structure_part(charge_t, cos_ref, sin_ref, wave_ref, part_ref, scale)


def fold_kernel(in_ref, out_ref, *, members, copies):
    rows = in_ref.shape[0] // members
    total = in_ref[0:rows, :].astype(F32)
    for m in range(1, members):
        total = total + in_ref[m * rows : (m + 1) * rows, :].astype(F32)
    total = total.astype(out_ref.dtype)
    for m in range(copies):
        out_ref[m * rows : (m + 1) * rows, :] = total


def project(sums_ref, cos_ref, sin_ref, wave_ref, charge_t, with_cos, with_sin):
    chan = charge_t.shape[0]
    waves = cos_ref.shape[1]
    for t in range(waves // 128):
        lanes = slice(t * 128, (t + 1) * 128)
        wave = wave_ref[:, lanes]
        cos_w = sums_ref[t * 2 * chan : t * 2 * chan + chan, :].astype(F32)
        sin_w = sums_ref[t * 2 * chan + chan : (t + 1) * 2 * chan, :].astype(F32)
        with_cos[0:chan, lanes] = cos_w.astype(BF16)
        with_sin[0:chan, lanes] = sin_w.astype(BF16)
        for c in range(3):
            at = slice((c + 1) * chan, (c + 2) * chan)
            with_cos[at, lanes] = (-wave[c : c + 1] * sin_w).astype(BF16)
            with_sin[at, lanes] = (wave[c : c + 1] * cos_w).astype(BF16)
    both = dot(with_cos[...], cos_ref[...], NT) + dot(with_sin[...], sin_ref[...], NT)
    potential_t = both[:chan]
    force = [
        jnp.sum(charge_t * both[(c + 1) * chan : (c + 2) * chan], axis=0, keepdims=True)
        for c in range(3)
    ]
    return potential_t, force


def first_project_kernel(
    sums_ref, cos_ref, sin_ref, wave_ref, feat_ref, wc_ref, wl_ref, wv_ref,
    hidden_ref, values_ref, force_ref, with_cos, with_sin,
):
    charge_t = dot(wc_ref[...], feat_ref[...], NT)
    potential_t, force = project(sums_ref, cos_ref, sin_ref, wave_ref, charge_t, with_cos, with_sin)
    for c in range(3):
        force_ref[c : c + 1, :] = force[c]
    lifted = dot(potential_t, wl_ref[...], TN, HIGHEST)
    hidden = (feat_ref[...].astype(F32) + silu(lifted)).astype(BF16)
    hidden_ref[...] = hidden
    values = dot(hidden, wv_ref[...]).astype(BF16)
    atoms = values.shape[0]
    for j in range(values_ref.shape[0] // atoms):
        values_ref[j * atoms : (j + 1) * atoms, :] = values


def last_project_kernel(
    sums_ref, cos_ref, sin_ref, wave_ref, hidden_ref, wc_ref, wl_ref, force_in,
    feat_out, force_out, with_cos, with_sin,
):
    charge_t = dot(wc_ref[...], hidden_ref[...], NT)
    potential_t, force = project(sums_ref, cos_ref, sin_ref, wave_ref, charge_t, with_cos, with_sin)
    for c in range(3):
        force_out[c : c + 1, :] = force_in[c : c + 1, :] + force[c]
    lifted = dot(potential_t, wl_ref[...], TN, HIGHEST)
    feat_out[...] = (hidden_ref[...].astype(F32) + silu(lifted)).astype(BF16)


def row_tile(table, rows, bits):
    tiles = [table[pl.ds(row, 8, stride=0), :] for row in rows]
    for bit in bits:
        tiles = [jnp.where(bit, odd, even) for even, odd in zip(tiles[::2], tiles[1::2])]
    return tiles[0]


def sublane_bits():
    sub = lax.broadcasted_iota(jnp.int32, (8, 128), 0)
    return [(sub & bit) != 0 for bit in (1, 2, 4)]


def halo_kernel(*refs, far):
    lists, (values_ref, out_ref, table, picked) = refs[:-4], refs[-4:]
    core = lax.axis_index("core")
    side = 1 - core if far else core
    table[0 : values_ref.shape[0], :] = values_ref[...].astype(F32)
    bits = sublane_bits()

    def some_rows(g, carry):
        first = g * 8
        for b, list_ref in enumerate(lists):
            rows = [list_ref[side, first + j] for j in range(8)]
            picked[pl.ds(pl.multiple_of(b * 128 + first, 8), 8), :] = row_tile(table, rows, bits)
        return carry

    lax.fori_loop(0, 16, some_rows, 0)
    out_ref[...] = picked[...].astype(BF16)


def weight_kernel(count_ref, dist_ref, wf_ref, out_ref, turned, near, taper, wide):
    step = pl.program_id(0)
    slots, atoms = dist_ref.shape
    basis = wf_ref.shape[0]
    pairs = out_ref.shape[0] // 2
    sharpness = ((basis - 1) / 4.5) ** 2

    def paired(block):
        turned[...] = jnp.transpose(block)
        return jnp.concatenate(
            [turned[pl.ds(0, atoms // 2, stride=2), :], turned[pl.ds(1, atoms // 2, stride=2), :]], axis=1
        )

    @pl.when(step == 0)
    def _():
        dist = dist_ref[...]
        scaled = dist * 0.1
        height = 0.5 * (horner(COS_COEF, scaled * scaled) + 1.0)
        slot = lax.broadcasted_iota(jnp.int32, (slots, atoms), 0)
        near[...] = paired(dist)
        taper[...] = paired(jnp.where(slot < count_ref[...], height, 0.0))
        wf_high = wf_ref[...].astype(BF16)
        wide[0:basis, :] = wf_high
        wide[basis : 2 * basis, :] = (wf_ref[...] - wf_high.astype(F32)).astype(BF16)

    centers = 0.5 + 4.5 / (basis - 1) * lax.broadcasted_iota(jnp.int32, (basis, 2 * slots), 0).astype(F32)
    for p in range(pairs):
        row = pl.ds(step * pairs + p, 1)
        away = near[row, :] - centers
        radial = (jnp.exp(-sharpness * (away * away)) * taper[row, :]).astype(BF16)
        both = dot(jnp.concatenate([radial, radial], axis=0), wide[...], TN)
        out_ref[2 * p] = both[:slots]
        out_ref[2 * p + 1] = both[slots:]


def neighbour_kernel(*refs, scale):
    count_ref, index_refs = refs[0], refs[1:-13]
    (
        weight_ref, values_ref, far_ref, near_ref, hidden_ref, wc_ref, cos_ref, sin_ref, wave_ref,
        hidden_out, part_ref, table, sums,
    ) = refs[-13:]
    own = values_ref.shape[0]
    halo = far_ref.shape[0]
    atoms, slots, _ = weight_ref.shape
    core = lax.axis_index("core")
    table[0:own, :] = values_ref[...].astype(F32)
    table[pl.ds(pl.multiple_of(own + (1 - core) * halo, 8), halo), :] = near_ref[...].astype(F32)
    table[pl.ds(pl.multiple_of(own + core * halo, 8), halo), :] = far_ref[...].astype(F32)
    bits = sublane_bits()

    def one_atom(atom, carry):
        at = pl.ds(pl.multiple_of(atom * 8, 8), 8)
        spots = [atom + q * atoms for q in range(4)]

        def some_slots(blocks):
            total = jnp.zeros((8, 128), F32)
            for b in blocks:
                rows = [index_refs[2 * b + s // 4][spots[s % 4]] for s in range(8)]
                total = total + row_tile(table, rows, bits) * weight_ref[atom, 8 * b : 8 * b + 8, :]
            return total

        middle = slots // 16
        sums[at, :] = some_slots(range(middle))

        @pl.when(count_ref[atom] > middle * 8)
        def _():
            sums[at, :] = sums[at, :] + some_slots(range(middle, slots // 8))

        return carry

    lax.fori_loop(0, atoms, one_atom, 0)
    message = sums[pl.ds(0, atoms, stride=8), :]
    for k in range(1, 8):
        message = message + sums[pl.ds(k, atoms, stride=8), :]
    hidden = (hidden_ref[...].astype(F32) + silu(message)).astype(BF16)
    hidden_out[...] = hidden
    charge_t = dot(wc_ref[...], hidden, NT)
    structure_part(charge_t, cos_ref, sin_ref, wave_ref, part_ref, scale)


def shape(dims, kind):
    return jax.ShapeDtypeStruct(dims, kind)


def in_hbm(*arrays):
    return tuple(pltpu.with_memory_space_constraint(array, pltpu.HBM) for array in arrays)


def vmem(mib):
    return pltpu.CompilerParams(vmem_limit_bytes=mib * 1024 * 1024)


def fold(sums, members, copies, kind):
    rows = sums.shape[0] // members
    return pl.pallas_call(
        lambda *refs: fold_kernel(*refs, members=members, copies=copies),
        out_shape=shape((copies * rows, sums.shape[1]), kind),
        compiler_params=vmem(2),
    )(sums)


def everything(part):
    line = lax.axis_size(LINE)
    plane = lax.axis_size(PLANE)
    share = lax.all_to_all(part, PLANE, 0, 0, tiled=True)
    share = fold(share, plane, line, F32)
    share = lax.all_to_all(share, LINE, 0, 0, tiled=True)
    share = fold(share, line, plane, BF16)
    return lax.all_to_all(share, PLANE, 0, 0, tiled=True)


def local(
    positions, features, nbr_index, nbr_count, nbr_dist, halo_lists, wave_vectors,
    w_charge_first, w_long_first, w_value, w_filter, w_charge_second, w_long_second,
):
    atoms, hid = features.shape
    chan = w_charge_first.shape[1]
    waves = wave_vectors.shape[1]
    slots = nbr_index.shape[1]
    kv = lax.axis_size(KV)
    doms = lax.axis_size(DOM)
    total_atoms = atoms * doms * kv
    scale = LONG_SCALE / math.sqrt(waves) / math.sqrt(total_atoms)
    part_rows = 2 * chan * waves // 128
    halo = halo_lists.shape[2]
    smem = pl.BlockSpec(memory_space=pltpu.SMEM)
    w_charge_first = w_charge_first.T
    w_charge_second = w_charge_second.T
    lists = halo_lists[0]
    index_t = nbr_index.T
    dist_t = nbr_dist.T

    kept = (
        features, w_charge_first, wave_vectors, w_long_first, w_value, w_charge_second, w_long_second,
        dist_t, nbr_count.reshape(1, atoms), w_filter,
    )
    cos_table, sin_table, part, *kept = pl.pallas_call(
        lambda *refs: table_kernel(*refs, scale=scale),
        out_shape=(
            shape((atoms, waves), BF16), shape((atoms, waves), BF16), shape((part_rows, 128), BF16),
            *(shape(a.shape, a.dtype) for a in kept),
        ),
        scratch_shapes=[pltpu.VMEM((3, atoms, 128), F32), pltpu.VMEM((8, atoms), F32)],
        compiler_params=vmem(6),
        name="tables",
    )(*in_hbm(positions, *kept))
    (
        features, w_charge_first, wave_vectors, w_long_first, w_value, w_charge_second, w_long_second,
        dist_t, count_row, w_filter,
    ) = kept
    sums = everything(part)
    hidden_first, values, force_first = pl.pallas_call(
        first_project_kernel,
        out_shape=(shape((atoms, hid), BF16), shape((kv * atoms, hid), BF16), shape((3, atoms), F32)),
        scratch_shapes=[pltpu.VMEM((4 * chan, waves), BF16)] * 2,
        compiler_params=vmem(6),
        name="project_first",
    )(sums, cos_table, sin_table, wave_vectors, features, w_charge_first, w_long_first, w_value)

    v_dom = lax.all_to_all(values, KV, 0, 0, tiled=True)

    def halo_rows(far, source):
        return pl.pallas_call(
            lambda *refs: halo_kernel(*refs, far=far),
            grid=(1,),
            in_specs=[
                pl.BlockSpec((2, 128), lambda i, b=b: (0, b), memory_space=pltpu.SMEM) for b in range(halo // 128)
            ] + [pl.BlockSpec((kv * atoms, hid), lambda i: (0, 0))],
            out_specs=pl.BlockSpec((halo, hid), lambda i: (0, 0)),
            out_shape=shape((halo, hid), BF16),
            scratch_shapes=[pltpu.VMEM((kv * atoms + 8, hid), F32), pltpu.VMEM((halo, hid), F32)],
            compiler_params=vmem(6),
            cost_estimate=pl.CostEstimate(flops=halo * hid, bytes_accessed=4 * kv * atoms * hid, transcendentals=0),
            name="halo_far" if far else "halo_near",
        )(*in_hbm(*[lists] * (halo // 128)), source)

    to_far = halo_rows(True, v_dom)
    to_far, source, index_t = lax.optimization_barrier((to_far, v_dom, index_t))
    from_far = lax.ppermute(to_far, DOM, [(i, (i - 1 + 2 * (i % 2)) % doms) for i in range(doms)])
    to_near = halo_rows(False, source)
    from_near = lax.ppermute(to_near, DOM, [(i, i + 1 - 2 * (i % 2)) for i in range(doms)])

    steps = 8
    whole = lambda dims: pl.BlockSpec(dims, lambda i: (0, 0))
    weights = pl.pallas_call(
        weight_kernel,
        grid=(steps,),
        in_specs=[
            whole((1, atoms)),
            whole((slots, atoms)),
            whole(w_filter.shape),
        ],
        out_specs=pl.BlockSpec((atoms // steps, slots, hid), lambda i: (i, 0, 0)),
        out_shape=shape((atoms, slots, hid), F32),
        scratch_shapes=[
            pltpu.VMEM((atoms, slots), F32),
            pltpu.VMEM((atoms // 2, 2 * slots), F32),
            pltpu.VMEM((atoms // 2, 2 * slots), F32),
            pltpu.VMEM((2 * w_filter.shape[0], hid), BF16),
        ],
        cost_estimate=pl.CostEstimate(
            flops=2 * atoms * slots * hid * 32,
            bytes_accessed=atoms * slots * hid * 4,
            transcendentals=atoms * slots * 16,
        ),
        compiler_params=vmem(6),
        name="slot_weights",
    )(count_row, dist_t, w_filter)

    blocks = range(slots // 4)
    index_flat = index_t.reshape(slots * atoms)
    hidden_second, part = pl.pallas_call(
        lambda *refs: neighbour_kernel(*refs, scale=scale),
        grid=(1,),
        in_specs=[smem] + [
            pl.BlockSpec((4 * atoms,), lambda i, at=at: (at,), memory_space=pltpu.SMEM) for at in blocks
        ] + [
            pl.BlockSpec((atoms, slots, hid), lambda i: (0, 0, 0)),
            whole((kv * atoms, hid)),
            whole((halo, hid)),
            whole((halo, hid)),
            whole((atoms, hid)),
            whole((chan, hid)),
            whole((atoms, waves)),
            whole((atoms, waves)),
            whole((3, waves)),
        ],
        out_specs=(whole((atoms, hid)), whole((part_rows, 128))),
        out_shape=(shape((atoms, hid), BF16), shape((part_rows, 128), BF16)),
        scratch_shapes=[pltpu.VMEM((kv * atoms + 2 * halo + 8, hid), F32), pltpu.VMEM((8 * atoms, hid), F32)],
        compiler_params=vmem(20),
        name="neighbours",
    )(
        *in_hbm(nbr_count), *[index_flat] * len(blocks), weights, v_dom, from_far, from_near,
        hidden_first, w_charge_second, cos_table, sin_table, wave_vectors,
    )
    sums = everything(part)
    return pl.pallas_call(
        last_project_kernel,
        out_shape=(shape((atoms, hid), BF16), shape((3, atoms), F32)),
        scratch_shapes=[pltpu.VMEM((4 * chan, waves), BF16)] * 2,
        compiler_params=vmem(6),
        name="project_second",
    )(
        sums, cos_table, sin_table, wave_vectors, hidden_second, w_charge_second, w_long_second, force_first,
    )


def solution(mesh):
    sizes = tuple(size for _, size in PARTS)
    return jax.shard_map(
        local,
        mesh=jax.sharding.Mesh(mesh.devices.reshape(sizes), EVERY),
        in_specs=(
            P(None, EVERY), P(EVERY, None), P(EVERY, None), P(EVERY), P(EVERY, None), P(DOM, None, None),
            P(), P(), P(), P(), P(), P(), P(),
        ),
        out_specs=(P(EVERY, None), P(None, EVERY)),
        check_vma=False,
    )
```

```python
import math

import jax
import jax.numpy as jnp
from jax import lax
from jax.experimental import pallas as pl
from jax.experimental.pallas import tpu as pltpu
from jax.sharding import PartitionSpec as P

F32 = jnp.float32
BF16 = jnp.bfloat16
HIGHEST = lax.Precision.HIGHEST
LONG_SCALE = 2.0
CELL = 60.0
PARTS = (("xlo", 2), ("z", 8), ("core", 2), ("y", 4), ("xhi", 2))
EVERY = tuple(name for name, _ in PARTS)
DOM = ("xlo", "z", "core")
KV = ("y", "xhi")
UNROLL = 2
LINE = ("z",)
PLANE = ("xlo", "core", "y", "xhi")

COS_COEF = (
    0.9999992251396179,
    -19.738981246948242,
    64.92865753173828,
    -85.27162170410156,
    58.79049301147461,
    -21.07110595703125,
)
SIN_COEF = (
    6.283185005187988,
    -41.341590881347656,
    81.59994506835938,
    -76.61447143554688,
    41.3428840637207,
    -12.471243858337402,
)

NN = (((1,), (0,)), ((), ()))
NT = (((1,), (1,)), ((), ()))
TN = (((0,), (0,)), ((), ()))


def horner(coefs, v):
    total = v * coefs[-1] + coefs[-2]
    for coef in coefs[-3::-1]:
        total = total * v + coef
    return total


def dot(a, b, dims=NN, precision=None):
    return lax.dot_general(a, b, dims, precision=precision, preferred_element_type=F32)


def silu(x):
    return x / (1.0 + jnp.exp(-x))


def wave_weight(wave):
    sq_norm = wave[0:1] * wave[0:1] + wave[1:2] * wave[1:2] + wave[2:3] * wave[2:3]
    return jnp.exp(-0.5 * sq_norm) / (sq_norm + 1.0)


def split_rows(x):
    high = x.astype(BF16)
    return jnp.concatenate([high, (x - high.astype(F32)).astype(BF16)], axis=0)


def structure_part(charge_t, cos_ref, sin_ref, wave_ref, part_ref, scale):
    chan = charge_t.shape[0]
    waves = cos_ref.shape[1]
    rows = split_rows(charge_t)
    cos_sum = dot(rows, cos_ref[...])
    sin_sum = dot(rows, sin_ref[...])
    weight = wave_weight(wave_ref[...]) * scale
    cos_sum = (cos_sum[:chan] + cos_sum[chan:]) * weight
    sin_sum = (sin_sum[:chan] + sin_sum[chan:]) * weight
    for t in range(waves // 128):
        lanes = slice(t * 128, (t + 1) * 128)
        part_ref[t * 2 * chan : t * 2 * chan + chan, :] = cos_sum[:, lanes].astype(BF16)
        part_ref[t * 2 * chan + chan : (t + 1) * 2 * chan, :] = sin_sum[:, lanes].astype(BF16)


def table_kernel(*refs, scale):
    later = (len(refs) - 6) // 2
    pos_ref, kept_in, cos_ref, sin_ref, part_ref = refs[0], refs[1 : 1 + later], *refs[1 + later : 4 + later]
    kept_out, turns, pad = refs[4 + later : -2], *refs[-2:]
    feat_ref, wc_ref, wave_ref = kept_in[:3]
    atoms, waves = cos_ref.shape
    for in_ref, out_ref in zip(kept_in, kept_out):
        out_ref[...] = in_ref[...]
    pad[...] = jnp.zeros_like(pad)
    pad[0:3, :] = pos_ref[...] * (1.0 / CELL)
    columns = jnp.transpose(pad[...])
    for c in range(3):
        turns[c] = jnp.broadcast_to(columns[:, c : c + 1], (atoms, 128))
    rows = 64

    def one_tile(t, carry):
        lanes = pl.ds(pl.multiple_of(t * 128, 128), 128)
        whole = jnp.round(wave_ref[:, lanes] * (CELL / (2.0 * math.pi)))
        for b in range(atoms // rows):
            at = slice(b * rows, (b + 1) * rows)
            u = (
                turns[0, at, :] * whole[0:1]
                + turns[1, at, :] * whole[1:2]
                + turns[2, at, :] * whole[2:3]
            )
            u = u - jnp.round(u)
            v = u * u
            cos_ref[at, lanes] = horner(COS_COEF, v).astype(BF16)
            sin_ref[at, lanes] = (u * horner(SIN_COEF, v)).astype(BF16)
        return carry

    lax.fori_loop(0, waves // 128, one_tile, 0)
    charge_t = dot(wc_ref[...], feat_ref[...], NT)
    structure_part(charge_t, cos_ref, sin_ref, wave_ref, part_ref, scale)


def fold_kernel(in_ref, out_ref, *, members, copies):
    rows = in_ref.shape[0] // members
    total = in_ref[0:rows, :].astype(F32)
    for m in range(1, members):
        total = total + in_ref[m * rows : (m + 1) * rows, :].astype(F32)
    total = total.astype(out_ref.dtype)
    for m in range(copies):
        out_ref[m * rows : (m + 1) * rows, :] = total


def project(sums_ref, cos_ref, sin_ref, wave_ref, charge_t, with_cos, with_sin):
    chan = charge_t.shape[0]
    waves = cos_ref.shape[1]
    for t in range(waves // 128):
        lanes = slice(t * 128, (t + 1) * 128)
        wave = wave_ref[:, lanes]
        cos_w = sums_ref[t * 2 * chan : t * 2 * chan + chan, :].astype(F32)
        sin_w = sums_ref[t * 2 * chan + chan : (t + 1) * 2 * chan, :].astype(F32)
        with_cos[0:chan, lanes] = cos_w.astype(BF16)
        with_sin[0:chan, lanes] = sin_w.astype(BF16)
        for c in range(3):
            at = slice((c + 1) * chan, (c + 2) * chan)
            with_cos[at, lanes] = (-wave[c : c + 1] * sin_w).astype(BF16)
            with_sin[at, lanes] = (wave[c : c + 1] * cos_w).astype(BF16)
    both = dot(with_cos[...], cos_ref[...], NT) + dot(with_sin[...], sin_ref[...], NT)
    potential_t = both[:chan]
    force = [
        jnp.sum(charge_t * both[(c + 1) * chan : (c + 2) * chan], axis=0, keepdims=True)
        for c in range(3)
    ]
    return potential_t, force


def first_project_kernel(
    sums_ref, cos_ref, sin_ref, feat_ref, wl_ref, wv_ref, hidden_ref, values_ref, with_cos, with_sin,
):
    chan, waves = with_cos.shape
    for t in range(waves // 128):
        lanes = slice(t * 128, (t + 1) * 128)
        with_cos[:, lanes] = sums_ref[t * 2 * chan : t * 2 * chan + chan, :]
        with_sin[:, lanes] = sums_ref[t * 2 * chan + chan : (t + 1) * 2 * chan, :]
    potential_t = dot(with_cos[...], cos_ref[...], NT) + dot(with_sin[...], sin_ref[...], NT)
    lifted = dot(potential_t, wl_ref[...], TN, HIGHEST)
    hidden = (feat_ref[...].astype(F32) + silu(lifted)).astype(BF16)
    hidden_ref[...] = hidden
    values = dot(hidden, wv_ref[...]).astype(BF16)
    atoms = values.shape[0]
    for j in range(values_ref.shape[0] // atoms):
        values_ref[j * atoms : (j + 1) * atoms, :] = values


def first_force_kernel(sums_ref, cos_ref, sin_ref, wave_ref, feat_ref, wc_ref, force_ref, with_cos, with_sin):
    charge_t = dot(wc_ref[...], feat_ref[...], NT)
    _, force = project(sums_ref, cos_ref, sin_ref, wave_ref, charge_t, with_cos, with_sin)
    for c in range(3):
        force_ref[c : c + 1, :] = force[c]


def last_project_kernel(
    sums_ref, cos_ref, sin_ref, wave_ref, hidden_ref, wc_ref, wl_ref, force_in,
    feat_out, force_out, with_cos, with_sin,
):
    charge_t = dot(wc_ref[...], hidden_ref[...], NT)
    potential_t, force = project(sums_ref, cos_ref, sin_ref, wave_ref, charge_t, with_cos, with_sin)
    for c in range(3):
        force_out[c : c + 1, :] = force_in[c : c + 1, :] + force[c]
    lifted = dot(potential_t, wl_ref[...], TN, HIGHEST)
    feat_out[...] = (hidden_ref[...].astype(F32) + silu(lifted)).astype(BF16)


def row_tile(table, rows, bits):
    tiles = [table[pl.ds(row, 8, stride=0), :] for row in rows]
    for bit in bits:
        tiles = [jnp.where(bit, odd, even) for even, odd in zip(tiles[::2], tiles[1::2])]
    return tiles[0]


def sublane_bits():
    sub = lax.broadcasted_iota(jnp.int32, (8, 128), 0)
    return [(sub & bit) != 0 for bit in (1, 2, 4)]


def halo_kernel(*refs, far):
    lists, (values_ref, out_ref, table, picked) = refs[:-4], refs[-4:]
    core = lax.axis_index("core")
    side = 1 - core if far else core
    table[0 : values_ref.shape[0], :] = values_ref[...].astype(F32)
    bits = sublane_bits()

    def some_rows(g, carry):
        first = g * 8
        for b, list_ref in enumerate(lists):
            rows = [list_ref[side, first + j] for j in range(8)]
            picked[pl.ds(pl.multiple_of(b * 128 + first, 8), 8), :] = row_tile(table, rows, bits)
        return carry

    lax.fori_loop(0, 16, some_rows, 0)
    out_ref[...] = picked[...].astype(BF16)


def weight_kernel(count_ref, dist_ref, wf_ref, out_ref, turned, near, taper, wide):
    step = pl.program_id(0)
    slots, atoms = dist_ref.shape
    basis = wf_ref.shape[0]
    pairs = out_ref.shape[0] // 2
    sharpness = ((basis - 1) / 4.5) ** 2

    def paired(block):
        turned[...] = jnp.transpose(block)
        return jnp.concatenate(
            [turned[pl.ds(0, atoms // 2, stride=2), :], turned[pl.ds(1, atoms // 2, stride=2), :]], axis=1
        )

    @pl.when(step == 0)
    def _():
        dist = dist_ref[...]
        scaled = dist * 0.1
        height = 0.5 * (horner(COS_COEF, scaled * scaled) + 1.0)
        slot = lax.broadcasted_iota(jnp.int32, (slots, atoms), 0)
        near[...] = paired(dist)
        taper[...] = paired(jnp.where(slot < count_ref[...], height, 0.0))
        wf_high = wf_ref[...].astype(BF16)
        wide[0:basis, :] = wf_high
        wide[basis : 2 * basis, :] = (wf_ref[...] - wf_high.astype(F32)).astype(BF16)

    centers = 0.5 + 4.5 / (basis - 1) * lax.broadcasted_iota(jnp.int32, (basis, 2 * slots), 0).astype(F32)
    for p in range(pairs):
        row = pl.ds(step * pairs + p, 1)
        away = near[row, :] - centers
        radial = (jnp.exp(-sharpness * (away * away)) * taper[row, :]).astype(BF16)
        both = dot(jnp.concatenate([radial, radial], axis=0), wide[...], TN)
        out_ref[2 * p] = both[:slots]
        out_ref[2 * p + 1] = both[slots:]


def neighbour_kernel(*refs, scale):
    count_ref, index_refs = refs[0], refs[1:-13]
    (
        weight_ref, values_ref, far_ref, near_ref, hidden_ref, wc_ref, cos_ref, sin_ref, wave_ref,
        hidden_out, part_ref, table, sums,
    ) = refs[-13:]
    own = values_ref.shape[0]
    halo = far_ref.shape[0]
    atoms, slots, _ = weight_ref.shape
    core = lax.axis_index("core")
    table[0:own, :] = values_ref[...].astype(F32)
    table[pl.ds(pl.multiple_of(own + (1 - core) * halo, 8), halo), :] = near_ref[...].astype(F32)
    table[pl.ds(pl.multiple_of(own + core * halo, 8), halo), :] = far_ref[...].astype(F32)
    bits = sublane_bits()

    def some_atoms(group, carry):
        for k in range(UNROLL):
            one_atom(group * UNROLL + k)
        return carry

    def one_atom(atom):
        at = pl.ds(pl.multiple_of(atom * 8, 8), 8)
        spots = [atom + q * atoms for q in range(4)]

        def some_slots(blocks):
            total = jnp.zeros((8, 128), F32)
            for b in blocks:
                rows = [index_refs[2 * b + s // 4][spots[s % 4]] for s in range(8)]
                total = total + row_tile(table, rows, bits) * weight_ref[atom, 8 * b : 8 * b + 8, :]
            return total

        middle = slots // 16
        sums[at, :] = some_slots(range(middle))

        @pl.when(count_ref[atom] > middle * 8)
        def _():
            sums[at, :] = sums[at, :] + some_slots(range(middle, slots // 8))

    lax.fori_loop(0, atoms // UNROLL, some_atoms, 0)
    message = sums[pl.ds(0, atoms, stride=8), :]
    for k in range(1, 8):
        message = message + sums[pl.ds(k, atoms, stride=8), :]
    hidden = (hidden_ref[...].astype(F32) + silu(message)).astype(BF16)
    hidden_out[...] = hidden
    charge_t = dot(wc_ref[...], hidden, NT)
    structure_part(charge_t, cos_ref, sin_ref, wave_ref, part_ref, scale)


def shape(dims, kind):
    return jax.ShapeDtypeStruct(dims, kind)


def in_hbm(*arrays):
    return tuple(pltpu.with_memory_space_constraint(array, pltpu.HBM) for array in arrays)


def vmem(mib):
    return pltpu.CompilerParams(vmem_limit_bytes=mib * 1024 * 1024)


def fold(sums, members, copies, kind):
    rows = sums.shape[0] // members
    return pl.pallas_call(
        lambda *refs: fold_kernel(*refs, members=members, copies=copies),
        out_shape=shape((copies * rows, sums.shape[1]), kind),
        compiler_params=vmem(2),
    )(sums)


def everything(part):
    line = lax.axis_size(LINE)
    plane = lax.axis_size(PLANE)
    share = lax.all_to_all(part, PLANE, 0, 0, tiled=True)
    share = fold(share, plane, line, F32)
    share = lax.all_to_all(share, LINE, 0, 0, tiled=True)
    share = fold(share, line, plane, BF16)
    return lax.all_to_all(share, PLANE, 0, 0, tiled=True)


def local(
    positions, features, nbr_index, nbr_count, nbr_dist, halo_lists, wave_vectors,
    w_charge_first, w_long_first, w_value, w_filter, w_charge_second, w_long_second,
):
    atoms, hid = features.shape
    chan = w_charge_first.shape[1]
    waves = wave_vectors.shape[1]
    slots = nbr_index.shape[1]
    kv = lax.axis_size(KV)
    doms = lax.axis_size(DOM)
    total_atoms = atoms * doms * kv
    scale = LONG_SCALE / math.sqrt(waves) / math.sqrt(total_atoms)
    part_rows = 2 * chan * waves // 128
    halo = halo_lists.shape[2]
    smem = pl.BlockSpec(memory_space=pltpu.SMEM)
    w_charge_first = w_charge_first.T
    w_charge_second = w_charge_second.T
    lists = halo_lists[0]
    index_t = nbr_index.T
    dist_t = nbr_dist.T

    kept = (
        features, w_charge_first, wave_vectors, w_long_first, w_value, w_charge_second, w_long_second,
        dist_t, nbr_count.reshape(1, atoms), w_filter, lists,
    )
    cos_table, sin_table, part, *kept = pl.pallas_call(
        lambda *refs: table_kernel(*refs, scale=scale),
        out_shape=(
            shape((atoms, waves), BF16), shape((atoms, waves), BF16), shape((part_rows, 128), BF16),
            *(shape(a.shape, a.dtype) for a in kept),
        ),
        scratch_shapes=[pltpu.VMEM((3, atoms, 128), F32), pltpu.VMEM((8, atoms), F32)],
        compiler_params=vmem(6),
        name="tables",
    )(*in_hbm(positions, *kept))
    (
        features, w_charge_first, wave_vectors, w_long_first, w_value, w_charge_second, w_long_second,
        dist_t, count_row, w_filter, lists,
    ) = kept
    sums = everything(part)
    hidden_first, values = pl.pallas_call(
        first_project_kernel,
        out_shape=(shape((atoms, hid), BF16), shape((kv * atoms, hid), BF16)),
        scratch_shapes=[pltpu.VMEM((chan, waves), BF16)] * 2,
        compiler_params=vmem(6),
        name="project_first",
    )(sums, cos_table, sin_table, features, w_long_first, w_value)

    v_dom = lax.all_to_all(values, KV, 0, 0, tiled=True)

    def halo_rows(far, source):
        return pl.pallas_call(
            lambda *refs: halo_kernel(*refs, far=far),
            grid=(1,),
            in_specs=[
                pl.BlockSpec((2, 128), lambda i, b=b: (0, b), memory_space=pltpu.SMEM) for b in range(halo // 128)
            ] + [pl.BlockSpec((kv * atoms, hid), lambda i: (0, 0))],
            out_specs=pl.BlockSpec((halo, hid), lambda i: (0, 0)),
            out_shape=shape((halo, hid), BF16),
            scratch_shapes=[pltpu.VMEM((kv * atoms + 8, hid), F32), pltpu.VMEM((halo, hid), F32)],
            compiler_params=vmem(6),
            cost_estimate=pl.CostEstimate(flops=halo * hid, bytes_accessed=4 * kv * atoms * hid, transcendentals=0),
            name="halo_far" if far else "halo_near",
        )(*[lists] * (halo // 128), source)

    to_far = halo_rows(True, v_dom)
    to_far, source, index_t, sums = lax.optimization_barrier((to_far, v_dom, index_t, sums))
    from_far = lax.ppermute(to_far, DOM, [(i, (i - 1 + 2 * (i % 2)) % doms) for i in range(doms)])
    to_near = halo_rows(False, source)
    force_first = pl.pallas_call(
        first_force_kernel,
        out_shape=shape((3, atoms), F32),
        scratch_shapes=[pltpu.VMEM((4 * chan, waves), BF16)] * 2,
        compiler_params=vmem(6),
        name="force_first",
    )(sums, cos_table, sin_table, wave_vectors, features, w_charge_first)
    from_near = lax.ppermute(to_near, DOM, [(i, i + 1 - 2 * (i % 2)) for i in range(doms)])

    steps = 8
    whole = lambda dims: pl.BlockSpec(dims, lambda i: (0, 0))
    weights = pl.pallas_call(
        weight_kernel,
        grid=(steps,),
        in_specs=[
            whole((1, atoms)),
            whole((slots, atoms)),
            whole(w_filter.shape),
        ],
        out_specs=pl.BlockSpec((atoms // steps, slots, hid), lambda i: (i, 0, 0)),
        out_shape=shape((atoms, slots, hid), F32),
        scratch_shapes=[
            pltpu.VMEM((atoms, slots), F32),
            pltpu.VMEM((atoms // 2, 2 * slots), F32),
            pltpu.VMEM((atoms // 2, 2 * slots), F32),
            pltpu.VMEM((2 * w_filter.shape[0], hid), BF16),
        ],
        cost_estimate=pl.CostEstimate(
            flops=2 * atoms * slots * hid * 32,
            bytes_accessed=atoms * slots * hid * 4,
            transcendentals=atoms * slots * 16,
        ),
        compiler_params=vmem(6),
        name="slot_weights",
    )(count_row, dist_t, w_filter)

    blocks = range(slots // 4)
    index_flat = index_t.reshape(slots * atoms)
    hidden_second, part = pl.pallas_call(
        lambda *refs: neighbour_kernel(*refs, scale=scale),
        grid=(1,),
        in_specs=[smem] + [
            pl.BlockSpec((4 * atoms,), lambda i, at=at: (at,), memory_space=pltpu.SMEM) for at in blocks
        ] + [
            pl.BlockSpec((atoms, slots, hid), lambda i: (0, 0, 0)),
            whole((kv * atoms, hid)),
            whole((halo, hid)),
            whole((halo, hid)),
            whole((atoms, hid)),
            whole((chan, hid)),
            whole((atoms, waves)),
            whole((atoms, waves)),
            whole((3, waves)),
        ],
        out_specs=(whole((atoms, hid)), whole((part_rows, 128))),
        out_shape=(shape((atoms, hid), BF16), shape((part_rows, 128), BF16)),
        scratch_shapes=[pltpu.VMEM((kv * atoms + 2 * halo + 8, hid), F32), pltpu.VMEM((8 * atoms, hid), F32)],
        compiler_params=vmem(20),
        name="neighbours",
    )(
        *in_hbm(nbr_count), *[index_flat] * len(blocks), weights, v_dom, from_far, from_near,
        hidden_first, w_charge_second, cos_table, sin_table, wave_vectors,
    )
    sums = everything(part)
    return pl.pallas_call(
        last_project_kernel,
        out_shape=(shape((atoms, hid), BF16), shape((3, atoms), F32)),
        scratch_shapes=[pltpu.VMEM((4 * chan, waves), BF16)] * 2,
        compiler_params=vmem(6),
        name="project_second",
    )(
        sums, cos_table, sin_table, wave_vectors, hidden_second, w_charge_second, w_long_second, force_first,
    )


def solution(mesh):
    sizes = tuple(size for _, size in PARTS)
    return jax.shard_map(
        local,
        mesh=jax.sharding.Mesh(mesh.devices.reshape(sizes), EVERY),
        in_specs=(
            P(None, EVERY), P(EVERY, None), P(EVERY, None), P(EVERY), P(EVERY, None), P(DOM, None, None),
            P(), P(), P(), P(), P(), P(), P(),
        ),
        out_specs=(P(EVERY, None), P(None, EVERY)),
        check_vma=False,
    )
```

```python
import math

import jax
import jax.numpy as jnp
from jax import lax
from jax.experimental import pallas as pl
from jax.experimental.pallas import tpu as pltpu
from jax.sharding import PartitionSpec as P

F32 = jnp.float32
BF16 = jnp.bfloat16
HIGHEST = lax.Precision.HIGHEST
LONG_SCALE = 2.0
CELL = 60.0
PARTS = (("xlo", 2), ("z", 8), ("core", 2), ("y", 4), ("xhi", 2))
EVERY = tuple(name for name, _ in PARTS)
DOM = ("xlo", "z", "core")
KV = ("y", "xhi")
UNROLL = 2
LINE = ("z",)
PLANE = ("xlo", "core", "y", "xhi")

COS_COEF = (
    0.9999992251396179,
    -19.738981246948242,
    64.92865753173828,
    -85.27162170410156,
    58.79049301147461,
    -21.07110595703125,
)
SIN_COEF = (
    6.283185005187988,
    -41.341590881347656,
    81.59994506835938,
    -76.61447143554688,
    41.3428840637207,
    -12.471243858337402,
)

NN = (((1,), (0,)), ((), ()))
NT = (((1,), (1,)), ((), ()))
TN = (((0,), (0,)), ((), ()))


def horner(coefs, v):
    total = v * coefs[-1] + coefs[-2]
    for coef in coefs[-3::-1]:
        total = total * v + coef
    return total


def dot(a, b, dims=NN, precision=None):
    return lax.dot_general(a, b, dims, precision=precision, preferred_element_type=F32)


def silu(x):
    return x / (1.0 + jnp.exp(-x))


def wave_weight(wave):
    sq_norm = wave[0:1] * wave[0:1] + wave[1:2] * wave[1:2] + wave[2:3] * wave[2:3]
    return jnp.exp(-0.5 * sq_norm) / (sq_norm + 1.0)


def split_rows(x):
    high = x.astype(BF16)
    return jnp.concatenate([high, (x - high.astype(F32)).astype(BF16)], axis=0)


def structure_part(charge_t, cos_ref, sin_ref, wave_ref, part_ref, scale):
    chan = charge_t.shape[0]
    waves = cos_ref.shape[1]
    rows = split_rows(charge_t)
    cos_sum = dot(rows, cos_ref[...])
    sin_sum = dot(rows, sin_ref[...])
    weight = wave_weight(wave_ref[...]) * scale
    cos_sum = (cos_sum[:chan] + cos_sum[chan:]) * weight
    sin_sum = (sin_sum[:chan] + sin_sum[chan:]) * weight
    for t in range(waves // 128):
        lanes = slice(t * 128, (t + 1) * 128)
        part_ref[t * 2 * chan : t * 2 * chan + chan, :] = cos_sum[:, lanes].astype(BF16)
        part_ref[t * 2 * chan + chan : (t + 1) * 2 * chan, :] = sin_sum[:, lanes].astype(BF16)


def table_kernel(*refs, scale):
    later = (len(refs) - 8) // 2
    pos_ref, kept_in, cos_ref, sin_ref, part_ref = refs[0], refs[1 : 1 + later], *refs[1 + later : 4 + later]
    kept_out, pieces, whole, turns_even, turns_odd = refs[4 + later : -4], *refs[-4:]
    feat_ref, wc_ref, wave_ref = kept_in[:3]
    atoms, waves = cos_ref.shape
    for in_ref, out_ref in zip(kept_in, kept_out):
        out_ref[...] = in_ref[...]
    rest = pos_ref[...] * (1.0 / CELL)
    pieces[...] = jnp.zeros_like(pieces)
    whole[...] = jnp.zeros_like(whole)
    for p in range(3):
        piece = rest.astype(BF16).astype(F32)
        pieces[3 * p : 3 * p + 3, :] = piece
        whole[3 * p : 3 * p + 3, :] = jnp.round(wave_ref[...] * (CELL / (2.0 * math.pi)))
        rest = rest - piece
    columns = jnp.transpose(pieces[...]).astype(BF16)
    tiles = waves // 128
    rows = 64

    def fill(t, turns):
        lanes = pl.ds(pl.multiple_of(t * 128, 128), 128)
        turns[...] = dot(columns, whole[:, lanes].astype(BF16))

    def finish(t, turns):
        lanes = pl.ds(pl.multiple_of(t * 128, 128), 128)
        for b in range(atoms // rows):
            at = slice(b * rows, (b + 1) * rows)
            u = turns[at, :]
            u = u - jnp.round(u)
            v = u * u
            cos_ref[at, lanes] = horner(COS_COEF, v).astype(BF16)
            sin_ref[at, lanes] = (u * horner(SIN_COEF, v)).astype(BF16)

    def two_tiles(t, carry):
        fill(2 * t + 1, turns_odd)
        finish(2 * t, turns_even)
        fill(lax.rem(2 * t + 2, tiles), turns_even)
        finish(2 * t + 1, turns_odd)
        return carry

    fill(0, turns_even)
    lax.fori_loop(0, tiles // 2, two_tiles, 0)
    charge_t = dot(wc_ref[...], feat_ref[...], NT)
    structure_part(charge_t, cos_ref, sin_ref, wave_ref, part_ref, scale)


def fold_kernel(in_ref, out_ref, *, members, copies):
    rows = in_ref.shape[0] // members
    total = in_ref[0:rows, :].astype(F32)
    for m in range(1, members):
        total = total + in_ref[m * rows : (m + 1) * rows, :].astype(F32)
    total = total.astype(out_ref.dtype)
    for m in range(copies):
        out_ref[m * rows : (m + 1) * rows, :] = total


def project(sums_ref, cos_ref, sin_ref, wave_ref, charge_t, with_cos, with_sin):
    chan = charge_t.shape[0]
    waves = cos_ref.shape[1]
    for t in range(waves // 128):
        lanes = slice(t * 128, (t + 1) * 128)
        wave = wave_ref[:, lanes]
        cos_w = sums_ref[t * 2 * chan : t * 2 * chan + chan, :].astype(F32)
        sin_w = sums_ref[t * 2 * chan + chan : (t + 1) * 2 * chan, :].astype(F32)
        with_cos[0:chan, lanes] = cos_w.astype(BF16)
        with_sin[0:chan, lanes] = sin_w.astype(BF16)
        for c in range(3):
            at = slice((c + 1) * chan, (c + 2) * chan)
            with_cos[at, lanes] = (-wave[c : c + 1] * sin_w).astype(BF16)
            with_sin[at, lanes] = (wave[c : c + 1] * cos_w).astype(BF16)
    both = dot(with_cos[...], cos_ref[...], NT) + dot(with_sin[...], sin_ref[...], NT)
    potential_t = both[:chan]
    force = [
        jnp.sum(charge_t * both[(c + 1) * chan : (c + 2) * chan], axis=0, keepdims=True)
        for c in range(3)
    ]
    return potential_t, force


def first_project_kernel(
    sums_ref, cos_ref, sin_ref, feat_ref, wl_ref, wv_ref, hidden_ref, values_ref, with_cos, with_sin,
):
    chan, waves = with_cos.shape
    for t in range(waves // 128):
        lanes = slice(t * 128, (t + 1) * 128)
        with_cos[:, lanes] = sums_ref[t * 2 * chan : t * 2 * chan + chan, :]
        with_sin[:, lanes] = sums_ref[t * 2 * chan + chan : (t + 1) * 2 * chan, :]
    potential_t = dot(with_cos[...], cos_ref[...], NT) + dot(with_sin[...], sin_ref[...], NT)
    lifted = dot(potential_t, wl_ref[...], TN, HIGHEST)
    hidden = (feat_ref[...].astype(F32) + silu(lifted)).astype(BF16)
    hidden_ref[...] = hidden
    values = dot(hidden, wv_ref[...]).astype(BF16)
    atoms = values.shape[0]
    for j in range(values_ref.shape[0] // atoms):
        values_ref[j * atoms : (j + 1) * atoms, :] = values


def first_force_kernel(sums_ref, cos_ref, sin_ref, wave_ref, feat_ref, wc_ref, force_ref, with_cos, with_sin):
    charge_t = dot(wc_ref[...], feat_ref[...], NT)
    _, force = project(sums_ref, cos_ref, sin_ref, wave_ref, charge_t, with_cos, with_sin)
    for c in range(3):
        force_ref[c : c + 1, :] = force[c]


def last_project_kernel(
    sums_ref, cos_ref, sin_ref, wave_ref, hidden_ref, wc_ref, wl_ref, force_in,
    feat_out, force_out, with_cos, with_sin,
):
    charge_t = dot(wc_ref[...], hidden_ref[...], NT)
    potential_t, force = project(sums_ref, cos_ref, sin_ref, wave_ref, charge_t, with_cos, with_sin)
    for c in range(3):
        force_out[c : c + 1, :] = force_in[c : c + 1, :] + force[c]
    lifted = dot(potential_t, wl_ref[...], TN, HIGHEST)
    feat_out[...] = (hidden_ref[...].astype(F32) + silu(lifted)).astype(BF16)


def row_tile(table, rows, bits):
    tiles = [table[pl.ds(row, 8, stride=0), :] for row in rows]
    for bit in bits:
        tiles = [jnp.where(bit, odd, even) for even, odd in zip(tiles[::2], tiles[1::2])]
    return tiles[0]


def sublane_bits():
    sub = lax.broadcasted_iota(jnp.int32, (8, 128), 0)
    return [(sub & bit) != 0 for bit in (1, 2, 4)]


def halo_kernel(*refs, far):
    lists, (values_ref, out_ref, table, picked) = refs[:-4], refs[-4:]
    core = lax.axis_index("core")
    side = 1 - core if far else core
    table[0 : values_ref.shape[0], :] = values_ref[...].astype(F32)
    bits = sublane_bits()

    def some_rows(g, carry):
        first = g * 8
        for b, list_ref in enumerate(lists):
            rows = [list_ref[side, first + j] for j in range(8)]
            picked[pl.ds(pl.multiple_of(b * 128 + first, 8), 8), :] = row_tile(table, rows, bits)
        return carry

    lax.fori_loop(0, 16, some_rows, 0)
    out_ref[...] = picked[...].astype(BF16)


def weight_kernel(count_ref, dist_ref, wf_ref, out_ref, turned, near, taper, wide):
    step = pl.program_id(0)
    slots, atoms = dist_ref.shape
    basis = wf_ref.shape[0]
    pairs = out_ref.shape[0] // 2
    sharpness = ((basis - 1) / 4.5) ** 2

    def paired(block):
        turned[...] = jnp.transpose(block)
        return jnp.concatenate(
            [turned[pl.ds(0, atoms // 2, stride=2), :], turned[pl.ds(1, atoms // 2, stride=2), :]], axis=1
        )

    @pl.when(step == 0)
    def _():
        dist = dist_ref[...]
        scaled = dist * 0.1
        height = 0.5 * (horner(COS_COEF, scaled * scaled) + 1.0)
        slot = lax.broadcasted_iota(jnp.int32, (slots, atoms), 0)
        near[...] = paired(dist)
        taper[...] = paired(jnp.where(slot < count_ref[...], height, 0.0))
        wf_high = wf_ref[...].astype(BF16)
        wide[0:basis, :] = wf_high
        wide[basis : 2 * basis, :] = (wf_ref[...] - wf_high.astype(F32)).astype(BF16)

    centers = 0.5 + 4.5 / (basis - 1) * lax.broadcasted_iota(jnp.int32, (basis, 2 * slots), 0).astype(F32)
    for p in range(pairs):
        row = pl.ds(step * pairs + p, 1)
        away = near[row, :] - centers
        radial = (jnp.exp(-sharpness * (away * away)) * taper[row, :]).astype(BF16)
        both = dot(jnp.concatenate([radial, radial], axis=0), wide[...], TN)
        out_ref[2 * p] = both[:slots]
        out_ref[2 * p + 1] = both[slots:]


def neighbour_kernel(*refs, scale):
    count_ref, index_refs = refs[0], refs[1:-13]
    (
        weight_ref, values_ref, far_ref, near_ref, hidden_ref, wc_ref, cos_ref, sin_ref, wave_ref,
        hidden_out, part_ref, table, sums,
    ) = refs[-13:]
    own = values_ref.shape[0]
    halo = far_ref.shape[0]
    atoms, slots, _ = weight_ref.shape
    core = lax.axis_index("core")
    table[0:own, :] = values_ref[...].astype(F32)
    table[pl.ds(pl.multiple_of(own + (1 - core) * halo, 8), halo), :] = near_ref[...].astype(F32)
    table[pl.ds(pl.multiple_of(own + core * halo, 8), halo), :] = far_ref[...].astype(F32)
    bits = sublane_bits()

    def some_atoms(group, carry):
        for k in range(UNROLL):
            one_atom(group * UNROLL + k)
        return carry

    def one_atom(atom):
        at = pl.ds(pl.multiple_of(atom * 8, 8), 8)
        spots = [atom + q * atoms for q in range(4)]

        def some_slots(blocks):
            total = jnp.zeros((8, 128), F32)
            for b in blocks:
                rows = [index_refs[2 * b + s // 4][spots[s % 4]] for s in range(8)]
                total = total + row_tile(table, rows, bits) * weight_ref[atom, 8 * b : 8 * b + 8, :]
            return total

        middle = slots // 16
        sums[at, :] = some_slots(range(middle))

        @pl.when(count_ref[atom] > middle * 8)
        def _():
            sums[at, :] = sums[at, :] + some_slots(range(middle, slots // 8))

    lax.fori_loop(0, atoms // UNROLL, some_atoms, 0)
    message = sums[pl.ds(0, atoms, stride=8), :]
    for k in range(1, 8):
        message = message + sums[pl.ds(k, atoms, stride=8), :]
    hidden = (hidden_ref[...].astype(F32) + silu(message)).astype(BF16)
    hidden_out[...] = hidden
    charge_t = dot(wc_ref[...], hidden, NT)
    structure_part(charge_t, cos_ref, sin_ref, wave_ref, part_ref, scale)


def shape(dims, kind):
    return jax.ShapeDtypeStruct(dims, kind)


def in_hbm(*arrays):
    return tuple(pltpu.with_memory_space_constraint(array, pltpu.HBM) for array in arrays)


def vmem(mib):
    return pltpu.CompilerParams(vmem_limit_bytes=mib * 1024 * 1024)


def fold(sums, members, copies, kind):
    rows = sums.shape[0] // members
    return pl.pallas_call(
        lambda *refs: fold_kernel(*refs, members=members, copies=copies),
        out_shape=shape((copies * rows, sums.shape[1]), kind),
        compiler_params=vmem(2),
    )(sums)


def everything(part):
    line = lax.axis_size(LINE)
    plane = lax.axis_size(PLANE)
    share = lax.all_to_all(part, PLANE, 0, 0, tiled=True)
    share = fold(share, plane, line, F32)
    share = lax.all_to_all(share, LINE, 0, 0, tiled=True)
    share = fold(share, line, plane, BF16)
    return lax.all_to_all(share, PLANE, 0, 0, tiled=True)


def local(
    positions, features, nbr_index, nbr_count, nbr_dist, halo_lists, wave_vectors,
    w_charge_first, w_long_first, w_value, w_filter, w_charge_second, w_long_second,
):
    atoms, hid = features.shape
    chan = w_charge_first.shape[1]
    waves = wave_vectors.shape[1]
    slots = nbr_index.shape[1]
    kv = lax.axis_size(KV)
    doms = lax.axis_size(DOM)
    total_atoms = atoms * doms * kv
    scale = LONG_SCALE / math.sqrt(waves) / math.sqrt(total_atoms)
    part_rows = 2 * chan * waves // 128
    halo = halo_lists.shape[2]
    smem = pl.BlockSpec(memory_space=pltpu.SMEM)
    w_charge_first = w_charge_first.T
    w_charge_second = w_charge_second.T
    lists = halo_lists[0]
    index_t = nbr_index.T
    dist_t = nbr_dist.T

    kept = (
        features, w_charge_first, wave_vectors, w_long_first, w_value, w_charge_second, w_long_second,
        dist_t, nbr_count.reshape(1, atoms), w_filter, lists,
    )
    cos_table, sin_table, part, *kept = pl.pallas_call(
        lambda *refs: table_kernel(*refs, scale=scale),
        out_shape=(
            shape((atoms, waves), BF16), shape((atoms, waves), BF16), shape((part_rows, 128), BF16),
            *(shape(a.shape, a.dtype) for a in kept),
        ),
        scratch_shapes=[pltpu.VMEM((16, atoms), F32), pltpu.VMEM((16, waves), F32)] + [pltpu.VMEM((atoms, 128), F32)] * 2,
        compiler_params=vmem(6),
        name="tables",
    )(*in_hbm(positions, *kept))
    (
        features, w_charge_first, wave_vectors, w_long_first, w_value, w_charge_second, w_long_second,
        dist_t, count_row, w_filter, lists,
    ) = kept
    sums = everything(part)
    hidden_first, values = pl.pallas_call(
        first_project_kernel,
        out_shape=(shape((atoms, hid), BF16), shape((kv * atoms, hid), BF16)),
        scratch_shapes=[pltpu.VMEM((chan, waves), BF16)] * 2,
        compiler_params=vmem(6),
        name="project_first",
    )(sums, cos_table, sin_table, features, w_long_first, w_value)

    v_dom = lax.all_to_all(values, KV, 0, 0, tiled=True)

    def halo_rows(far, source):
        return pl.pallas_call(
            lambda *refs: halo_kernel(*refs, far=far),
            grid=(1,),
            in_specs=[
                pl.BlockSpec((2, 128), lambda i, b=b: (0, b), memory_space=pltpu.SMEM) for b in range(halo // 128)
            ] + [pl.BlockSpec((kv * atoms, hid), lambda i: (0, 0))],
            out_specs=pl.BlockSpec((halo, hid), lambda i: (0, 0)),
            out_shape=shape((halo, hid), BF16),
            scratch_shapes=[pltpu.VMEM((kv * atoms + 8, hid), F32), pltpu.VMEM((halo, hid), F32)],
            compiler_params=vmem(6),
            cost_estimate=pl.CostEstimate(flops=halo * hid, bytes_accessed=4 * kv * atoms * hid, transcendentals=0),
            name="halo_far" if far else "halo_near",
        )(*[lists] * (halo // 128), source)

    to_far = halo_rows(True, v_dom)
    to_far, source, index_t, sums = lax.optimization_barrier((to_far, v_dom, index_t, sums))
    from_far = lax.ppermute(to_far, DOM, [(i, (i - 1 + 2 * (i % 2)) % doms) for i in range(doms)])
    to_near = halo_rows(False, source)
    force_first = pl.pallas_call(
        first_force_kernel,
        out_shape=shape((3, atoms), F32),
        scratch_shapes=[pltpu.VMEM((4 * chan, waves), BF16)] * 2,
        compiler_params=vmem(6),
        name="force_first",
    )(sums, cos_table, sin_table, wave_vectors, features, w_charge_first)
    from_near = lax.ppermute(to_near, DOM, [(i, i + 1 - 2 * (i % 2)) for i in range(doms)])

    steps = 8
    whole = lambda dims: pl.BlockSpec(dims, lambda i: (0, 0))
    weights = pl.pallas_call(
        weight_kernel,
        grid=(steps,),
        in_specs=[
            whole((1, atoms)),
            whole((slots, atoms)),
            whole(w_filter.shape),
        ],
        out_specs=pl.BlockSpec((atoms // steps, slots, hid), lambda i: (i, 0, 0)),
        out_shape=shape((atoms, slots, hid), F32),
        scratch_shapes=[
            pltpu.VMEM((atoms, slots), F32),
            pltpu.VMEM((atoms // 2, 2 * slots), F32),
            pltpu.VMEM((atoms // 2, 2 * slots), F32),
            pltpu.VMEM((2 * w_filter.shape[0], hid), BF16),
        ],
        cost_estimate=pl.CostEstimate(
            flops=2 * atoms * slots * hid * 32,
            bytes_accessed=atoms * slots * hid * 4,
            transcendentals=atoms * slots * 16,
        ),
        compiler_params=vmem(6),
        name="slot_weights",
    )(count_row, dist_t, w_filter)

    blocks = range(slots // 4)
    index_flat = index_t.reshape(slots * atoms)
    hidden_second, part = pl.pallas_call(
        lambda *refs: neighbour_kernel(*refs, scale=scale),
        grid=(1,),
        in_specs=[smem] + [
            pl.BlockSpec((4 * atoms,), lambda i, at=at: (at,), memory_space=pltpu.SMEM) for at in blocks
        ] + [
            pl.BlockSpec((atoms, slots, hid), lambda i: (0, 0, 0)),
            whole((kv * atoms, hid)),
            whole((halo, hid)),
            whole((halo, hid)),
            whole((atoms, hid)),
            whole((chan, hid)),
            whole((atoms, waves)),
            whole((atoms, waves)),
            whole((3, waves)),
        ],
        out_specs=(whole((atoms, hid)), whole((part_rows, 128))),
        out_shape=(shape((atoms, hid), BF16), shape((part_rows, 128), BF16)),
        scratch_shapes=[pltpu.VMEM((kv * atoms + 2 * halo + 8, hid), F32), pltpu.VMEM((8 * atoms, hid), F32)],
        compiler_params=vmem(20),
        name="neighbours",
    )(
        *in_hbm(nbr_count), *[index_flat] * len(blocks), weights, v_dom, from_far, from_near,
        hidden_first, w_charge_second, cos_table, sin_table, wave_vectors,
    )
    sums = everything(part)
    return pl.pallas_call(
        last_project_kernel,
        out_shape=(shape((atoms, hid), BF16), shape((3, atoms), F32)),
        scratch_shapes=[pltpu.VMEM((4 * chan, waves), BF16)] * 2,
        compiler_params=vmem(6),
        name="project_second",
    )(
        sums, cos_table, sin_table, wave_vectors, hidden_second, w_charge_second, w_long_second, force_first,
    )


def solution(mesh):
    sizes = tuple(size for _, size in PARTS)
    return jax.shard_map(
        local,
        mesh=jax.sharding.Mesh(mesh.devices.reshape(sizes), EVERY),
        in_specs=(
            P(None, EVERY), P(EVERY, None), P(EVERY, None), P(EVERY), P(EVERY, None), P(DOM, None, None),
            P(), P(), P(), P(), P(), P(), P(),
        ),
        out_specs=(P(EVERY, None), P(None, EVERY)),
        check_vma=False,
    )
```

```python
import math

import jax
import jax.numpy as jnp
from jax import lax
from jax.experimental import pallas as pl
from jax.experimental.pallas import tpu as pltpu
from jax.sharding import PartitionSpec as P

F32 = jnp.float32
BF16 = jnp.bfloat16
HIGHEST = lax.Precision.HIGHEST
LONG_SCALE = 2.0
CELL = 60.0
PARTS = (("xlo", 2), ("z", 8), ("core", 2), ("y", 4), ("xhi", 2))
EVERY = tuple(name for name, _ in PARTS)
DOM = ("xlo", "z", "core")
KV = ("y", "xhi")
UNROLL = 2
STEPS = 2
LINE = ("z",)
PLANE = ("xlo", "core", "y", "xhi")

COS_COEF = (
    0.9999992251396179,
    -19.738981246948242,
    64.92865753173828,
    -85.27162170410156,
    58.79049301147461,
    -21.07110595703125,
)
SIN_COEF = (
    6.283185005187988,
    -41.341590881347656,
    81.59994506835938,
    -76.61447143554688,
    41.3428840637207,
    -12.471243858337402,
)

NN = (((1,), (0,)), ((), ()))
NT = (((1,), (1,)), ((), ()))
TN = (((0,), (0,)), ((), ()))


def horner(coefs, v):
    total = v * coefs[-1] + coefs[-2]
    for coef in coefs[-3::-1]:
        total = total * v + coef
    return total


def dot(a, b, dims=NN, precision=None):
    return lax.dot_general(a, b, dims, precision=precision, preferred_element_type=F32)


def silu(x):
    return x / (1.0 + jnp.exp(-x))


def wave_weight(wave):
    sq_norm = wave[0:1] * wave[0:1] + wave[1:2] * wave[1:2] + wave[2:3] * wave[2:3]
    return jnp.exp(-0.5 * sq_norm) / (sq_norm + 1.0)


def split_rows(x):
    high = x.astype(BF16)
    return jnp.concatenate([high, (x - high.astype(F32)).astype(BF16)], axis=0)


def structure_part(charge_t, cos_ref, sin_ref, wave_ref, part_ref, scale):
    chan = charge_t.shape[0]
    waves = cos_ref.shape[1]
    rows = split_rows(charge_t)
    cos_sum = dot(rows, cos_ref[...])
    sin_sum = dot(rows, sin_ref[...])
    weight = wave_weight(wave_ref[...]) * scale
    cos_sum = (cos_sum[:chan] + cos_sum[chan:]) * weight
    sin_sum = (sin_sum[:chan] + sin_sum[chan:]) * weight
    for t in range(waves // 128):
        lanes = slice(t * 128, (t + 1) * 128)
        part_ref[t * 2 * chan : t * 2 * chan + chan, :] = cos_sum[:, lanes].astype(BF16)
        part_ref[t * 2 * chan + chan : (t + 1) * 2 * chan, :] = sin_sum[:, lanes].astype(BF16)


def table_kernel(*refs, scale):
    later = (len(refs) - 6) // 2
    pos_ref, kept_in, cos_ref, sin_ref, part_ref = refs[0], refs[1 : 1 + later], *refs[1 + later : 4 + later]
    kept_out, turns, pad = refs[4 + later : -2], *refs[-2:]
    feat_ref, wc_ref, wave_ref = kept_in[:3]
    atoms, waves = cos_ref.shape
    for in_ref, out_ref in zip(kept_in, kept_out):
        out_ref[...] = in_ref[...]
    pad[...] = jnp.zeros_like(pad)
    pad[0:3, :] = pos_ref[...] * (1.0 / CELL)
    columns = jnp.transpose(pad[...])
    for c in range(3):
        turns[c] = jnp.broadcast_to(columns[:, c : c + 1], (atoms, 128))
    rows = 64

    def one_tile(t, carry):
        lanes = pl.ds(pl.multiple_of(t * 128, 128), 128)
        whole = jnp.round(wave_ref[:, lanes] * (CELL / (2.0 * math.pi)))
        for b in range(atoms // rows):
            at = slice(b * rows, (b + 1) * rows)
            u = (
                turns[0, at, :] * whole[0:1]
                + turns[1, at, :] * whole[1:2]
                + turns[2, at, :] * whole[2:3]
            )
            u = u - jnp.round(u)
            v = u * u
            cos_ref[at, lanes] = horner(COS_COEF, v).astype(BF16)
            sin_ref[at, lanes] = (u * horner(SIN_COEF, v)).astype(BF16)
        return carry

    lax.fori_loop(0, waves // 128, one_tile, 0)
    charge_t = dot(wc_ref[...], feat_ref[...], NT)
    structure_part(charge_t, cos_ref, sin_ref, wave_ref, part_ref, scale)


def fold_kernel(in_ref, out_ref, *, members, copies):
    rows = in_ref.shape[0] // members
    total = in_ref[0:rows, :].astype(F32)
    for m in range(1, members):
        total = total + in_ref[m * rows : (m + 1) * rows, :].astype(F32)
    total = total.astype(out_ref.dtype)
    for m in range(copies):
        out_ref[m * rows : (m + 1) * rows, :] = total


def project(sums_ref, cos_ref, sin_ref, wave_ref, charge_t, with_cos, with_sin):
    chan = charge_t.shape[0]
    waves = cos_ref.shape[1]
    for t in range(waves // 128):
        lanes = slice(t * 128, (t + 1) * 128)
        wave = wave_ref[:, lanes]
        cos_w = sums_ref[t * 2 * chan : t * 2 * chan + chan, :].astype(F32)
        sin_w = sums_ref[t * 2 * chan + chan : (t + 1) * 2 * chan, :].astype(F32)
        with_cos[0:chan, lanes] = cos_w.astype(BF16)
        with_sin[0:chan, lanes] = sin_w.astype(BF16)
        for c in range(3):
            at = slice((c + 1) * chan, (c + 2) * chan)
            with_cos[at, lanes] = (-wave[c : c + 1] * sin_w).astype(BF16)
            with_sin[at, lanes] = (wave[c : c + 1] * cos_w).astype(BF16)
    both = dot(with_cos[...], cos_ref[...], NT) + dot(with_sin[...], sin_ref[...], NT)
    potential_t = both[:chan]
    force = [
        jnp.sum(charge_t * both[(c + 1) * chan : (c + 2) * chan], axis=0, keepdims=True)
        for c in range(3)
    ]
    return potential_t, force


def first_project_kernel(
    sums_ref, cos_ref, sin_ref, wave_ref, feat_ref, wc_ref, wl_ref, wv_ref,
    hidden_ref, values_ref, force_ref, with_cos, with_sin,
):
    charge_t = dot(wc_ref[...], feat_ref[...], NT)
    potential_t, force = project(sums_ref, cos_ref, sin_ref, wave_ref, charge_t, with_cos, with_sin)
    for c in range(3):
        force_ref[c : c + 1, :] = force[c]
    lifted = dot(potential_t, wl_ref[...], TN, HIGHEST)
    hidden = (feat_ref[...].astype(F32) + silu(lifted)).astype(BF16)
    hidden_ref[...] = hidden
    values = dot(hidden, wv_ref[...]).astype(BF16)
    atoms = values.shape[0]
    for j in range(values_ref.shape[0] // atoms):
        values_ref[j * atoms : (j + 1) * atoms, :] = values


def last_project_kernel(
    sums_ref, cos_ref, sin_ref, wave_ref, hidden_ref, wc_ref, wl_ref, force_in,
    feat_out, force_out, with_cos, with_sin,
):
    charge_t = dot(wc_ref[...], hidden_ref[...], NT)
    potential_t, force = project(sums_ref, cos_ref, sin_ref, wave_ref, charge_t, with_cos, with_sin)
    for c in range(3):
        force_out[c : c + 1, :] = force_in[c : c + 1, :] + force[c]
    lifted = dot(potential_t, wl_ref[...], TN, HIGHEST)
    feat_out[...] = (hidden_ref[...].astype(F32) + silu(lifted)).astype(BF16)


def row_tile(table, rows, bits):
    tiles = [table[pl.ds(row, 8, stride=0), :] for row in rows]
    for bit in bits:
        tiles = [jnp.where(bit, odd, even) for even, odd in zip(tiles[::2], tiles[1::2])]
    return tiles[0]


def sublane_bits():
    sub = lax.broadcasted_iota(jnp.int32, (8, 128), 0)
    return [(sub & bit) != 0 for bit in (1, 2, 4)]


def halo_kernel(*refs, far):
    lists, (values_ref, out_ref, table, picked) = refs[:-4], refs[-4:]
    core = lax.axis_index("core")
    side = 1 - core if far else core
    table[0 : values_ref.shape[0], :] = values_ref[...].astype(F32)
    bits = sublane_bits()

    def some_rows(g, carry):
        first = g * 8
        for b, list_ref in enumerate(lists):
            rows = [list_ref[side, first + j] for j in range(8)]
            picked[pl.ds(pl.multiple_of(b * 128 + first, 8), 8), :] = row_tile(table, rows, bits)
        return carry

    lax.fori_loop(0, 16, some_rows, 0)
    out_ref[...] = picked[...].astype(BF16)


def weight_kernel(count_ref, dist_ref, wf_ref, out_ref, turned, near, taper, wide, *, steps):
    slots, atoms = dist_ref.shape
    basis = wf_ref.shape[0]
    pairs = atoms // 2 // steps
    sharpness = ((basis - 1) / 4.5) ** 2

    def paired(block):
        turned[...] = jnp.transpose(block)
        return jnp.concatenate(
            [turned[pl.ds(0, atoms // 2, stride=2), :], turned[pl.ds(1, atoms // 2, stride=2), :]], axis=1
        )

    dist = dist_ref[...]
    scaled = dist * 0.1
    height = 0.5 * (horner(COS_COEF, scaled * scaled) + 1.0)
    slot = lax.broadcasted_iota(jnp.int32, (slots, atoms), 0)
    near[...] = paired(dist)
    taper[...] = paired(jnp.where(slot < count_ref[...], height, 0.0))
    wf_high = wf_ref[...].astype(BF16)
    wide[0:basis, :] = wf_high
    wide[basis : 2 * basis, :] = (wf_ref[...] - wf_high.astype(F32)).astype(BF16)
    centers = 0.5 + 4.5 / (basis - 1) * lax.broadcasted_iota(jnp.int32, (basis, 2 * slots), 0).astype(F32)

    def some_pairs(step, carry):
        for p in range(pairs):
            row = pl.ds(step * pairs + p, 1)
            away = near[row, :] - centers
            radial = (jnp.exp(-sharpness * (away * away)) * taper[row, :]).astype(BF16)
            both = dot(jnp.concatenate([radial, radial], axis=0), wide[...], TN)
            out_ref[2 * (step * pairs + p)] = both[:slots]
            out_ref[2 * (step * pairs + p) + 1] = both[slots:]
        return carry

    lax.fori_loop(0, steps, some_pairs, 0)


def neighbour_kernel(*refs, scale):
    count_ref, index_refs = refs[0], refs[1:-13]
    (
        weight_ref, values_ref, far_ref, near_ref, hidden_ref, wc_ref, cos_ref, sin_ref, wave_ref,
        hidden_out, part_ref, table, sums,
    ) = refs[-13:]
    own = values_ref.shape[0]
    halo = far_ref.shape[0]
    atoms, slots, _ = weight_ref.shape
    core = lax.axis_index("core")
    table[0:own, :] = values_ref[...].astype(F32)
    table[pl.ds(pl.multiple_of(own + (1 - core) * halo, 8), halo), :] = near_ref[...].astype(F32)
    table[pl.ds(pl.multiple_of(own + core * halo, 8), halo), :] = far_ref[...].astype(F32)
    bits = sublane_bits()

    def some_atoms(group, carry):
        for k in range(UNROLL):
            one_atom(group * UNROLL + k)
        return carry

    def one_atom(atom):
        at = pl.ds(pl.multiple_of(atom * 8, 8), 8)
        spots = [atom + q * atoms for q in range(4)]

        def some_slots(blocks):
            total = jnp.zeros((8, 128), F32)
            for b in blocks:
                rows = [index_refs[2 * b + s // 4][spots[s % 4]] for s in range(8)]
                total = total + row_tile(table, rows, bits) * weight_ref[atom, 8 * b : 8 * b + 8, :]
            return total

        middle = slots // 16
        sums[at, :] = some_slots(range(middle))

        @pl.when(count_ref[atom] > middle * 8)
        def _():
            sums[at, :] = sums[at, :] + some_slots(range(middle, slots // 8))

    lax.fori_loop(0, atoms // UNROLL, some_atoms, 0)
    message = sums[pl.ds(0, atoms, stride=8), :]
    for k in range(1, 8):
        message = message + sums[pl.ds(k, atoms, stride=8), :]
    hidden = (hidden_ref[...].astype(F32) + silu(message)).astype(BF16)
    hidden_out[...] = hidden
    charge_t = dot(wc_ref[...], hidden, NT)
    structure_part(charge_t, cos_ref, sin_ref, wave_ref, part_ref, scale)


def shape(dims, kind):
    return jax.ShapeDtypeStruct(dims, kind)


def in_hbm(*arrays):
    return tuple(pltpu.with_memory_space_constraint(array, pltpu.HBM) for array in arrays)


def vmem(mib):
    return pltpu.CompilerParams(vmem_limit_bytes=mib * 1024 * 1024)


def fold(sums, members, copies, kind):
    rows = sums.shape[0] // members
    return pl.pallas_call(
        lambda *refs: fold_kernel(*refs, members=members, copies=copies),
        out_shape=shape((copies * rows, sums.shape[1]), kind),
        compiler_params=vmem(2),
    )(sums)


def everything(part):
    line = lax.axis_size(LINE)
    plane = lax.axis_size(PLANE)
    share = lax.all_to_all(part, PLANE, 0, 0, tiled=True)
    share = fold(share, plane, line, F32)
    share = lax.all_to_all(share, LINE, 0, 0, tiled=True)
    share = fold(share, line, plane, BF16)
    return lax.all_to_all(share, PLANE, 0, 0, tiled=True)


def local(
    positions, features, nbr_index, nbr_count, nbr_dist, halo_lists, wave_vectors,
    w_charge_first, w_long_first, w_value, w_filter, w_charge_second, w_long_second,
):
    atoms, hid = features.shape
    chan = w_charge_first.shape[1]
    waves = wave_vectors.shape[1]
    slots = nbr_index.shape[1]
    kv = lax.axis_size(KV)
    doms = lax.axis_size(DOM)
    total_atoms = atoms * doms * kv
    scale = LONG_SCALE / math.sqrt(waves) / math.sqrt(total_atoms)
    part_rows = 2 * chan * waves // 128
    halo = halo_lists.shape[2]
    smem = pl.BlockSpec(memory_space=pltpu.SMEM)
    w_charge_first = w_charge_first.T
    w_charge_second = w_charge_second.T
    lists = halo_lists[0]
    index_t = nbr_index.T
    dist_t = nbr_dist.T

    kept = (
        features, w_charge_first, wave_vectors, w_long_first, w_value, w_charge_second, w_long_second,
        dist_t, nbr_count.reshape(1, atoms), w_filter, lists,
    )
    cos_table, sin_table, part, *kept = pl.pallas_call(
        lambda *refs: table_kernel(*refs, scale=scale),
        out_shape=(
            shape((atoms, waves), BF16), shape((atoms, waves), BF16), shape((part_rows, 128), BF16),
            *(shape(a.shape, a.dtype) for a in kept),
        ),
        scratch_shapes=[pltpu.VMEM((3, atoms, 128), F32), pltpu.VMEM((8, atoms), F32)],
        compiler_params=vmem(6),
        name="tables",
    )(*in_hbm(positions, *kept))
    (
        features, w_charge_first, wave_vectors, w_long_first, w_value, w_charge_second, w_long_second,
        dist_t, count_row, w_filter, lists,
    ) = kept
    sums = everything(part)
    hidden_first, values, force_first = pl.pallas_call(
        first_project_kernel,
        out_shape=(shape((atoms, hid), BF16), shape((kv * atoms, hid), BF16), shape((3, atoms), F32)),
        scratch_shapes=[pltpu.VMEM((4 * chan, waves), BF16)] * 2,
        compiler_params=vmem(6),
        name="project_first",
    )(sums, cos_table, sin_table, wave_vectors, features, w_charge_first, w_long_first, w_value)

    v_dom = lax.all_to_all(values, KV, 0, 0, tiled=True)

    def halo_rows(far, source):
        return pl.pallas_call(
            lambda *refs: halo_kernel(*refs, far=far),
            grid=(1,),
            in_specs=[
                pl.BlockSpec((2, 128), lambda i, b=b: (0, b), memory_space=pltpu.SMEM) for b in range(halo // 128)
            ] + [pl.BlockSpec((kv * atoms, hid), lambda i: (0, 0))],
            out_specs=pl.BlockSpec((halo, hid), lambda i: (0, 0)),
            out_shape=shape((halo, hid), BF16),
            scratch_shapes=[pltpu.VMEM((kv * atoms + 8, hid), F32), pltpu.VMEM((halo, hid), F32)],
            compiler_params=vmem(6),
            cost_estimate=pl.CostEstimate(flops=halo * hid, bytes_accessed=4 * kv * atoms * hid, transcendentals=0),
            name="halo_far" if far else "halo_near",
        )(*[lists] * (halo // 128), source)

    to_far = halo_rows(True, v_dom)
    to_far, source, index_t = lax.optimization_barrier((to_far, v_dom, index_t))
    from_far = lax.ppermute(to_far, DOM, [(i, (i - 1 + 2 * (i % 2)) % doms) for i in range(doms)])
    to_near = halo_rows(False, source)
    from_near = lax.ppermute(to_near, DOM, [(i, i + 1 - 2 * (i % 2)) for i in range(doms)])

    whole = lambda dims: pl.BlockSpec(dims, lambda i: (0,) * len(dims))
    weights = pl.pallas_call(
        lambda *refs: weight_kernel(*refs, steps=STEPS),
        grid=(1,),
        in_specs=[whole((1, atoms)), whole((slots, atoms)), whole(w_filter.shape)],
        out_specs=whole((atoms, slots, hid)),
        out_shape=shape((atoms, slots, hid), F32),
        scratch_shapes=[
            pltpu.VMEM((atoms, slots), F32),
            pltpu.VMEM((atoms // 2, 2 * slots), F32),
            pltpu.VMEM((atoms // 2, 2 * slots), F32),
            pltpu.VMEM((2 * w_filter.shape[0], hid), BF16),
        ],
        cost_estimate=pl.CostEstimate(
            flops=2 * atoms * slots * hid * 32,
            bytes_accessed=atoms * slots * hid * 4,
            transcendentals=atoms * slots * 16,
        ),
        compiler_params=vmem(12),
        name="slot_weights",
    )(count_row, dist_t, w_filter)

    blocks = range(slots // 4)
    index_flat = index_t.reshape(slots * atoms)
    hidden_second, part = pl.pallas_call(
        lambda *refs: neighbour_kernel(*refs, scale=scale),
        grid=(1,),
        in_specs=[smem] + [
            pl.BlockSpec((4 * atoms,), lambda i, at=at: (at,), memory_space=pltpu.SMEM) for at in blocks
        ] + [
            pl.BlockSpec((atoms, slots, hid), lambda i: (0, 0, 0)),
            whole((kv * atoms, hid)),
            whole((halo, hid)),
            whole((halo, hid)),
            whole((atoms, hid)),
            whole((chan, hid)),
            whole((atoms, waves)),
            whole((atoms, waves)),
            whole((3, waves)),
        ],
        out_specs=(whole((atoms, hid)), whole((part_rows, 128))),
        out_shape=(shape((atoms, hid), BF16), shape((part_rows, 128), BF16)),
        scratch_shapes=[pltpu.VMEM((kv * atoms + 2 * halo + 8, hid), F32), pltpu.VMEM((8 * atoms, hid), F32)],
        compiler_params=vmem(20),
        name="neighbours",
    )(
        *in_hbm(nbr_count), *[index_flat] * len(blocks), weights, v_dom, from_far, from_near,
        hidden_first, w_charge_second, cos_table, sin_table, wave_vectors,
    )
    sums = everything(part)
    return pl.pallas_call(
        last_project_kernel,
        out_shape=(shape((atoms, hid), BF16), shape((3, atoms), F32)),
        scratch_shapes=[pltpu.VMEM((4 * chan, waves), BF16)] * 2,
        compiler_params=vmem(6),
        name="project_second",
    )(
        sums, cos_table, sin_table, wave_vectors, hidden_second, w_charge_second, w_long_second, force_first,
    )


def solution(mesh):
    sizes = tuple(size for _, size in PARTS)
    return jax.shard_map(
        local,
        mesh=jax.sharding.Mesh(mesh.devices.reshape(sizes), EVERY),
        in_specs=(
            P(None, EVERY), P(EVERY, None), P(EVERY, None), P(EVERY), P(EVERY, None), P(DOM, None, None),
            P(), P(), P(), P(), P(), P(), P(),
        ),
        out_specs=(P(EVERY, None), P(None, EVERY)),
        check_vma=False,
    )
```

```python
import math

import jax
import jax.numpy as jnp
from jax import lax
from jax.experimental import pallas as pl
from jax.experimental.pallas import tpu as pltpu
from jax.sharding import PartitionSpec as P

F32 = jnp.float32
BF16 = jnp.bfloat16
HIGHEST = lax.Precision.HIGHEST
LONG_SCALE = 2.0
CELL = 60.0
PARTS = (("xlo", 2), ("z", 8), ("core", 2), ("y", 4), ("xhi", 2))
EVERY = tuple(name for name, _ in PARTS)
DOM = ("xlo", "z", "core")
KV = ("y", "xhi")
UNROLL = 2
TILES = 4
STEPS = 2
LINE = ("z",)
PLANE = ("xlo", "core", "y", "xhi")

COS_COEF = (
    0.9999992251396179,
    -19.738981246948242,
    64.92865753173828,
    -85.27162170410156,
    58.79049301147461,
    -21.07110595703125,
)
SIN_COEF = (
    6.283185005187988,
    -41.341590881347656,
    81.59994506835938,
    -76.61447143554688,
    41.3428840637207,
    -12.471243858337402,
)

NN = (((1,), (0,)), ((), ()))
NT = (((1,), (1,)), ((), ()))
TN = (((0,), (0,)), ((), ()))


def horner(coefs, v):
    total = v * coefs[-1] + coefs[-2]
    for coef in coefs[-3::-1]:
        total = total * v + coef
    return total


def dot(a, b, dims=NN, precision=None):
    return lax.dot_general(a, b, dims, precision=precision, preferred_element_type=F32)


def silu(x):
    return x / (1.0 + jnp.exp(-x))


def wave_weight(wave):
    sq_norm = wave[0:1] * wave[0:1] + wave[1:2] * wave[1:2] + wave[2:3] * wave[2:3]
    return jnp.exp(-0.5 * sq_norm) / (sq_norm + 1.0)


def split_rows(x):
    high = x.astype(BF16)
    return jnp.concatenate([high, (x - high.astype(F32)).astype(BF16)], axis=0)


def structure_part(charge_t, cos_ref, sin_ref, wave_ref, part_ref, scale):
    chan = charge_t.shape[0]
    waves = cos_ref.shape[1]
    rows = split_rows(charge_t)
    cos_sum = dot(rows, cos_ref[...])
    sin_sum = dot(rows, sin_ref[...])
    weight = wave_weight(wave_ref[...]) * scale
    cos_sum = (cos_sum[:chan] + cos_sum[chan:]) * weight
    sin_sum = (sin_sum[:chan] + sin_sum[chan:]) * weight
    for t in range(waves // 128):
        lanes = slice(t * 128, (t + 1) * 128)
        part_ref[t * 2 * chan : t * 2 * chan + chan, :] = cos_sum[:, lanes].astype(BF16)
        part_ref[t * 2 * chan + chan : (t + 1) * 2 * chan, :] = sin_sum[:, lanes].astype(BF16)


def table_kernel(*refs, scale):
    later = (len(refs) - 6) // 2
    pos_ref, kept_in, cos_ref, sin_ref, part_ref = refs[0], refs[1 : 1 + later], *refs[1 + later : 4 + later]
    kept_out, turns, pad = refs[4 + later : -2], *refs[-2:]
    feat_ref, wc_ref, wave_ref = kept_in[:3]
    atoms, waves = cos_ref.shape
    for in_ref, out_ref in zip(kept_in, kept_out):
        out_ref[...] = in_ref[...]
    pad[...] = jnp.zeros_like(pad)
    pad[0:3, :] = pos_ref[...] * (1.0 / CELL)
    columns = jnp.transpose(pad[...])
    for c in range(3):
        turns[c] = jnp.broadcast_to(columns[:, c : c + 1], (atoms, 128))
    rows = 64

    def one_tile(t):
        lanes = pl.ds(pl.multiple_of(t * 128, 128), 128)
        whole = jnp.round(wave_ref[:, lanes] * (CELL / (2.0 * math.pi)))
        for b in range(atoms // rows):
            at = slice(b * rows, (b + 1) * rows)
            u = (
                turns[0, at, :] * whole[0:1]
                + turns[1, at, :] * whole[1:2]
                + turns[2, at, :] * whole[2:3]
            )
            u = u - jnp.round(u)
            v = u * u
            cos_ref[at, lanes] = horner(COS_COEF, v).astype(BF16)
            sin_ref[at, lanes] = (u * horner(SIN_COEF, v)).astype(BF16)

    def some_tiles(g, carry):
        for k in range(TILES):
            one_tile(g * TILES + k)
        return carry

    lax.fori_loop(0, waves // 128 // TILES, some_tiles, 0)
    charge_t = dot(wc_ref[...], feat_ref[...], NT)
    structure_part(charge_t, cos_ref, sin_ref, wave_ref, part_ref, scale)


def fold_kernel(in_ref, out_ref, *, members, copies):
    rows = in_ref.shape[0] // members
    total = in_ref[0:rows, :].astype(F32)
    for m in range(1, members):
        total = total + in_ref[m * rows : (m + 1) * rows, :].astype(F32)
    total = total.astype(out_ref.dtype)
    for m in range(copies):
        out_ref[m * rows : (m + 1) * rows, :] = total


def project(sums_ref, cos_ref, sin_ref, wave_ref, charge_t, with_cos, with_sin):
    chan = charge_t.shape[0]
    waves = cos_ref.shape[1]
    for t in range(waves // 128):
        lanes = slice(t * 128, (t + 1) * 128)
        wave = wave_ref[:, lanes]
        cos_w = sums_ref[t * 2 * chan : t * 2 * chan + chan, :].astype(F32)
        sin_w = sums_ref[t * 2 * chan + chan : (t + 1) * 2 * chan, :].astype(F32)
        with_cos[0:chan, lanes] = cos_w.astype(BF16)
        with_sin[0:chan, lanes] = sin_w.astype(BF16)
        for c in range(3):
            at = slice((c + 1) * chan, (c + 2) * chan)
            with_cos[at, lanes] = (-wave[c : c + 1] * sin_w).astype(BF16)
            with_sin[at, lanes] = (wave[c : c + 1] * cos_w).astype(BF16)
    both = dot(with_cos[...], cos_ref[...], NT) + dot(with_sin[...], sin_ref[...], NT)
    potential_t = both[:chan]
    force = [
        jnp.sum(charge_t * both[(c + 1) * chan : (c + 2) * chan], axis=0, keepdims=True)
        for c in range(3)
    ]
    return potential_t, force


def first_project_kernel(
    sums_ref, cos_ref, sin_ref, wave_ref, feat_ref, wc_ref, wl_ref, wv_ref,
    hidden_ref, values_ref, force_ref, with_cos, with_sin,
):
    charge_t = dot(wc_ref[...], feat_ref[...], NT)
    potential_t, force = project(sums_ref, cos_ref, sin_ref, wave_ref, charge_t, with_cos, with_sin)
    for c in range(3):
        force_ref[c : c + 1, :] = force[c]
    lifted = dot(potential_t, wl_ref[...], TN, HIGHEST)
    hidden = (feat_ref[...].astype(F32) + silu(lifted)).astype(BF16)
    hidden_ref[...] = hidden
    values = dot(hidden, wv_ref[...]).astype(BF16)
    atoms = values.shape[0]
    for j in range(values_ref.shape[0] // atoms):
        values_ref[j * atoms : (j + 1) * atoms, :] = values


def last_project_kernel(
    sums_ref, cos_ref, sin_ref, wave_ref, hidden_ref, wc_ref, wl_ref, force_in,
    feat_out, force_out, with_cos, with_sin,
):
    charge_t = dot(wc_ref[...], hidden_ref[...], NT)
    potential_t, force = project(sums_ref, cos_ref, sin_ref, wave_ref, charge_t, with_cos, with_sin)
    for c in range(3):
        force_out[c : c + 1, :] = force_in[c : c + 1, :] + force[c]
    lifted = dot(potential_t, wl_ref[...], TN, HIGHEST)
    feat_out[...] = (hidden_ref[...].astype(F32) + silu(lifted)).astype(BF16)


def row_tile(table, rows, bits):
    tiles = [table[pl.ds(row, 8, stride=0), :] for row in rows]
    for bit in bits:
        tiles = [jnp.where(bit, odd, even) for even, odd in zip(tiles[::2], tiles[1::2])]
    return tiles[0]


def sublane_bits():
    sub = lax.broadcasted_iota(jnp.int32, (8, 128), 0)
    return [(sub & bit) != 0 for bit in (1, 2, 4)]


def halo_kernel(*refs, far):
    list_ref, values_ref, out_ref, table, picked, arrived = refs[:6]
    lists = refs[6:]
    fetches = [
        pltpu.make_async_copy(list_ref.at[:, pl.ds(b * 128, 128)], part_ref, arrived.at[b])
        for b, part_ref in enumerate(lists)
    ]
    for fetch in fetches:
        fetch.start()
    core = lax.axis_index("core")
    side = 1 - core if far else core
    table[0 : values_ref.shape[0], :] = values_ref[...].astype(F32)
    bits = sublane_bits()
    for fetch in fetches:
        fetch.wait()

    def some_rows(g, carry):
        first = g * 8
        for b, part_ref in enumerate(lists):
            rows = [part_ref[side, first + j] for j in range(8)]
            picked[pl.ds(pl.multiple_of(b * 128 + first, 8), 8), :] = row_tile(table, rows, bits)
        return carry

    lax.fori_loop(0, 16, some_rows, 0)
    out_ref[...] = picked[...].astype(BF16)


def weight_kernel(count_ref, dist_ref, wf_ref, out_ref, turned, near, taper, wide, *, steps):
    slots, atoms = dist_ref.shape
    basis = wf_ref.shape[0]
    pairs = atoms // 2 // steps
    sharpness = ((basis - 1) / 4.5) ** 2

    def paired(block):
        turned[...] = jnp.transpose(block)
        return jnp.concatenate(
            [turned[pl.ds(0, atoms // 2, stride=2), :], turned[pl.ds(1, atoms // 2, stride=2), :]], axis=1
        )

    dist = dist_ref[...]
    scaled = dist * 0.1
    height = 0.5 * (horner(COS_COEF, scaled * scaled) + 1.0)
    slot = lax.broadcasted_iota(jnp.int32, (slots, atoms), 0)
    near[...] = paired(dist)
    taper[...] = paired(jnp.where(slot < count_ref[...], height, 0.0))
    wf_high = wf_ref[...].astype(BF16)
    wide[0:basis, :] = wf_high
    wide[basis : 2 * basis, :] = (wf_ref[...] - wf_high.astype(F32)).astype(BF16)
    centers = 0.5 + 4.5 / (basis - 1) * lax.broadcasted_iota(jnp.int32, (basis, 2 * slots), 0).astype(F32)

    def some_pairs(step, carry):
        for p in range(pairs):
            row = pl.ds(step * pairs + p, 1)
            away = near[row, :] - centers
            radial = (jnp.exp(-sharpness * (away * away)) * taper[row, :]).astype(BF16)
            both = dot(jnp.concatenate([radial, radial], axis=0), wide[...], TN)
            out_ref[2 * (step * pairs + p)] = both[:slots]
            out_ref[2 * (step * pairs + p) + 1] = both[slots:]
        return carry

    lax.fori_loop(0, steps, some_pairs, 0)


def neighbour_kernel(*refs, scale):
    (
        count_ref, list_ref, weight_ref, values_ref, far_ref, near_ref, hidden_ref, wc_ref, cos_ref, sin_ref, wave_ref,
        hidden_out, part_ref, table, sums, arrived,
    ) = refs[:16]
    index_refs = refs[16:]
    size = index_refs[0].shape[0]
    fetches = [
        pltpu.make_async_copy(list_ref.at[pl.ds(b * size, size)], index_ref, arrived.at[b])
        for b, index_ref in enumerate(index_refs)
    ]
    for fetch in fetches:
        fetch.start()
    own = values_ref.shape[0]
    halo = far_ref.shape[0]
    atoms, slots, _ = weight_ref.shape
    core = lax.axis_index("core")
    table[0:own, :] = values_ref[...].astype(F32)
    table[pl.ds(pl.multiple_of(own + (1 - core) * halo, 8), halo), :] = near_ref[...].astype(F32)
    table[pl.ds(pl.multiple_of(own + core * halo, 8), halo), :] = far_ref[...].astype(F32)
    bits = sublane_bits()
    for fetch in fetches:
        fetch.wait()

    def some_atoms(group, carry):
        for k in range(UNROLL):
            one_atom(group * UNROLL + k)
        return carry

    def one_atom(atom):
        at = pl.ds(pl.multiple_of(atom * 8, 8), 8)
        spots = [atom + q * atoms for q in range(4)]

        def some_slots(blocks):
            total = jnp.zeros((8, 128), F32)
            for b in blocks:
                rows = [index_refs[2 * b + s // 4][spots[s % 4]] for s in range(8)]
                total = total + row_tile(table, rows, bits) * weight_ref[atom, 8 * b : 8 * b + 8, :]
            return total

        middle = slots // 16
        sums[at, :] = some_slots(range(middle))

        @pl.when(count_ref[atom] > middle * 8)
        def _():
            sums[at, :] = sums[at, :] + some_slots(range(middle, slots // 8))

    lax.fori_loop(0, atoms // UNROLL, some_atoms, 0)
    message = sums[pl.ds(0, atoms, stride=8), :]
    for k in range(1, 8):
        message = message + sums[pl.ds(k, atoms, stride=8), :]
    hidden = (hidden_ref[...].astype(F32) + silu(message)).astype(BF16)
    hidden_out[...] = hidden
    charge_t = dot(wc_ref[...], hidden, NT)
    structure_part(charge_t, cos_ref, sin_ref, wave_ref, part_ref, scale)


def shape(dims, kind):
    return jax.ShapeDtypeStruct(dims, kind)


def in_hbm(*arrays):
    return tuple(pltpu.with_memory_space_constraint(array, pltpu.HBM) for array in arrays)


def vmem(mib):
    return pltpu.CompilerParams(vmem_limit_bytes=mib * 1024 * 1024)


def fold(sums, members, copies, kind):
    rows = sums.shape[0] // members
    return pl.pallas_call(
        lambda *refs: fold_kernel(*refs, members=members, copies=copies),
        out_shape=shape((copies * rows, sums.shape[1]), kind),
        compiler_params=vmem(2),
    )(sums)


def everything(part):
    line = lax.axis_size(LINE)
    plane = lax.axis_size(PLANE)
    share = lax.all_to_all(part, PLANE, 0, 0, tiled=True)
    share = fold(share, plane, line, F32)
    share = lax.all_to_all(share, LINE, 0, 0, tiled=True)
    share = fold(share, line, plane, BF16)
    return lax.all_to_all(share, PLANE, 0, 0, tiled=True)


def local(
    positions, features, nbr_index, nbr_count, nbr_dist, halo_lists, wave_vectors,
    w_charge_first, w_long_first, w_value, w_filter, w_charge_second, w_long_second,
):
    atoms, hid = features.shape
    chan = w_charge_first.shape[1]
    waves = wave_vectors.shape[1]
    slots = nbr_index.shape[1]
    kv = lax.axis_size(KV)
    doms = lax.axis_size(DOM)
    total_atoms = atoms * doms * kv
    scale = LONG_SCALE / math.sqrt(waves) / math.sqrt(total_atoms)
    part_rows = 2 * chan * waves // 128
    halo = halo_lists.shape[2]
    smem = pl.BlockSpec(memory_space=pltpu.SMEM)
    w_charge_first = w_charge_first.T
    w_charge_second = w_charge_second.T
    lists = halo_lists[0]
    index_t = nbr_index.T
    dist_t = nbr_dist.T

    kept = (
        features, w_charge_first, wave_vectors, w_long_first, w_value, w_charge_second, w_long_second,
        dist_t, nbr_count.reshape(1, atoms), w_filter, lists,
    )
    cos_table, sin_table, part, *kept = pl.pallas_call(
        lambda *refs: table_kernel(*refs, scale=scale),
        out_shape=(
            shape((atoms, waves), BF16), shape((atoms, waves), BF16), shape((part_rows, 128), BF16),
            *(shape(a.shape, a.dtype) for a in kept),
        ),
        scratch_shapes=[pltpu.VMEM((3, atoms, 128), F32), pltpu.VMEM((8, atoms), F32)],
        compiler_params=vmem(6),
        name="tables",
    )(*in_hbm(positions, *kept))
    (
        features, w_charge_first, wave_vectors, w_long_first, w_value, w_charge_second, w_long_second,
        dist_t, count_row, w_filter, lists,
    ) = kept
    sums = everything(part)
    hidden_first, values, force_first = pl.pallas_call(
        first_project_kernel,
        out_shape=(shape((atoms, hid), BF16), shape((kv * atoms, hid), BF16), shape((3, atoms), F32)),
        scratch_shapes=[pltpu.VMEM((4 * chan, waves), BF16)] * 2,
        compiler_params=vmem(6),
        name="project_first",
    )(sums, cos_table, sin_table, wave_vectors, features, w_charge_first, w_long_first, w_value)

    v_dom = lax.all_to_all(values, KV, 0, 0, tiled=True)

    def halo_rows(far, source):
        return pl.pallas_call(
            lambda *refs: halo_kernel(*refs, far=far),
            grid=(1,),
            in_specs=[pl.BlockSpec(memory_space=pl.ANY), pl.BlockSpec((kv * atoms, hid), lambda i: (0, 0))],
            out_specs=pl.BlockSpec((halo, hid), lambda i: (0, 0)),
            out_shape=shape((halo, hid), BF16),
            scratch_shapes=[
                pltpu.VMEM((kv * atoms + 8, hid), F32),
                pltpu.VMEM((halo, hid), F32),
                pltpu.SemaphoreType.DMA((halo // 128,)),
            ] + [pltpu.SMEM((2, 128), jnp.int32)] * (halo // 128),
            compiler_params=vmem(6),
            cost_estimate=pl.CostEstimate(flops=halo * hid, bytes_accessed=4 * kv * atoms * hid, transcendentals=0),
            name="halo_far" if far else "halo_near",
        )(lists, source)

    to_far = halo_rows(True, v_dom)
    to_far, source, index_t = lax.optimization_barrier((to_far, v_dom, index_t))
    from_far = lax.ppermute(to_far, DOM, [(i, (i - 1 + 2 * (i % 2)) % doms) for i in range(doms)])
    to_near = halo_rows(False, source)
    from_near = lax.ppermute(to_near, DOM, [(i, i + 1 - 2 * (i % 2)) for i in range(doms)])

    whole = lambda dims: pl.BlockSpec(dims, lambda i: (0,) * len(dims))
    weights = pl.pallas_call(
        lambda *refs: weight_kernel(*refs, steps=STEPS),
        grid=(1,),
        in_specs=[whole((1, atoms)), whole((slots, atoms)), whole(w_filter.shape)],
        out_specs=whole((atoms, slots, hid)),
        out_shape=shape((atoms, slots, hid), F32),
        scratch_shapes=[
            pltpu.VMEM((atoms, slots), F32),
            pltpu.VMEM((atoms // 2, 2 * slots), F32),
            pltpu.VMEM((atoms // 2, 2 * slots), F32),
            pltpu.VMEM((2 * w_filter.shape[0], hid), BF16),
        ],
        cost_estimate=pl.CostEstimate(
            flops=2 * atoms * slots * hid * 32,
            bytes_accessed=atoms * slots * hid * 4,
            transcendentals=atoms * slots * 16,
        ),
        compiler_params=vmem(12),
        name="slot_weights",
    )(count_row, dist_t, w_filter)

    blocks = slots // 4
    index_flat = index_t.reshape(slots * atoms)
    hidden_second, part = pl.pallas_call(
        lambda *refs: neighbour_kernel(*refs, scale=scale),
        grid=(1,),
        in_specs=[
            smem,
            pl.BlockSpec(memory_space=pl.ANY),
            pl.BlockSpec((atoms, slots, hid), lambda i: (0, 0, 0)),
            whole((kv * atoms, hid)),
            whole((halo, hid)),
            whole((halo, hid)),
            whole((atoms, hid)),
            whole((chan, hid)),
            whole((atoms, waves)),
            whole((atoms, waves)),
            whole((3, waves)),
        ],
        out_specs=(whole((atoms, hid)), whole((part_rows, 128))),
        out_shape=(shape((atoms, hid), BF16), shape((part_rows, 128), BF16)),
        scratch_shapes=[
            pltpu.VMEM((kv * atoms + 2 * halo + 8, hid), F32),
            pltpu.VMEM((8 * atoms, hid), F32),
            pltpu.SemaphoreType.DMA((blocks,)),
        ] + [pltpu.SMEM((4 * atoms,), jnp.int32)] * blocks,
        compiler_params=vmem(20),
        name="neighbours",
    )(
        *in_hbm(nbr_count), index_flat, weights, v_dom, from_far, from_near,
        hidden_first, w_charge_second, cos_table, sin_table, wave_vectors,
    )
    sums = everything(part)
    return pl.pallas_call(
        last_project_kernel,
        out_shape=(shape((atoms, hid), BF16), shape((3, atoms), F32)),
        scratch_shapes=[pltpu.VMEM((4 * chan, waves), BF16)] * 2,
        compiler_params=vmem(6),
        name="project_second",
    )(
        sums, cos_table, sin_table, wave_vectors, hidden_second, w_charge_second, w_long_second, force_first,
    )


def solution(mesh):
    sizes = tuple(size for _, size in PARTS)
    return jax.shard_map(
        local,
        mesh=jax.sharding.Mesh(mesh.devices.reshape(sizes), EVERY),
        in_specs=(
            P(None, EVERY), P(EVERY, None), P(EVERY, None), P(EVERY), P(EVERY, None), P(DOM, None, None),
            P(), P(), P(), P(), P(), P(), P(),
        ),
        out_specs=(P(EVERY, None), P(None, EVERY)),
        check_vma=False,
    )
```

```python
import math

import jax
import jax.numpy as jnp
from jax import lax
from jax.experimental import pallas as pl
from jax.experimental.pallas import tpu as pltpu
from jax.sharding import PartitionSpec as P

F32 = jnp.float32
BF16 = jnp.bfloat16
HIGHEST = lax.Precision.HIGHEST
LONG_SCALE = 2.0
CELL = 60.0
PARTS = (("xlo", 2), ("z", 8), ("core", 2), ("y", 4), ("xhi", 2))
EVERY = tuple(name for name, _ in PARTS)
DOM = ("xlo", "z", "core")
KV = ("y", "xhi")
UNROLL = 2
TILES = 4
STEPS = 2
LINE = ("z",)
PLANE = ("xlo", "core", "y", "xhi")

COS_COEF = (
    0.9999992251396179,
    -19.738981246948242,
    64.92865753173828,
    -85.27162170410156,
    58.79049301147461,
    -21.07110595703125,
)
SIN_COEF = (
    6.283185005187988,
    -41.341590881347656,
    81.59994506835938,
    -76.61447143554688,
    41.3428840637207,
    -12.471243858337402,
)

NN = (((1,), (0,)), ((), ()))
NT = (((1,), (1,)), ((), ()))
TN = (((0,), (0,)), ((), ()))


def horner(coefs, v):
    total = v * coefs[-1] + coefs[-2]
    for coef in coefs[-3::-1]:
        total = total * v + coef
    return total


def dot(a, b, dims=NN, precision=None):
    return lax.dot_general(a, b, dims, precision=precision, preferred_element_type=F32)


def silu(x):
    return x / (1.0 + jnp.exp(-x))


def wave_weight(wave):
    sq_norm = wave[0:1] * wave[0:1] + wave[1:2] * wave[1:2] + wave[2:3] * wave[2:3]
    return jnp.exp(-0.5 * sq_norm) / (sq_norm + 1.0)


def split_rows(x):
    high = x.astype(BF16)
    return jnp.concatenate([high, (x - high.astype(F32)).astype(BF16)], axis=0)


def structure_part(charge_t, cos_ref, sin_ref, wave_ref, part_ref, scale):
    chan = charge_t.shape[0]
    waves = cos_ref.shape[1]
    rows = split_rows(charge_t)
    cos_sum = dot(rows, cos_ref[...])
    sin_sum = dot(rows, sin_ref[...])
    weight = wave_weight(wave_ref[...]) * scale
    cos_sum = (cos_sum[:chan] + cos_sum[chan:]) * weight
    sin_sum = (sin_sum[:chan] + sin_sum[chan:]) * weight
    for t in range(waves // 128):
        lanes = slice(t * 128, (t + 1) * 128)
        part_ref[t * 2 * chan : t * 2 * chan + chan, :] = cos_sum[:, lanes].astype(BF16)
        part_ref[t * 2 * chan + chan : (t + 1) * 2 * chan, :] = sin_sum[:, lanes].astype(BF16)


def table_kernel(*refs, scale):
    later = (len(refs) - 6) // 2
    pos_ref, kept_in, cos_ref, sin_ref, part_ref = refs[0], refs[1 : 1 + later], *refs[1 + later : 4 + later]
    kept_out, turns, pad = refs[4 + later : -2], *refs[-2:]
    feat_ref, wc_ref, wave_ref = kept_in[:3]
    atoms, waves = cos_ref.shape
    for in_ref, out_ref in zip(kept_in, kept_out):
        out_ref[...] = in_ref[...]
    pad[...] = jnp.zeros_like(pad)
    pad[0:3, :] = pos_ref[...] * (1.0 / CELL)
    columns = jnp.transpose(pad[...])
    for c in range(3):
        turns[c] = jnp.broadcast_to(columns[:, c : c + 1], (atoms, 128))
    rows = 64

    def one_tile(t):
        lanes = pl.ds(pl.multiple_of(t * 128, 128), 128)
        whole = jnp.round(wave_ref[:, lanes] * (CELL / (2.0 * math.pi)))
        for b in range(atoms // rows):
            at = slice(b * rows, (b + 1) * rows)
            u = (
                turns[0, at, :] * whole[0:1]
                + turns[1, at, :] * whole[1:2]
                + turns[2, at, :] * whole[2:3]
            )
            u = u - jnp.round(u)
            v = u * u
            cos_ref[at, lanes] = horner(COS_COEF, v).astype(BF16)
            sin_ref[at, lanes] = (u * horner(SIN_COEF, v)).astype(BF16)

    def some_tiles(g, carry):
        for k in range(TILES):
            one_tile(g * TILES + k)
        return carry

    lax.fori_loop(0, waves // 128 // TILES, some_tiles, 0)
    charge_t = dot(wc_ref[...], feat_ref[...], NT)
    structure_part(charge_t, cos_ref, sin_ref, wave_ref, part_ref, scale)


def fold_kernel(in_ref, out_ref, *, members, copies):
    rows = in_ref.shape[0] // members
    total = in_ref[0:rows, :].astype(F32)
    for m in range(1, members):
        total = total + in_ref[m * rows : (m + 1) * rows, :].astype(F32)
    total = total.astype(out_ref.dtype)
    for m in range(copies):
        out_ref[m * rows : (m + 1) * rows, :] = total


def project(sums_ref, cos_ref, sin_ref, wave_ref, charge_t, with_cos, with_sin):
    chan = charge_t.shape[0]
    waves = cos_ref.shape[1]
    for t in range(waves // 128):
        lanes = slice(t * 128, (t + 1) * 128)
        wave = wave_ref[:, lanes]
        cos_w = sums_ref[t * 2 * chan : t * 2 * chan + chan, :].astype(F32)
        sin_w = sums_ref[t * 2 * chan + chan : (t + 1) * 2 * chan, :].astype(F32)
        with_cos[0:chan, lanes] = cos_w.astype(BF16)
        with_sin[0:chan, lanes] = sin_w.astype(BF16)
        for c in range(3):
            at = slice((c + 1) * chan, (c + 2) * chan)
            with_cos[at, lanes] = (-wave[c : c + 1] * sin_w).astype(BF16)
            with_sin[at, lanes] = (wave[c : c + 1] * cos_w).astype(BF16)
    both = dot(with_cos[...], cos_ref[...], NT) + dot(with_sin[...], sin_ref[...], NT)
    potential_t = both[:chan]
    force = [
        jnp.sum(charge_t * both[(c + 1) * chan : (c + 2) * chan], axis=0, keepdims=True)
        for c in range(3)
    ]
    return potential_t, force


def first_project_kernel(
    sums_ref, cos_ref, sin_ref, wave_ref, feat_ref, wc_ref, wl_ref, wv_ref,
    hidden_ref, values_ref, force_ref, with_cos, with_sin,
):
    charge_t = dot(wc_ref[...], feat_ref[...], NT)
    potential_t, force = project(sums_ref, cos_ref, sin_ref, wave_ref, charge_t, with_cos, with_sin)
    for c in range(3):
        force_ref[c : c + 1, :] = force[c]
    lifted = dot(potential_t, wl_ref[...], TN, HIGHEST)
    hidden = (feat_ref[...].astype(F32) + silu(lifted)).astype(BF16)
    hidden_ref[...] = hidden
    values = dot(hidden, wv_ref[...]).astype(BF16)
    atoms = values.shape[0]
    for j in range(values_ref.shape[0] // atoms):
        values_ref[j * atoms : (j + 1) * atoms, :] = values


def last_project_kernel(
    sums_ref, cos_ref, sin_ref, wave_ref, hidden_ref, wc_ref, wl_ref, force_in,
    feat_out, force_out, with_cos, with_sin,
):
    charge_t = dot(wc_ref[...], hidden_ref[...], NT)
    potential_t, force = project(sums_ref, cos_ref, sin_ref, wave_ref, charge_t, with_cos, with_sin)
    for c in range(3):
        force_out[c : c + 1, :] = force_in[c : c + 1, :] + force[c]
    lifted = dot(potential_t, wl_ref[...], TN, HIGHEST)
    feat_out[...] = (hidden_ref[...].astype(F32) + silu(lifted)).astype(BF16)


def row_tile(table, rows, bits):
    tiles = [table[pl.ds(row, 8, stride=0), :] for row in rows]
    for bit in bits:
        tiles = [jnp.where(bit, odd, even) for even, odd in zip(tiles[::2], tiles[1::2])]
    return tiles[0]


def sublane_bits():
    sub = lax.broadcasted_iota(jnp.int32, (8, 128), 0)
    return [(sub & bit) != 0 for bit in (1, 2, 4)]


def halo_kernel(*refs, far, skipped):
    list_ref, values_ref, out_ref, table, picked, arrived = refs[:6]
    lists = refs[6:]
    fetches = [
        pltpu.make_async_copy(list_ref.at[:, pl.ds(skipped + b * 128, 128)], part_ref, arrived.at[b])
        for b, part_ref in enumerate(lists)
    ]
    for fetch in fetches:
        fetch.start()
    core = lax.axis_index("core")
    side = 1 - core if far else core
    table[0 : values_ref.shape[0], :] = values_ref[...].astype(F32)
    bits = sublane_bits()
    for fetch in fetches:
        fetch.wait()

    def some_rows(g, carry):
        first = g * 8
        for b, part_ref in enumerate(lists):
            rows = [part_ref[side, first + j] for j in range(8)]
            picked[pl.ds(pl.multiple_of(b * 128 + first, 8), 8), :] = row_tile(table, rows, bits)
        return carry

    lax.fori_loop(0, 16, some_rows, 0)
    out_ref[...] = picked[...].astype(BF16)


def weight_kernel(count_ref, dist_ref, wf_ref, out_ref, turned, near, taper, wide, *, steps):
    slots, atoms = dist_ref.shape
    basis = wf_ref.shape[0]
    pairs = atoms // 2 // steps
    sharpness = ((basis - 1) / 4.5) ** 2

    def paired(block):
        turned[...] = jnp.transpose(block)
        return jnp.concatenate(
            [turned[pl.ds(0, atoms // 2, stride=2), :], turned[pl.ds(1, atoms // 2, stride=2), :]], axis=1
        )

    dist = dist_ref[...]
    scaled = dist * 0.1
    height = 0.5 * (horner(COS_COEF, scaled * scaled) + 1.0)
    slot = lax.broadcasted_iota(jnp.int32, (slots, atoms), 0)
    near[...] = paired(dist)
    taper[...] = paired(jnp.where(slot < count_ref[...], height, 0.0))
    wf_high = wf_ref[...].astype(BF16)
    wide[0:basis, :] = wf_high
    wide[basis : 2 * basis, :] = (wf_ref[...] - wf_high.astype(F32)).astype(BF16)
    centers = 0.5 + 4.5 / (basis - 1) * lax.broadcasted_iota(jnp.int32, (basis, 2 * slots), 0).astype(F32)

    def some_pairs(step, carry):
        for p in range(pairs):
            row = pl.ds(step * pairs + p, 1)
            away = near[row, :] - centers
            radial = (jnp.exp(-sharpness * (away * away)) * taper[row, :]).astype(BF16)
            both = dot(jnp.concatenate([radial, radial], axis=0), wide[...], TN)
            out_ref[2 * (step * pairs + p)] = both[:slots]
            out_ref[2 * (step * pairs + p) + 1] = both[slots:]
        return carry

    lax.fori_loop(0, steps, some_pairs, 0)


def neighbour_kernel(*refs, scale):
    (
        count_ref, list_ref, weight_ref, values_ref, far_a_ref, far_b_ref, near_ref, hidden_ref, wc_ref, cos_ref, sin_ref, wave_ref,
        hidden_out, part_ref, table, sums, arrived,
    ) = refs[:17]
    index_refs = refs[17:]
    size = index_refs[0].shape[0]
    fetches = [
        pltpu.make_async_copy(list_ref.at[pl.ds(b * size, size)], index_ref, arrived.at[b])
        for b, index_ref in enumerate(index_refs)
    ]
    for fetch in fetches:
        fetch.start()
    own = values_ref.shape[0]
    halo = near_ref.shape[0]
    atoms, slots, _ = weight_ref.shape
    core = lax.axis_index("core")
    table[0:own, :] = values_ref[...].astype(F32)
    table[pl.ds(pl.multiple_of(own + (1 - core) * halo, 8), halo), :] = near_ref[...].astype(F32)
    table[pl.ds(pl.multiple_of(own + core * halo, 8), halo // 2), :] = far_a_ref[...].astype(F32)
    table[pl.ds(pl.multiple_of(own + core * halo + halo // 2, 8), halo // 2), :] = far_b_ref[...].astype(F32)
    bits = sublane_bits()
    for fetch in fetches:
        fetch.wait()

    def some_atoms(group, carry):
        for k in range(UNROLL):
            one_atom(group * UNROLL + k)
        return carry

    def one_atom(atom):
        at = pl.ds(pl.multiple_of(atom * 8, 8), 8)
        spots = [atom + q * atoms for q in range(4)]

        def some_slots(blocks):
            total = jnp.zeros((8, 128), F32)
            for b in blocks:
                rows = [index_refs[2 * b + s // 4][spots[s % 4]] for s in range(8)]
                total = total + row_tile(table, rows, bits) * weight_ref[atom, 8 * b : 8 * b + 8, :]
            return total

        middle = slots // 16
        sums[at, :] = some_slots(range(middle))

        @pl.when(count_ref[atom] > middle * 8)
        def _():
            sums[at, :] = sums[at, :] + some_slots(range(middle, slots // 8))

    lax.fori_loop(0, atoms // UNROLL, some_atoms, 0)
    message = sums[pl.ds(0, atoms, stride=8), :]
    for k in range(1, 8):
        message = message + sums[pl.ds(k, atoms, stride=8), :]
    hidden = (hidden_ref[...].astype(F32) + silu(message)).astype(BF16)
    hidden_out[...] = hidden
    charge_t = dot(wc_ref[...], hidden, NT)
    structure_part(charge_t, cos_ref, sin_ref, wave_ref, part_ref, scale)


def shape(dims, kind):
    return jax.ShapeDtypeStruct(dims, kind)


def in_hbm(*arrays):
    return tuple(pltpu.with_memory_space_constraint(array, pltpu.HBM) for array in arrays)


def vmem(mib):
    return pltpu.CompilerParams(vmem_limit_bytes=mib * 1024 * 1024)


def fold(sums, members, copies, kind):
    rows = sums.shape[0] // members
    return pl.pallas_call(
        lambda *refs: fold_kernel(*refs, members=members, copies=copies),
        out_shape=shape((copies * rows, sums.shape[1]), kind),
        compiler_params=vmem(2),
    )(sums)


def everything(part):
    line = lax.axis_size(LINE)
    plane = lax.axis_size(PLANE)
    share = lax.all_to_all(part, PLANE, 0, 0, tiled=True)
    share = fold(share, plane, line, F32)
    share = lax.all_to_all(share, LINE, 0, 0, tiled=True)
    share = fold(share, line, plane, BF16)
    return lax.all_to_all(share, PLANE, 0, 0, tiled=True)


def local(
    positions, features, nbr_index, nbr_count, nbr_dist, halo_lists, wave_vectors,
    w_charge_first, w_long_first, w_value, w_filter, w_charge_second, w_long_second,
):
    atoms, hid = features.shape
    chan = w_charge_first.shape[1]
    waves = wave_vectors.shape[1]
    slots = nbr_index.shape[1]
    kv = lax.axis_size(KV)
    doms = lax.axis_size(DOM)
    total_atoms = atoms * doms * kv
    scale = LONG_SCALE / math.sqrt(waves) / math.sqrt(total_atoms)
    part_rows = 2 * chan * waves // 128
    halo = halo_lists.shape[2]
    smem = pl.BlockSpec(memory_space=pltpu.SMEM)
    w_charge_first = w_charge_first.T
    w_charge_second = w_charge_second.T
    lists = halo_lists[0]
    index_t = nbr_index.T
    dist_t = nbr_dist.T

    kept = (
        features, w_charge_first, wave_vectors, w_long_first, w_value, w_charge_second, w_long_second,
        dist_t, nbr_count.reshape(1, atoms), w_filter, lists,
    )
    cos_table, sin_table, part, *kept = pl.pallas_call(
        lambda *refs: table_kernel(*refs, scale=scale),
        out_shape=(
            shape((atoms, waves), BF16), shape((atoms, waves), BF16), shape((part_rows, 128), BF16),
            *(shape(a.shape, a.dtype) for a in kept),
        ),
        scratch_shapes=[pltpu.VMEM((3, atoms, 128), F32), pltpu.VMEM((8, atoms), F32)],
        compiler_params=vmem(6),
        name="tables",
    )(*in_hbm(positions, *kept))
    (
        features, w_charge_first, wave_vectors, w_long_first, w_value, w_charge_second, w_long_second,
        dist_t, count_row, w_filter, lists,
    ) = kept
    sums = everything(part)
    hidden_first, values, force_first = pl.pallas_call(
        first_project_kernel,
        out_shape=(shape((atoms, hid), BF16), shape((kv * atoms, hid), BF16), shape((3, atoms), F32)),
        scratch_shapes=[pltpu.VMEM((4 * chan, waves), BF16)] * 2,
        compiler_params=vmem(6),
        name="project_first",
    )(sums, cos_table, sin_table, wave_vectors, features, w_charge_first, w_long_first, w_value)

    v_dom = lax.all_to_all(values, KV, 0, 0, tiled=True)

    def halo_rows(far, source, first, count):
        return pl.pallas_call(
            lambda *refs: halo_kernel(*refs, far=far, skipped=first),
            grid=(1,),
            in_specs=[pl.BlockSpec(memory_space=pl.ANY), pl.BlockSpec((kv * atoms, hid), lambda i: (0, 0))],
            out_specs=pl.BlockSpec((count, hid), lambda i: (0, 0)),
            out_shape=shape((count, hid), BF16),
            scratch_shapes=[
                pltpu.VMEM((kv * atoms + 8, hid), F32),
                pltpu.VMEM((count, hid), F32),
                pltpu.SemaphoreType.DMA((count // 128,)),
            ] + [pltpu.SMEM((2, 128), jnp.int32)] * (count // 128),
            compiler_params=vmem(6),
            cost_estimate=pl.CostEstimate(flops=count * hid, bytes_accessed=4 * kv * atoms * hid, transcendentals=0),
        )(lists, source)

    part_count = halo // 2
    to_far = [(i, (i - 1 + 2 * (i % 2)) % doms) for i in range(doms)]
    to_near = [(i, i + 1 - 2 * (i % 2)) for i in range(doms)]
    rows_a = halo_rows(True, v_dom, 0, part_count)
    rows_a, source, index_t = lax.optimization_barrier((rows_a, v_dom, index_t))
    far_a = lax.ppermute(rows_a, DOM, to_far)
    rows_b = halo_rows(True, source, part_count, part_count)
    rows_b, source = lax.optimization_barrier((rows_b, source))
    far_b = lax.ppermute(rows_b, DOM, to_far)
    rows_near = halo_rows(False, source, 0, halo)
    from_near = lax.ppermute(rows_near, DOM, to_near)

    index_flat = index_t.reshape(slots * atoms)
    whole = lambda dims: pl.BlockSpec(dims, lambda i: (0,) * len(dims))
    weights = pl.pallas_call(
        lambda *refs: weight_kernel(*refs, steps=STEPS),
        grid=(1,),
        in_specs=[whole((1, atoms)), whole((slots, atoms)), whole(w_filter.shape)],
        out_specs=whole((atoms, slots, hid)),
        out_shape=shape((atoms, slots, hid), F32),
        scratch_shapes=[
            pltpu.VMEM((atoms, slots), F32),
            pltpu.VMEM((atoms // 2, 2 * slots), F32),
            pltpu.VMEM((atoms // 2, 2 * slots), F32),
            pltpu.VMEM((2 * w_filter.shape[0], hid), BF16),
        ],
        cost_estimate=pl.CostEstimate(
            flops=2 * atoms * slots * hid * 32,
            bytes_accessed=atoms * slots * hid * 4,
            transcendentals=atoms * slots * 16,
        ),
        compiler_params=vmem(12),
        name="slot_weights",
    )(count_row, dist_t, w_filter)

    blocks = slots // 4
    hidden_second, part = pl.pallas_call(
        lambda *refs: neighbour_kernel(*refs, scale=scale),
        grid=(1,),
        in_specs=[
            smem,
            pl.BlockSpec(memory_space=pl.ANY),
            pl.BlockSpec((atoms, slots, hid), lambda i: (0, 0, 0)),
            whole((kv * atoms, hid)),
            whole((part_count, hid)),
            whole((part_count, hid)),
            whole((halo, hid)),
            whole((atoms, hid)),
            whole((chan, hid)),
            whole((atoms, waves)),
            whole((atoms, waves)),
            whole((3, waves)),
        ],
        out_specs=(whole((atoms, hid)), whole((part_rows, 128))),
        out_shape=(shape((atoms, hid), BF16), shape((part_rows, 128), BF16)),
        scratch_shapes=[
            pltpu.VMEM((kv * atoms + 2 * halo + 8, hid), F32),
            pltpu.VMEM((8 * atoms, hid), F32),
            pltpu.SemaphoreType.DMA((blocks,)),
        ] + [pltpu.SMEM((4 * atoms,), jnp.int32)] * blocks,
        compiler_params=vmem(20),
        name="neighbours",
    )(
        *in_hbm(nbr_count), index_flat, weights, v_dom, far_a, far_b, from_near,
        hidden_first, w_charge_second, cos_table, sin_table, wave_vectors,
    )
    sums = everything(part)
    return pl.pallas_call(
        last_project_kernel,
        out_shape=(shape((atoms, hid), BF16), shape((3, atoms), F32)),
        scratch_shapes=[pltpu.VMEM((4 * chan, waves), BF16)] * 2,
        compiler_params=vmem(6),
        name="project_second",
    )(
        sums, cos_table, sin_table, wave_vectors, hidden_second, w_charge_second, w_long_second, force_first,
    )


def solution(mesh):
    sizes = tuple(size for _, size in PARTS)
    return jax.shard_map(
        local,
        mesh=jax.sharding.Mesh(mesh.devices.reshape(sizes), EVERY),
        in_specs=(
            P(None, EVERY), P(EVERY, None), P(EVERY, None), P(EVERY), P(EVERY, None), P(DOM, None, None),
            P(), P(), P(), P(), P(), P(), P(),
        ),
        out_specs=(P(EVERY, None), P(None, EVERY)),
        check_vma=False,
    )
```

```python
import math

import jax
import jax.numpy as jnp
from jax import lax
from jax.experimental import pallas as pl
from jax.experimental.pallas import tpu as pltpu
from jax.sharding import PartitionSpec as P

F32 = jnp.float32
BF16 = jnp.bfloat16
HIGHEST = lax.Precision.HIGHEST
LONG_SCALE = 2.0
CELL = 60.0
PARTS = (("xlo", 2), ("z", 8), ("core", 2), ("y", 4), ("xhi", 2))
EVERY = tuple(name for name, _ in PARTS)
DOM = ("xlo", "z", "core")
KV = ("y", "xhi")
UNROLL = 2
STEPS = 2
LINE = ("z",)
PLANE = ("xlo", "core", "y", "xhi")

COS_COEF = (
    0.9999992251396179,
    -19.738981246948242,
    64.92865753173828,
    -85.27162170410156,
    58.79049301147461,
    -21.07110595703125,
)
SIN_COEF = (
    6.283185005187988,
    -41.341590881347656,
    81.59994506835938,
    -76.61447143554688,
    41.3428840637207,
    -12.471243858337402,
)

NN = (((1,), (0,)), ((), ()))
NT = (((1,), (1,)), ((), ()))
TN = (((0,), (0,)), ((), ()))


def horner(coefs, v):
    total = v * coefs[-1] + coefs[-2]
    for coef in coefs[-3::-1]:
        total = total * v + coef
    return total


def dot(a, b, dims=NN, precision=None):
    return lax.dot_general(a, b, dims, precision=precision, preferred_element_type=F32)


def silu(x):
    return x / (1.0 + jnp.exp(-x))


def wave_weight(wave):
    sq_norm = wave[0:1] * wave[0:1] + wave[1:2] * wave[1:2] + wave[2:3] * wave[2:3]
    return jnp.exp(-0.5 * sq_norm) / (sq_norm + 1.0)


def split_rows(x):
    high = x.astype(BF16)
    return jnp.concatenate([high, (x - high.astype(F32)).astype(BF16)], axis=0)


def structure_part(charge_t, cos_ref, sin_ref, wave_ref, part_ref, scale):
    chan = charge_t.shape[0]
    waves = cos_ref.shape[1]
    rows = split_rows(charge_t)
    cos_sum = dot(rows, cos_ref[...])
    sin_sum = dot(rows, sin_ref[...])
    weight = wave_weight(wave_ref[...]) * scale
    cos_sum = (cos_sum[:chan] + cos_sum[chan:]) * weight
    sin_sum = (sin_sum[:chan] + sin_sum[chan:]) * weight
    for t in range(waves // 128):
        lanes = slice(t * 128, (t + 1) * 128)
        part_ref[t * 2 * chan : t * 2 * chan + chan, :] = cos_sum[:, lanes].astype(BF16)
        part_ref[t * 2 * chan + chan : (t + 1) * 2 * chan, :] = sin_sum[:, lanes].astype(BF16)


def table_kernel(*refs, scale):
    later = (len(refs) - 6) // 2
    pos_ref, kept_in, cos_ref, sin_ref, part_ref = refs[0], refs[1 : 1 + later], *refs[1 + later : 4 + later]
    kept_out, turns, pad = refs[4 + later : -2], *refs[-2:]
    feat_ref, wc_ref, wave_ref = kept_in[:3]
    atoms, waves = cos_ref.shape
    for in_ref, out_ref in zip(kept_in, kept_out):
        out_ref[...] = in_ref[...]
    pad[...] = jnp.zeros_like(pad)
    pad[0:3, :] = pos_ref[...] * (1.0 / CELL)
    columns = jnp.transpose(pad[...])
    for c in range(3):
        turns[c] = jnp.broadcast_to(columns[:, c : c + 1], (atoms, 128))
    rows = 64

    def one_tile(t):
        lanes = pl.ds(pl.multiple_of(t * 128, 128), 128)
        whole = jnp.round(wave_ref[:, lanes] * (CELL / (2.0 * math.pi)))
        for b in range(atoms // rows):
            at = slice(b * rows, (b + 1) * rows)
            u = (
                turns[0, at, :] * whole[0:1]
                + turns[1, at, :] * whole[1:2]
                + turns[2, at, :] * whole[2:3]
            )
            u = u - jnp.round(u)
            v = u * u
            cos_ref[at, lanes] = horner(COS_COEF, v).astype(BF16)
            sin_ref[at, lanes] = (u * horner(SIN_COEF, v)).astype(BF16)

    def some_tiles(g, carry):
        for k in range(4):
            one_tile(g * 4 + k)
        return carry

    lax.fori_loop(0, waves // 512, some_tiles, 0)
    charge_t = dot(wc_ref[...], feat_ref[...], NT)
    structure_part(charge_t, cos_ref, sin_ref, wave_ref, part_ref, scale)


def fold_kernel(in_ref, out_ref, *, members, copies):
    rows = in_ref.shape[0] // members
    total = in_ref[0:rows, :].astype(F32)
    for m in range(1, members):
        total = total + in_ref[m * rows : (m + 1) * rows, :].astype(F32)
    total = total.astype(out_ref.dtype)
    for m in range(copies):
        out_ref[m * rows : (m + 1) * rows, :] = total


def project(sums_ref, cos_ref, sin_ref, wave_ref, charge_t, with_cos, with_sin):
    chan = charge_t.shape[0]
    waves = cos_ref.shape[1]
    for t in range(waves // 128):
        lanes = slice(t * 128, (t + 1) * 128)
        wave = wave_ref[:, lanes]
        cos_w = sums_ref[t * 2 * chan : t * 2 * chan + chan, :].astype(F32)
        sin_w = sums_ref[t * 2 * chan + chan : (t + 1) * 2 * chan, :].astype(F32)
        with_cos[0:chan, lanes] = cos_w.astype(BF16)
        with_sin[0:chan, lanes] = sin_w.astype(BF16)
        for c in range(3):
            at = slice((c + 1) * chan, (c + 2) * chan)
            with_cos[at, lanes] = (-wave[c : c + 1] * sin_w).astype(BF16)
            with_sin[at, lanes] = (wave[c : c + 1] * cos_w).astype(BF16)
    both = dot(with_cos[...], cos_ref[...], NT) + dot(with_sin[...], sin_ref[...], NT)
    potential_t = both[:chan]
    force = [
        jnp.sum(charge_t * both[(c + 1) * chan : (c + 2) * chan], axis=0, keepdims=True)
        for c in range(3)
    ]
    return potential_t, force


def first_project_kernel(
    sums_ref, cos_ref, sin_ref, wave_ref, feat_ref, wc_ref, wl_ref, wv_ref,
    hidden_ref, values_ref, force_ref, with_cos, with_sin,
):
    charge_t = dot(wc_ref[...], feat_ref[...], NT)
    potential_t, force = project(sums_ref, cos_ref, sin_ref, wave_ref, charge_t, with_cos, with_sin)
    for c in range(3):
        force_ref[c : c + 1, :] = force[c]
    lifted = dot(potential_t, wl_ref[...], TN, HIGHEST)
    hidden = (feat_ref[...].astype(F32) + silu(lifted)).astype(BF16)
    hidden_ref[...] = hidden
    values = dot(hidden, wv_ref[...]).astype(BF16)
    atoms = values.shape[0]
    for j in range(values_ref.shape[0] // atoms):
        values_ref[j * atoms : (j + 1) * atoms, :] = values


def last_project_kernel(
    sums_ref, cos_ref, sin_ref, wave_ref, hidden_ref, wc_ref, wl_ref, force_in,
    feat_out, force_out, with_cos, with_sin,
):
    charge_t = dot(wc_ref[...], hidden_ref[...], NT)
    potential_t, force = project(sums_ref, cos_ref, sin_ref, wave_ref, charge_t, with_cos, with_sin)
    for c in range(3):
        force_out[c : c + 1, :] = force_in[c : c + 1, :] + force[c]
    lifted = dot(potential_t, wl_ref[...], TN, HIGHEST)
    feat_out[...] = (hidden_ref[...].astype(F32) + silu(lifted)).astype(BF16)


def row_tile(table, rows, bits):
    tiles = [table[pl.ds(row, 8, stride=0), :] for row in rows]
    for bit in bits:
        tiles = [jnp.where(bit, odd, even) for even, odd in zip(tiles[::2], tiles[1::2])]
    return tiles[0]


def sublane_bits():
    sub = lax.broadcasted_iota(jnp.int32, (8, 128), 0)
    return [(sub & bit) != 0 for bit in (1, 2, 4)]


def halo_kernel(*refs, far):
    lists, (values_ref, out_ref, table, picked) = refs[:-4], refs[-4:]
    core = lax.axis_index("core")
    side = 1 - core if far else core
    table[0 : values_ref.shape[0], :] = values_ref[...].astype(F32)
    bits = sublane_bits()

    def some_rows(g, carry):
        first = g * 8
        for b, list_ref in enumerate(lists):
            rows = [list_ref[side, first + j] for j in range(8)]
            picked[pl.ds(pl.multiple_of(b * 128 + first, 8), 8), :] = row_tile(table, rows, bits)
        return carry

    lax.fori_loop(0, 16, some_rows, 0)
    out_ref[...] = picked[...].astype(BF16)


def weight_kernel(count_ref, dist_ref, wf_ref, out_ref, turned, near, taper, wide, *, steps):
    slots, atoms = dist_ref.shape
    basis = wf_ref.shape[0]
    pairs = atoms // 2 // steps
    sharpness = ((basis - 1) / 4.5) ** 2

    def paired(block):
        turned[...] = jnp.transpose(block)
        return jnp.concatenate(
            [turned[pl.ds(0, atoms // 2, stride=2), :], turned[pl.ds(1, atoms // 2, stride=2), :]], axis=1
        )

    dist = dist_ref[...]
    scaled = dist * 0.1
    height = 0.5 * (horner(COS_COEF, scaled * scaled) + 1.0)
    slot = lax.broadcasted_iota(jnp.int32, (slots, atoms), 0)
    near[...] = paired(dist)
    taper[...] = paired(jnp.where(slot < count_ref[...], height, 0.0))
    wf_high = wf_ref[...].astype(BF16)
    wide[0:basis, :] = wf_high
    wide[basis : 2 * basis, :] = (wf_ref[...] - wf_high.astype(F32)).astype(BF16)
    centers = 0.5 + 4.5 / (basis - 1) * lax.broadcasted_iota(jnp.int32, (basis, 2 * slots), 0).astype(F32)

    def some_pairs(step, carry):
        for p in range(pairs):
            row = pl.ds(step * pairs + p, 1)
            away = near[row, :] - centers
            radial = (jnp.exp(-sharpness * (away * away)) * taper[row, :]).astype(BF16)
            both = dot(jnp.concatenate([radial, radial], axis=0), wide[...], TN)
            out_ref[2 * (step * pairs + p)] = both[:slots]
            out_ref[2 * (step * pairs + p) + 1] = both[slots:]
        return carry

    lax.fori_loop(0, steps, some_pairs, 0)


def neighbour_kernel(*refs, scale):
    count_ref, index_refs = refs[0], refs[1:-13]
    (
        weight_ref, values_ref, far_ref, near_ref, hidden_ref, wc_ref, cos_ref, sin_ref, wave_ref,
        hidden_out, part_ref, table, sums,
    ) = refs[-13:]
    own = values_ref.shape[0]
    halo = far_ref.shape[0]
    atoms, slots, _ = weight_ref.shape
    core = lax.axis_index("core")
    table[0:own, :] = values_ref[...].astype(F32)
    table[pl.ds(pl.multiple_of(own + (1 - core) * halo, 8), halo), :] = near_ref[...].astype(F32)
    table[pl.ds(pl.multiple_of(own + core * halo, 8), halo), :] = far_ref[...].astype(F32)
    bits = sublane_bits()

    def some_atoms(group, carry):
        for k in range(UNROLL):
            one_atom(group * UNROLL + k)
        return carry

    def one_atom(atom):
        at = pl.ds(pl.multiple_of(atom * 8, 8), 8)
        spots = [atom + q * atoms for q in range(4)]

        def some_slots(blocks):
            total = jnp.zeros((8, 128), F32)
            for b in blocks:
                rows = [index_refs[2 * b + s // 4][spots[s % 4]] for s in range(8)]
                total = total + row_tile(table, rows, bits) * weight_ref[atom, 8 * b : 8 * b + 8, :]
            return total

        middle = slots // 16
        sums[at, :] = some_slots(range(middle))

        most = 3 * slots // 32
        count = count_ref[atom]

        @pl.when(count > most * 8)
        def _():
            sums[at, :] = sums[at, :] + some_slots(range(middle, slots // 8))

        @pl.when((count > middle * 8) & (count <= most * 8))
        def _():
            sums[at, :] = sums[at, :] + some_slots(range(middle, most))

    lax.fori_loop(0, atoms // UNROLL, some_atoms, 0)
    message = sums[pl.ds(0, atoms, stride=8), :]
    for k in range(1, 8):
        message = message + sums[pl.ds(k, atoms, stride=8), :]
    hidden = (hidden_ref[...].astype(F32) + silu(message)).astype(BF16)
    hidden_out[...] = hidden
    charge_t = dot(wc_ref[...], hidden, NT)
    structure_part(charge_t, cos_ref, sin_ref, wave_ref, part_ref, scale)


def shape(dims, kind):
    return jax.ShapeDtypeStruct(dims, kind)


def in_hbm(*arrays):
    return tuple(pltpu.with_memory_space_constraint(array, pltpu.HBM) for array in arrays)


def vmem(mib):
    return pltpu.CompilerParams(vmem_limit_bytes=mib * 1024 * 1024)


def fold(sums, members, copies, kind):
    rows = sums.shape[0] // members
    return pl.pallas_call(
        lambda *refs: fold_kernel(*refs, members=members, copies=copies),
        out_shape=shape((copies * rows, sums.shape[1]), kind),
        compiler_params=vmem(2),
    )(sums)


def everything(part):
    line = lax.axis_size(LINE)
    plane = lax.axis_size(PLANE)
    share = lax.all_to_all(part, PLANE, 0, 0, tiled=True)
    share = fold(share, plane, line, F32)
    share = lax.all_to_all(share, LINE, 0, 0, tiled=True)
    share = fold(share, line, plane, BF16)
    return lax.all_to_all(share, PLANE, 0, 0, tiled=True)


def local(
    positions, features, nbr_index, nbr_count, nbr_dist, halo_lists, wave_vectors,
    w_charge_first, w_long_first, w_value, w_filter, w_charge_second, w_long_second,
):
    atoms, hid = features.shape
    chan = w_charge_first.shape[1]
    waves = wave_vectors.shape[1]
    slots = nbr_index.shape[1]
    kv = lax.axis_size(KV)
    doms = lax.axis_size(DOM)
    total_atoms = atoms * doms * kv
    scale = LONG_SCALE / math.sqrt(waves) / math.sqrt(total_atoms)
    part_rows = 2 * chan * waves // 128
    halo = halo_lists.shape[2]
    smem = pl.BlockSpec(memory_space=pltpu.SMEM)
    w_charge_first = w_charge_first.T
    w_charge_second = w_charge_second.T
    lists = halo_lists[0]
    index_t = nbr_index.T
    dist_t = nbr_dist.T

    kept = (
        features, w_charge_first, wave_vectors, w_long_first, w_value, w_charge_second, w_long_second,
        dist_t, nbr_count.reshape(1, atoms), w_filter, lists,
    )
    cos_table, sin_table, part, *kept = pl.pallas_call(
        lambda *refs: table_kernel(*refs, scale=scale),
        out_shape=(
            shape((atoms, waves), BF16), shape((atoms, waves), BF16), shape((part_rows, 128), BF16),
            *(shape(a.shape, a.dtype) for a in kept),
        ),
        scratch_shapes=[pltpu.VMEM((3, atoms, 128), F32), pltpu.VMEM((8, atoms), F32)],
        compiler_params=vmem(6),
        name="tables",
    )(*in_hbm(positions, *kept))
    (
        features, w_charge_first, wave_vectors, w_long_first, w_value, w_charge_second, w_long_second,
        dist_t, count_row, w_filter, lists,
    ) = kept
    sums = everything(part)
    hidden_first, values, force_first = pl.pallas_call(
        first_project_kernel,
        out_shape=(shape((atoms, hid), BF16), shape((kv * atoms, hid), BF16), shape((3, atoms), F32)),
        scratch_shapes=[pltpu.VMEM((4 * chan, waves), BF16)] * 2,
        compiler_params=vmem(6),
        name="project_first",
    )(sums, cos_table, sin_table, wave_vectors, features, w_charge_first, w_long_first, w_value)

    v_dom = lax.all_to_all(values, KV, 0, 0, tiled=True)

    def halo_rows(far, source):
        return pl.pallas_call(
            lambda *refs: halo_kernel(*refs, far=far),
            grid=(1,),
            in_specs=[
                pl.BlockSpec((2, 128), lambda i, b=b: (0, b), memory_space=pltpu.SMEM) for b in range(halo // 128)
            ] + [pl.BlockSpec((kv * atoms, hid), lambda i: (0, 0))],
            out_specs=pl.BlockSpec((halo, hid), lambda i: (0, 0)),
            out_shape=shape((halo, hid), BF16),
            scratch_shapes=[pltpu.VMEM((kv * atoms + 8, hid), F32), pltpu.VMEM((halo, hid), F32)],
            compiler_params=vmem(6),
            cost_estimate=pl.CostEstimate(flops=halo * hid, bytes_accessed=4 * kv * atoms * hid, transcendentals=0),
            name="halo_far" if far else "halo_near",
        )(*[lists] * (halo // 128), source)

    to_far = halo_rows(True, v_dom)
    to_far, source, index_t = lax.optimization_barrier((to_far, v_dom, index_t))
    from_far = lax.ppermute(to_far, DOM, [(i, (i - 1 + 2 * (i % 2)) % doms) for i in range(doms)])
    to_near = halo_rows(False, source)
    from_near = lax.ppermute(to_near, DOM, [(i, i + 1 - 2 * (i % 2)) for i in range(doms)])

    whole = lambda dims: pl.BlockSpec(dims, lambda i: (0,) * len(dims))
    weights = pl.pallas_call(
        lambda *refs: weight_kernel(*refs, steps=STEPS),
        grid=(1,),
        in_specs=[whole((1, atoms)), whole((slots, atoms)), whole(w_filter.shape)],
        out_specs=whole((atoms, slots, hid)),
        out_shape=shape((atoms, slots, hid), F32),
        scratch_shapes=[
            pltpu.VMEM((atoms, slots), F32),
            pltpu.VMEM((atoms // 2, 2 * slots), F32),
            pltpu.VMEM((atoms // 2, 2 * slots), F32),
            pltpu.VMEM((2 * w_filter.shape[0], hid), BF16),
        ],
        cost_estimate=pl.CostEstimate(
            flops=2 * atoms * slots * hid * 32,
            bytes_accessed=atoms * slots * hid * 4,
            transcendentals=atoms * slots * 16,
        ),
        compiler_params=vmem(12),
        name="slot_weights",
    )(count_row, dist_t, w_filter)

    blocks = range(slots // 4)
    index_flat = index_t.reshape(slots * atoms)
    hidden_second, part = pl.pallas_call(
        lambda *refs: neighbour_kernel(*refs, scale=scale),
        grid=(1,),
        in_specs=[smem] + [
            pl.BlockSpec((4 * atoms,), lambda i, at=at: (at,), memory_space=pltpu.SMEM) for at in blocks
        ] + [
            pl.BlockSpec((atoms, slots, hid), lambda i: (0, 0, 0)),
            whole((kv * atoms, hid)),
            whole((halo, hid)),
            whole((halo, hid)),
            whole((atoms, hid)),
            whole((chan, hid)),
            whole((atoms, waves)),
            whole((atoms, waves)),
            whole((3, waves)),
        ],
        out_specs=(whole((atoms, hid)), whole((part_rows, 128))),
        out_shape=(shape((atoms, hid), BF16), shape((part_rows, 128), BF16)),
        scratch_shapes=[pltpu.VMEM((kv * atoms + 2 * halo + 8, hid), F32), pltpu.VMEM((8 * atoms, hid), F32)],
        compiler_params=vmem(20),
        name="neighbours",
    )(
        *in_hbm(nbr_count), *[index_flat] * len(blocks), weights, v_dom, from_far, from_near,
        hidden_first, w_charge_second, cos_table, sin_table, wave_vectors,
    )
    sums = everything(part)
    return pl.pallas_call(
        last_project_kernel,
        out_shape=(shape((atoms, hid), BF16), shape((3, atoms), F32)),
        scratch_shapes=[pltpu.VMEM((4 * chan, waves), BF16)] * 2,
        compiler_params=vmem(6),
        name="project_second",
    )(
        sums, cos_table, sin_table, wave_vectors, hidden_second, w_charge_second, w_long_second, force_first,
    )


def solution(mesh):
    sizes = tuple(size for _, size in PARTS)
    return jax.shard_map(
        local,
        mesh=jax.sharding.Mesh(mesh.devices.reshape(sizes), EVERY),
        in_specs=(
            P(None, EVERY), P(EVERY, None), P(EVERY, None), P(EVERY), P(EVERY, None), P(DOM, None, None),
            P(), P(), P(), P(), P(), P(), P(),
        ),
        out_specs=(P(EVERY, None), P(None, EVERY)),
        check_vma=False,
    )
```
